32 devices in a mesh: fsdp: 2 (over core), ctx: 4 (over z), tp: 4 (over y, x).
Axes of the slice: x: 2, y: 2, z: 4, core: 2. Of those that a mesh axis runs over, the one named last changes fastest.
Arguments:
- hidden_in: bfloat16 [8, 512, 2048], P('fsdp', 'ctx'), may hold values from -6 to 6
- seq_lengths: int32 [8], P('fsdp'), may hold values from 128 to 512, as said below
- mixer_gain: float32 [2048], replicated, may hold values from 0.5 to 1.5
- feed_gain: float32 [2048], replicated, may hold values from 0.5 to 1.5
- query_weight: bfloat16 [2048, 2048], P('fsdp', 'tp'), may hold values from -0.125 to 0.125
- key_weight: bfloat16 [2048, 2048], P('fsdp', 'tp'), may hold values from -0.125 to 0.125
- value_weight: bfloat16 [2048, 2048], P('fsdp', 'tp'), may hold values from -0.125 to 0.125
- rate_weight: bfloat16 [2048, 16], P('fsdp', 'tp'), may hold values from -0.125 to 0.125
- query_conv: float32 [4, 2048], P(None, 'tp'), may hold values from -3 to 3
- key_conv: float32 [4, 2048], P(None, 'tp'), may hold values from -3 to 3
- value_conv: float32 [4, 2048], P(None, 'tp'), may hold values from -3 to 3
- head_gain: float32 [128], replicated, may hold values from 0.5 to 1.5
- output_weight: bfloat16 [2048, 2048], P('tp', 'fsdp'), may hold values from -0.125 to 0.125
- gate_weight: bfloat16 [2048, 5632], P('fsdp', 'tp'), may hold values from -0.125 to 0.125
- up_weight: bfloat16 [2048, 5632], P('fsdp', 'tp'), may hold values from -0.125 to 0.125
- down_weight: bfloat16 [5632, 2048], P('tp', 'fsdp'), may hold values from -0.078125 to 0.078125
- query_left: bfloat16 [2048, 16], P(None, 'fsdp'), may hold values from -0.125 to 0.125
- query_right: bfloat16 [16, 2048], P('fsdp', 'tp'), may hold values from -1.5 to 1.5
- key_left: bfloat16 [2048, 16], P(None, 'fsdp'), may hold values from -0.125 to 0.125
- key_right: bfloat16 [16, 2048], P('fsdp', 'tp'), may hold values from -1.5 to 1.5
- value_left: bfloat16 [2048, 16], P(None, 'fsdp'), may hold values from -0.125 to 0.125
- value_right: bfloat16 [16, 2048], P('fsdp', 'tp'), may hold values from -1.5 to 1.5
- rate_left: bfloat16 [2048, 16], P(None, 'fsdp'), may hold values from -0.125 to 0.125
- rate_right: bfloat16 [16, 16], P('fsdp', 'tp'), may hold values from -1.5 to 1.5
- output_left: bfloat16 [2048, 16], P('tp', 'fsdp'), may hold values from -0.125 to 0.125
- output_right: bfloat16 [16, 2048], P('fsdp'), may hold values from -1.5 to 1.5
- gate_left: bfloat16 [2048, 16], P(None, 'fsdp'), may hold values from -0.125 to 0.125
- gate_right: bfloat16 [16, 5632], P('fsdp', 'tp'), may hold values from -1.5 to 1.5
- up_left: bfloat16 [2048, 16], P(None, 'fsdp'), may hold values from -0.125 to 0.125
- up_right: bfloat16 [16, 5632], P('fsdp', 'tp'), may hold values from -1.5 to 1.5
- down_left: bfloat16 [5632, 16], P('tp', 'fsdp'), may hold values from -0.078125 to 0.078125
- down_right: bfloat16 [16, 2048], P('fsdp'), may hold values from -1.5 to 1.5
- output_grad: bfloat16 [8, 512, 2048], P('fsdp', 'ctx'), may hold values from -6 to 6
Outputs:
- block_out: bfloat16 [8, 512, 2048], P('fsdp', 'ctx')
- input_grad: bfloat16 [8, 512, 2048], P('fsdp', 'ctx')
- query_left_grad: float32 [2048, 16], P(None, 'fsdp')
- query_right_grad: float32 [16, 2048], P('fsdp', 'tp')
- key_left_grad: float32 [2048, 16], P(None, 'fsdp')
- key_right_grad: float32 [16, 2048], P('fsdp', 'tp')
- value_left_grad: float32 [2048, 16], P(None, 'fsdp')
- value_right_grad: float32 [16, 2048], P('fsdp', 'tp')
- rate_left_grad: float32 [2048, 16], P(None, 'fsdp')
- rate_right_grad: float32 [16, 16], P('fsdp', 'tp')
- output_left_grad: float32 [2048, 16], P('tp', 'fsdp')
- output_right_grad: float32 [16, 2048], P('fsdp')
- gate_left_grad: float32 [2048, 16], P(None, 'fsdp')
- gate_right_grad: float32 [16, 5632], P('fsdp', 'tp')
- up_left_grad: float32 [2048, 16], P(None, 'fsdp')
- up_right_grad: float32 [16, 5632], P('fsdp', 'tp')
- down_left_grad: float32 [5632, 16], P('tp', 'fsdp')
- down_right_grad: float32 [16, 2048], P('fsdp')
The draws below stay inside these ranges and needn't reach their ends.
Inputs may be any that keep to these rules, and one draw needn't show every extreme that they name: `seq_lengths`: valid positions of each sequence, the rest padding; some sequence in every draw has all 512.
All inputs are finite; a program needn't handle non-finite values.
Results may differ from the reference program's by a relative error of at most 0.025.
Values may be sent and summed in bfloat16 or wider, within the bound.
A program may use at most 256 MiB of HBM per device.

```python
import jax
import jax.numpy as jnp
from jax import lax

D = 2048
HEADS = 16
HEAD_DIM = 128
FF = 5632
CONV = 4
GROUP = 64
RANK = 16
SEQS = 8
LEN = 512


def draw_seq_lengths(key, part):
    picked = jax.random.randint(key, (SEQS,), LEN // 4, LEN + 1)
    chosen = jax.random.randint(jax.random.fold_in(key, 7), (), 0, SEQS)
    return jnp.where(jnp.arange(SEQS) == chosen, LEN, picked).astype(jnp.int32)


def shard_levels(key, extent, cuts, least, top_value):
    level = 1.0
    for dim, blocks in cuts:
        draws = jax.random.uniform(jax.random.fold_in(jax.random.fold_in(key, 6), dim), (blocks,), jnp.float32, least / len(cuts), top_value / len(cuts))
        level = level * jnp.repeat(jnp.exp(draws), extent[dim] // blocks).reshape((-1,) + (1,) * (len(extent) - 1 - dim))
    return level


def gaussian(stream_key, extent, scale, most, pieces=(), held_as=jnp.bfloat16):
    array = jax.random.normal(stream_key, extent, jnp.float32) * scale
    if len(pieces) > 0:
        array = shard_levels(stream_key, extent, pieces, -0.22, 0.18) * array
    return jnp.clip(array, min=-most, max=most).astype(held_as)


def setup_inputs(seed: int = 0) -> dict:
    key_list = jax.random.split(jax.random.key(seed), 34)
    return {
        "hidden_in": gaussian(key_list[0], (SEQS, LEN, D), 1.0, 6.0, ((0, 2), (1, 4))),
        "seq_lengths": draw_seq_lengths(jax.random.fold_in(key_list[33], 71), 0),
        "mixer_gain": jnp.clip(1.0 + 0.1 * jax.random.normal(key_list[2], (D,), jnp.float32), 0.5, 1.5),
        "feed_gain": jnp.clip(1.0 + 0.1 * jax.random.normal(key_list[3], (D,), jnp.float32), 0.5, 1.5),
        "query_weight": gaussian(key_list[4], (D, D), D ** -0.5, 0.125, ((0, 2), (1, 4))),
        "key_weight": gaussian(key_list[5], (D, D), D ** -0.5, 0.125, ((0, 2), (1, 4))),
        "value_weight": gaussian(key_list[6], (D, D), D ** -0.5, 0.125, ((0, 2), (1, 4))),
        "rate_weight": gaussian(key_list[7], (D, HEADS), D ** -0.5, 0.125, ((0, 2), (1, 4))),
        "query_conv": gaussian(key_list[8], (CONV, D), 0.5, 3.0, ((1, 4),), jnp.float32),
        "key_conv": gaussian(key_list[9], (CONV, D), 0.5, 3.0, ((1, 4),), jnp.float32),
        "value_conv": gaussian(key_list[10], (CONV, D), 0.5, 3.0, ((1, 4),), jnp.float32),
        "head_gain": jnp.clip(1.0 + 0.1 * jax.random.normal(key_list[11], (HEAD_DIM,), jnp.float32), 0.5, 1.5),
        "output_weight": gaussian(key_list[12], (D, D), D ** -0.5, 0.125, ((0, 4), (1, 2))),
        "gate_weight": gaussian(key_list[13], (D, FF), D ** -0.5, 0.125, ((0, 2), (1, 4))),
        "up_weight": gaussian(key_list[14], (D, FF), D ** -0.5, 0.125, ((0, 2), (1, 4))),
        "down_weight": gaussian(key_list[15], (FF, D), FF ** -0.5, 0.078125, ((0, 4), (1, 2))),
        "query_left": gaussian(key_list[16], (D, RANK), D ** -0.5, 0.125, ((1, 2),)),
        "query_right": gaussian(key_list[17], (RANK, D), RANK ** -0.5, 1.5, ((0, 2), (1, 4))),
        "key_left": gaussian(key_list[18], (D, RANK), D ** -0.5, 0.125, ((1, 2),)),
        "key_right": gaussian(key_list[19], (RANK, D), RANK ** -0.5, 1.5, ((0, 2), (1, 4))),
        "value_left": gaussian(key_list[20], (D, RANK), D ** -0.5, 0.125, ((1, 2),)),
        "value_right": gaussian(key_list[21], (RANK, D), RANK ** -0.5, 1.5, ((0, 2), (1, 4))),
        "rate_left": gaussian(key_list[22], (D, RANK), D ** -0.5, 0.125, ((1, 2),)),
        "rate_right": gaussian(key_list[23], (RANK, HEADS), RANK ** -0.5, 1.5, ((0, 2), (1, 4))),
        "output_left": gaussian(key_list[24], (D, RANK), D ** -0.5, 0.125, ((0, 4), (1, 2))),
        "output_right": gaussian(key_list[25], (RANK, D), RANK ** -0.5, 1.5, ((0, 2),)),
        "gate_left": gaussian(key_list[26], (D, RANK), D ** -0.5, 0.125, ((1, 2),)),
        "gate_right": gaussian(key_list[27], (RANK, FF), RANK ** -0.5, 1.5, ((0, 2), (1, 4))),
        "up_left": gaussian(key_list[28], (D, RANK), D ** -0.5, 0.125, ((1, 2),)),
        "up_right": gaussian(key_list[29], (RANK, FF), RANK ** -0.5, 1.5, ((0, 2), (1, 4))),
        "down_left": gaussian(key_list[30], (FF, RANK), FF ** -0.5, 0.078125, ((0, 4), (1, 2))),
        "down_right": gaussian(key_list[31], (RANK, D), RANK ** -0.5, 1.5, ((0, 2),)),
        "output_grad": gaussian(key_list[32], (SEQS, LEN, D), 1.0, 6.0, ((0, 2), (1, 4))),
    }


adapter_scale = 0.5
epsilon = 1e-06

@jax.custom_vjp
def low(v):
    return lax.optimization_barrier(v.astype(jnp.bfloat16)).astype(jnp.float32)

@jax.custom_vjp
def low_back(v):
    return v

def low_keep(v):
    return (low(v), None)

def low_pass(kept, grad):
    return (grad,)

def back_keep(v):
    return (v, None)

def back_low(kept, grad):
    return (low(grad),)
low.defvjp(low_keep, low_pass)
low_back.defvjp(back_keep, back_low)

def precise(form, left_side, right_side):
    return jnp.einsum(form, left_side, right_side, precision=lax.Precision.HIGHEST)

def scaled_norm(values_in, scale_gain):
    return values_in * lax.rsqrt(lax.optimization_barrier(jnp.mean(values_in * values_in, axis=-1, keepdims=True)) + epsilon) * scale_gain

def unit_norm(values_in):
    return values_in * lax.rsqrt(lax.optimization_barrier(jnp.sum(values_in * values_in, axis=-1, keepdims=True)) + epsilon)

def rounded_both(values_in):
    return low(low_back(values_in))

def adapted(rows_in, frozen, into, back_out):
    inner = rounded_both(precise('td,dr->tr', rows_in, into))
    return low_back(precise('td,df->tf', rows_in, frozen) + adapter_scale * precise('tr,rf->tf', inner, back_out))

def causal_conv(pre_values, conv_taps):
    padded = jnp.pad(pre_values, ((CONV - 1, 0), (0, 0)))
    return sum((conv_taps[offset] * padded[offset:offset + LEN] for offset in range(CONV)))

def delta_rule(queries, key_rows, value_rows, rate_rows):
    head_count, seq_len, head_width = queries.shape
    blocks = seq_len // GROUP

    def to_blocks(stacked):
        return jnp.moveaxis(stacked.reshape((head_count, blocks, GROUP) + stacked.shape[2:]), 1, 0)
    causal = jnp.tril(jnp.ones((GROUP, GROUP), jnp.float32))
    strict = jnp.tril(jnp.ones((GROUP, GROUP), jnp.float32), -1)
    identity = jnp.eye(GROUP, dtype=jnp.float32)

    def advance(carry_state, block):
        query_block, key_block, value_block, rate_block = block
        system = identity + strict * rate_block[:, :, None] * precise('hid,hjd->hij', key_block, key_block)
        weighted_keys = lax.linalg.triangular_solve(system, rate_block[:, :, None] * key_block, left_side=True, lower=True, unit_diagonal=True)
        weighted_values = lax.linalg.triangular_solve(system, rate_block[:, :, None] * value_block, left_side=True, lower=True, unit_diagonal=True)
        fresh_values = weighted_values - precise('hid,hde->hie', weighted_keys, carry_state)
        scores = causal * precise('hid,hjd->hij', query_block, key_block)
        block_outs = precise('hid,hde->hie', query_block, carry_state) + precise('hij,hje->hie', scores, fresh_values)
        carry_state = carry_state + precise('hid,hie->hde', key_block, fresh_values)
        return (carry_state, block_outs)
    start_state = jnp.zeros((head_count, head_width, head_width), jnp.float32)
    blocked = (to_blocks(queries), to_blocks(key_rows), to_blocks(value_rows), to_blocks(rate_rows))
    end_state, block_outs = lax.scan(jax.checkpoint(advance), start_state, blocked)
    return jnp.moveaxis(block_outs, 0, 1).reshape(head_count, seq_len, head_width)

def layer_seq(seq_rows, seq_length, frozen, adapter_set):
    mixer_gain, feed_gain, query_weight, key_weight, value_weight, rate_weight, query_conv, key_conv, value_conv, head_gain, output_weight, gate_weight, up_weight, down_weight = frozen
    query_left, query_right, key_left, key_right, value_left, value_right, rate_left, rate_right, output_left, output_right, gate_left, gate_right, up_left, up_right, down_left, down_right = adapter_set
    valid_mask = (jnp.arange(LEN) < seq_length).astype(jnp.float32)
    first = low(scaled_norm(seq_rows, mixer_gain))
    pre_query = adapted(first, query_weight, query_left, query_right)
    pre_key = adapted(first, key_weight, key_left, key_right)
    pre_value = adapted(first, value_weight, value_left, value_right)
    pre_rate = adapted(first, rate_weight, rate_left, rate_right)
    queries = unit_norm(jax.nn.silu(causal_conv(pre_query, query_conv)).reshape(LEN, HEADS, HEAD_DIM))
    key_rows = unit_norm(jax.nn.silu(causal_conv(pre_key, key_conv)).reshape(LEN, HEADS, HEAD_DIM))
    value_rows = jax.nn.silu(causal_conv(pre_value, value_conv)).reshape(LEN, HEADS, HEAD_DIM)
    rate_rows = jax.nn.sigmoid(pre_rate) * valid_mask[:, None]
    mixed = delta_rule(jnp.transpose(queries, (1, 0, 2)), jnp.transpose(key_rows, (1, 0, 2)), jnp.transpose(value_rows, (1, 0, 2)), jnp.transpose(rate_rows))
    heads_low = low(jnp.transpose(scaled_norm(mixed, head_gain), (1, 0, 2)).reshape(LEN, D))
    residual = seq_rows + adapted(heads_low, output_weight, output_left, output_right)
    second = low(scaled_norm(residual, feed_gain))
    pre_gate = adapted(second, gate_weight, gate_left, gate_right)
    pre_up = adapted(second, up_weight, up_left, up_right)
    activated = low(jax.nn.silu(pre_gate) * pre_up)
    final = residual + adapted(activated, down_weight, down_left, down_right)
    return valid_mask[:, None] * final

def reference(hidden_in, seq_lengths, mixer_gain, feed_gain, query_weight, key_weight, value_weight, rate_weight, query_conv, key_conv, value_conv, head_gain, output_weight, gate_weight, up_weight, down_weight, query_left, query_right, key_left, key_right, value_left, value_right, rate_left, rate_right, output_left, output_right, gate_left, gate_right, up_left, up_right, down_left, down_right, output_grad):
    frozen = tuple((item.astype(jnp.float32) for item in (mixer_gain, feed_gain, query_weight, key_weight, value_weight, rate_weight, query_conv, key_conv, value_conv, head_gain, output_weight, gate_weight, up_weight, down_weight)))
    adapter_set = tuple((item.astype(jnp.float32) for item in (query_left, query_right, key_left, key_right, value_left, value_right, rate_left, rate_right, output_left, output_right, gate_left, gate_right, up_left, up_right, down_left, down_right)))

    def forward(inputs, adapters_in):

        def one_seq(paired):
            return layer_seq(paired[0], paired[1], frozen, adapters_in)
        return lax.map(jax.checkpoint(one_seq), (inputs, seq_lengths))
    block_out, pull_back = jax.vjp(forward, hidden_in.astype(jnp.float32), adapter_set)
    input_grad, grads = pull_back(output_grad.astype(jnp.float32))
    return (block_out.astype(jnp.bfloat16), input_grad.astype(jnp.bfloat16), grads[0], grads[1], grads[2], grads[3], grads[4], grads[5], grads[6], grads[7], grads[8], grads[9], grads[10], grads[11], grads[12], grads[13], grads[14], grads[15])
```

```python
import functools

import jax
import jax.numpy as jnp
from jax import lax
from jax.experimental import pallas as pl
from jax.experimental.pallas import tpu as pltpu
from jax.sharding import PartitionSpec as P

MESH = pl.DeviceIdType.MESH
ANY = pl.BlockSpec(memory_space=pl.ANY)
VMEM = pl.BlockSpec(memory_space=pltpu.VMEM)
DMA = pltpu.SemaphoreType.DMA
f32, bf16 = jnp.float32, jnp.bfloat16

CONV = 4
SCALE = 0.5
EPS = 1e-06
LANES = 128
RATE_AT = 64
HALO = 8


def shape(dims, kind):
    return jax.ShapeDtypeStruct(tuple(dims), kind)


def product(left, right, dims):
    return lax.dot_general(
        left.astype(bf16), right.astype(bf16), (dims, ((), ())), preferred_element_type=f32
    )


def mm(left, right):
    return product(left, right, ((1,), (0,)))


def mt(left, right):
    return product(left, right, ((1,), (1,)))


def tm(left, right):
    return product(left, right, ((0,), (0,)))


def params(collective, limit=58 << 20):
    return pltpu.CompilerParams(
        collective_id=collective, has_side_effects=True, vmem_limit_bytes=limit
    )


def grid_of(size):
    rows = lax.broadcasted_iota(jnp.int32, (size, size), 0)
    cols = lax.broadcasted_iota(jnp.int32, (size, size), 1)
    return rows, cols


def halves(values):
    high = values.astype(bf16)
    return high, (values - high.astype(f32)).astype(bf16)


def finer(left, right, dims):
    lhigh, llow = halves(left)
    rhigh, rlow = halves(right)
    (la,), (ra,) = dims
    return lax.dot_general(
        jnp.concatenate([lhigh, llow, lhigh], axis=la),
        jnp.concatenate([rhigh, rhigh, rlow], axis=ra),
        (dims, ((), ())),
        preferred_element_type=f32,
    )


def unit_inverses(stricts):
    size = stricts[0].shape[0]
    rows, cols = grid_of(size)
    eye = jnp.where(rows == cols, 1.0, 0.0)
    found = [eye - jnp.where((rows >> 1) == (cols >> 1), item, 0.0) for item in stricts]
    level = 1
    while (1 << level) < size:
        joined = ((rows >> (level + 1)) == (cols >> (level + 1))) & ((rows >> level) != (cols >> level))
        lows = [item.astype(bf16) for item in found]
        inner = [mm(jnp.where(joined, item, 0.0), low) for item, low in zip(stricts, lows)]
        found = [item - mm(low, part) for item, low, part in zip(found, lows, inner)]
        level += 1
    lows = [item.astype(bf16) for item in found]
    errors = []
    for item, low in zip(stricts, lows):
        pair = jnp.concatenate(halves(item), axis=1)
        errors.append(eye - low.astype(f32) - mm(pair, jnp.concatenate([low, low], axis=0)))
    return [low.astype(f32) + mm(low, error) for low, error in zip(lows, errors)]


def normed(values, gain):
    return values * lax.rsqrt(jnp.mean(values * values, axis=-1, keepdims=True) + EPS) * gain


def norm_back(values, gain, grad):
    scale = lax.rsqrt(jnp.mean(values * values, axis=-1, keepdims=True) + EPS)
    weighted = gain * grad
    return scale * weighted - values * (scale * scale * scale) * jnp.mean(
        values * weighted, axis=-1, keepdims=True
    )


def greet(barrier, peers):
    count = 0
    for peer, condition in peers:

        def tell(peer=peer):
            pl.semaphore_signal(barrier, inc=1, device_id=peer, device_id_type=MESH)

        if condition is None:
            tell()
            count = count + 1
        else:
            pl.when(condition)(tell)
            count = count + jnp.where(condition, 1, 0)
    pl.semaphore_wait(barrier, count)


def remote(source, target, send_sem, recv_sem, peer):
    return pltpu.make_async_remote_copy(
        src_ref=source,
        dst_ref=target,
        send_sem=send_sem,
        recv_sem=recv_sem,
        device_id=peer,
        device_id_type=MESH,
    )


def column(block, lane):
    return block[:, lane : lane + 1]


def convolved(ext_ref, taps, s, length, at, width):
    total = None
    for i in range(CONV):
        rows = ext_ref[s, pl.ds(HALO - (CONV - 1) + i, length), pl.ds(at, width)]
        term = taps[i : i + 1, at : at + width] * rows
        total = term if total is None else total + term
    return total


def kept(lens_ref, s, c, length):
    place = c * length + lax.broadcasted_iota(jnp.int32, (length, 1), 0)
    return jnp.where(place < lens_ref[s], 1.0, 0.0)


def part_of(at, size):
    return pl.ds(pl.multiple_of(at * size, size), size)


class Cube:
    def __init__(self, t, src, out, first, second, held, send_sem, recv_sem, chunks):
        self.y, self.x = t // 2, lax.rem(t, 2)
        self.t, self.src, self.out = t, src, out
        self.first, self.second, self.held = first, second, held
        self.send_sem, self.recv_sem = send_sem, recv_sem
        self.chunks = chunks
        self.block = src.shape[0] // 4
        self.half_width = src.shape[1] // 2
        self.width = self.half_width // chunks
        self.beside = self.y * 2 + (1 - self.x)
        self.above = (1 - self.y) * 2 + self.x

    def peer(self, side):
        return {"tp": self.beside * (1 - side) + self.above * side}

    def columns(self, half, chunk):
        return pl.ds(
            pl.multiple_of(half * self.half_width + chunk * self.width, self.width), self.width
        )

    def copy(self, stage, half, chunk, j):
        wide = self.columns(half, chunk)
        slim = part_of(chunk, self.width)
        send, recv = self.send_sem.at[stage, half, chunk, j], self.recv_sem.at[stage, half, chunk, j]
        across = self.above * (1 - half) + self.beside * half
        if stage == 0:
            g = (1 - half) * (2 * j + 1 - self.x) + half * (2 * (1 - self.y) + j)
            source, target = self.src.at[part_of(g, self.block), wide], self.first.at[half, j, :, slim]
            side = half
        elif stage == 1:
            source, target = self.held.at[half, :, slim], self.second.at[half, :, slim]
            side = 1 - half
        else:
            g = self.t if j == 0 else across
            source = target = self.out.at[part_of(g, self.block), wide]
            side = 1 - half if stage == 2 else half
        return remote(source, target, send, recv, self.peer(side))

    def each(self, body):
        @pl.loop(0, 2 * self.chunks)
        def _(k):
            body(lax.rem(k, 2), k // 2)

    def start(self, half, chunk):
        self.copy(0, half, chunk, 0).start()
        self.copy(0, half, chunk, 1).start()

    def middle(self):
        def body(half, chunk):
            wide = self.columns(half, chunk)
            slim = part_of(chunk, self.width)
            for j in range(2):
                self.copy(0, half, chunk, j).wait_recv()
            across = self.above * (1 - half) + self.beside * half
            other = (1 - half) * (1 - self.y) + half * (1 - self.x)
            self.held[half, :, slim] = (
                self.src[part_of(across, self.block), wide].astype(f32)
                + self.first[half, other, :, slim].astype(f32)
            ).astype(bf16)
            self.copy(1, half, chunk, 0).start()

        self.each(body)

    def finish(self, total_ref):
        def body(half, chunk):
            wide = self.columns(half, chunk)
            slim = part_of(chunk, self.width)
            self.copy(1, half, chunk, 0).wait_recv()
            mine = (1 - half) * self.y + half * self.x
            total_ref[:, wide] = (
                self.src[part_of(self.t, self.block), wide].astype(f32)
                + self.first[half, mine, :, slim].astype(f32)
                + self.second[half, :, slim].astype(f32)
            )

        self.each(body)

    def spread(self):
        def body(half, chunk):
            self.copy(2, half, chunk, 0).start()
            self.copy(3, half, chunk, 0).start()

        self.each(body)

    def relay(self):
        def body(half, chunk):
            self.copy(2, half, chunk, 0).wait_recv()
            self.copy(3, half, chunk, 1).start()

        self.each(body)

    def done(self):
        def body(half, chunk):
            for j in range(2):
                self.copy(3, half, chunk, j).wait_recv()
            for stage in range(4):
                for j in range(2 if stage in (0, 3) else 1):
                    self.copy(stage, half, chunk, j).wait_send()

        self.each(body)


class Tail:
    def __init__(self, t, src, out, got, send_sem, recv_sem, size):
        self.t, self.src, self.out, self.got, self.size = t, src, out, got, size
        self.send_sem, self.recv_sem = send_sem, recv_sem
        self.block = src.shape[0] // size

    def copies(self, stage):
        found = []
        for i in range(self.size - 1):
            g = lax.rem(self.t + 1 + i, self.size)
            if stage == 0:
                source, target = self.src.at[part_of(g, self.block)], self.got.at[self.size - 2 - i]
            else:
                source = target = self.out.at[part_of(self.t, self.block)]
            found.append(
                remote(
                    source,
                    target,
                    self.send_sem.at[stage, i],
                    self.recv_sem.at[stage, self.size - 2 - i],
                    {"tp": g},
                )
            )
        return found

    def start(self, stage):
        for copy in self.copies(stage):
            copy.start()

    def wait(self, stage):
        for copy in self.copies(stage):
            copy.wait_recv()

    def total(self):
        self.wait(0)
        total = self.src[part_of(self.t, self.block), :].astype(f32)
        for i in range(self.size - 1):
            total = total + self.got[i].astype(f32)
        return total

    def done(self):
        for stage in range(2):
            for copy in self.copies(stage):
                copy.wait_send()


CHUNKS = 4


def cube_scratch(rows, model):
    block = rows // 4
    return [
        pltpu.VMEM((rows, model), bf16),
        pltpu.VMEM((2, 2, block, model // 2), bf16),
        pltpu.VMEM((2, block, model // 2), bf16),
        pltpu.VMEM((2, block, model // 2), bf16),
        pltpu.VMEM((block, model), f32),
        DMA((4, 2, CHUNKS, 2)),
        DMA((4, 2, CHUNKS, 2)),
    ]


def tail_scratch(rows, size):
    return [
        pltpu.VMEM((rows, LANES), bf16),
        pltpu.VMEM((size - 1, rows // size, LANES), bf16),
        DMA((2, size - 1)),
        DMA((2, size - 1)),
    ]


def tp_peers(t, size):
    return [({"tp": lax.rem(t + 1 + i, size)}, None) for i in range(size - 1)]


def stacked(pieces):
    rows = sum(piece.shape[0] for piece in pieces)
    fill = jnp.zeros((LANES - rows, pieces[0].shape[1]), f32)
    return jnp.concatenate([piece.astype(f32) for piece in pieces] + [fill], axis=0).astype(bf16)


def slot_loads(pairs, f, sems):
    loads = []
    for i, (own, other, scratch) in enumerate(pairs):
        loads.append(pltpu.make_async_copy(own, scratch.at[f], sems.at[i, 0]))
        loads.append(pltpu.make_async_copy(other, scratch.at[1 - f], sems.at[i, 1]))
    for load in loads:
        load.start()
    return loads


def unit_steps(units, body):
    step = 2 * LANES
    whole = units // step

    @pl.loop(0, whole)
    def _(k):
        body(part_of(k, step))

    if units % step:
        body(pl.ds(whole * step, units % step))


def mixer_kernel(
    sizes,
    lens_ref,
    x_ref,
    gain_ref,
    qtaps_ref,
    ktaps_ref,
    vtaps_ref,
    wq_ref,
    wk_ref,
    wv_ref,
    wr_ref,
    wide0,
    wide1,
    wide2,
    wide3,
    wide4,
    wide5,
    wide6,
    wide7,
    slim0,
    slim1,
    slim2,
    slim3,
    slim4,
    slim5,
    slim6,
    slim7,
    wo_ref,
    wg_ref,
    wu_ref,
    wd_ref,
    n1_ref,
    wqkv_out,
    wo_out,
    wg_out,
    wu_out,
    wd_out,
    wide_out,
    slim_out,
    into_ref,
    back_ref,
    ext_ref,
    inner_ref,
    rates_ref,
    inv_ref,
    wkey_ref,
    wval_ref,
    reach_ref,
    local_ref,
    map_ref,
    end_ref,
    w_ref,
    wr_all,
    halo_out,
    halo_in,
    back_f32,
    into_f32,
    send_sem,
    recv_sem,
    local_sem,
    store_sem,
    halo_send,
    halo_recv,
):
    seqs, length, heads, width, ctx_size = sizes
    cols = heads * width
    rows = seqs * length
    half = wq_ref.shape[0]
    model = 2 * half
    f = lax.axis_index("fsdp")
    c = lax.axis_index("ctx")
    mate = {"fsdp": 1 - f}
    greet(
        pltpu.get_barrier_semaphore(),
        [(mate, None), ({"ctx": c - 1}, c > 0), ({"ctx": c + 1}, c < ctx_size - 1)],
    )
    top = pl.ds(pl.multiple_of(f * half, half), half)
    moves = []
    for i, ref in enumerate((wide0, wide1, wide2, wide3, wide4, wide5, wide6, wide7)):
        moves.append((ref, wide_out.at[f, i]))
    at = 0
    for ref in (slim0, slim1, slim2, slim3, slim4, slim5, slim6, slim7):
        moves.append((ref, slim_out.at[f, :, at : at + ref.shape[1]]))
        at += ref.shape[1]
    moves += [
        (wr_ref, wr_all.at[:, top]),
        (wq_ref, w_ref.at[0, top]),
        (wk_ref, w_ref.at[1, top]),
        (wv_ref, w_ref.at[2, top]),
    ]
    near = [pltpu.make_async_copy(src, dst, local_sem.at[i]) for i, (src, dst) in enumerate(moves)]
    local_count = len(moves)
    moves += [(wo_ref, wo_out), (wg_ref, wg_out), (wu_ref, wu_out), (wd_ref, wd_out)]
    across = [
        remote(src, dst, send_sem.at[i], recv_sem.at[i], mate) for i, (src, dst) in enumerate(moves)
    ]
    for copy in across[:local_count] + near + across[local_count:]:
        copy.start()

    @pl.loop(0, seqs)
    def _(s):
        here = pl.ds(pl.multiple_of(s * length, length), length)
        n1_ref[here, :] = normed(x_ref[here, :].astype(f32), gain_ref[...]).astype(bf16)

    for i in range(local_count):
        near[i].wait()
        across[i].wait_recv()
    kinds = 4
    into_f32[...] = jnp.zeros_like(into_f32)
    back_f32[...] = jnp.zeros_like(back_f32)
    for core in range(2):
        for kind in range(kinds):
            spot = core * 32 + kind * 8
            into_f32[spot : spot + 8, :] = wide_out[core, kind].astype(f32)
        for kind in range(kinds):
            at = kind * cols
            wide = cols if kind < 3 else LANES
            back_f32[core * 32 + kind * 8 : core * 32 + kind * 8 + 8, at : at + wide] = slim_out[
                core, :, at : at + wide
            ].astype(f32)
    into_f32[RATE_AT : RATE_AT + 8, :] = wr_all[...].astype(f32)
    into_ref[...] = into_f32[...].astype(bf16)
    back_ref[...] = back_f32[...].astype(bf16)
    keep_w = [
        pltpu.make_async_copy(w_ref.at[i], wqkv_out.at[i], store_sem.at[i]) for i in range(3)
    ]
    for copy in keep_w:
        copy.start()

    @pl.loop(0, seqs)
    def _(s):
        here = pl.ds(pl.multiple_of(s * length, length), length)
        block = n1_ref[here, :]
        tail = mt(block, into_ref[...])
        inner = tail.astype(bf16)
        inner_ref[here, :] = inner
        for i in range(3):
            pre = mm(block, w_ref[i]) + SCALE * mm(inner, back_ref[:, i * cols : (i + 1) * cols])
            ext_ref[s, HALO : HALO + length, i * cols : (i + 1) * cols] = pre
            halo_out[s, :, i * cols : (i + 1) * cols] = pre[length - HALO :, :].astype(bf16)
        pre_rate = tail + SCALE * mm(inner, back_ref[:, 3 * cols :])
        rates_ref[here, :] = jax.nn.sigmoid(pre_rate) * kept(lens_ref, s, c, length)

    halo = remote(halo_out, halo_in, halo_send, halo_recv, {"ctx": c + 1})

    @pl.when(c < ctx_size - 1)
    def _():
        halo.start()

    @pl.when(c > 0)
    def _():
        halo.wait_recv()
        ext_ref[:, 0:HALO, :] = halo_in[...].astype(f32)

    @pl.when(c == 0)
    def _():
        ext_ref[:, 0:HALO, :] = jnp.zeros((seqs, HALO, 3 * cols), f32)

    taps = jnp.concatenate([qtaps_ref[...], ktaps_ref[...], vtaps_ref[...]], axis=1)
    row_at, col_at = grid_of(length)

    @pl.loop(0, seqs)
    def _(s):
        here = pl.ds(pl.multiple_of(s * length, length), length)
        rate_block = rates_ref[here, :]
        queries, keys, values, rates, stricts = [], [], [], [], []
        for h in range(heads):
            at = h * width
            parts = [
                jax.nn.silu(convolved(ext_ref, taps, s, length, i * cols + at, width))
                for i in range(3)
            ]
            query, key = [
                a * lax.rsqrt(jnp.sum(a * a, axis=-1, keepdims=True) + EPS) for a in parts[:2]
            ]
            rate = column(rate_block, RATE_AT + h)
            queries.append(query)
            keys.append(key)
            values.append(parts[2])
            rates.append(rate)
            stricts.append(
                jnp.where(row_at > col_at, rate * finer(key, key, ((1,), (1,))), 0.0)
            )
        inverses = unit_inverses(stricts)
        for h in range(heads):
            pair = s * heads + h
            query, key, value, rate, inverse = queries[h], keys[h], values[h], rates[h], inverses[h]
            wkey = mm(inverse, rate * key)
            wval = mm(inverse, rate * value)
            scores = jnp.where(row_at >= col_at, mt(query, key), 0.0)
            inv_ref[pair] = inverse.astype(bf16)
            wkey_ref[pair] = wkey.astype(bf16)
            wval_ref[pair] = wval
            reach_ref[pair] = (query - mm(scores, wkey)).astype(bf16)
            local_ref[pair] = mm(scores, wval)
            map_ref[pair] = (jnp.where(row_at == col_at, 1.0, 0.0) - tm(key, wkey)).astype(bf16)
            end_ref[pair] = tm(key, wval)

    for copy in across[local_count:]:
        copy.wait_recv()
    for copy in keep_w:
        copy.wait()
    for copy in across:
        copy.wait_send()

    @pl.when(c < ctx_size - 1)
    def _():
        halo.wait_send()


def attend_kernel(
    sizes,
    lens_ref,
    x_ref,
    gain_ref,
    head_gain_ref,
    map_ref,
    end_ref,
    reach_ref,
    local_ref,
    wide_ref,
    slim_ref,
    grad_ref,
    wo_own,
    wo_other,
    wd_own,
    wd_other,
    n2_ref,
    out_inner_ref,
    resid_ref,
    heads_ref,
    start_ref,
    active_ref,
    down_inner_ref,
    chain_out,
    wo_ref,
    wd_ref,
    load_sem,
    chain_send,
    chain_recv,
    *scratch,
):
    seqs, length, heads, width, ctx_size, tp_size = sizes
    cols = heads * width
    model = x_ref.shape[1]
    half_model = model // 2
    units = active_ref.shape[1]
    left_at = 3 * cols + LANES
    down_at = left_at + cols + 2 * units
    f = lax.axis_index("fsdp")
    c = lax.axis_index("ctx")
    t = lax.axis_index("tp")
    loads = slot_loads([(wo_own, wo_other, wo_ref), (wd_own, wd_other, wd_ref)], f, load_sem)
    greet(
        pltpu.get_barrier_semaphore(),
        [({"ctx": c - 1}, c > 0), ({"ctx": c + 1}, c < ctx_size - 1)] + tp_peers(t, tp_size),
    )
    src, first, second, held, total_ref, send_sem, recv_sem = scratch[:7]
    tail_src, tail_got, tail_send, tail_recv = scratch[7:]
    cube = Cube(t, src, n2_ref, first, second, held, send_sem, recv_sem, CHUNKS)
    tail = Tail(t, tail_src, out_inner_ref, tail_got, tail_send, tail_recv, tp_size)
    gain = head_gain_ref[...]

    @pl.loop(0, seqs)
    def _(s):
        pairs = pl.ds(s * heads, heads)
        hop = remote(
            chain_out.at[s], start_ref.at[pairs], chain_send.at[s], chain_recv.at[s], {"ctx": c + 1}
        )

        @pl.when(c > 0)
        def _():
            hop.wait_recv()

        @pl.when(c == 0)
        def _():
            start_ref[pairs] = jnp.zeros((heads, width, width), bf16)

        @pl.when(c < ctx_size - 1)
        def _():
            for h in range(heads):
                pair = s * heads + h
                chain_out[s, h] = (mm(map_ref[pair], start_ref[pair]) + end_ref[pair]).astype(bf16)
            hop.start()

        here = part_of(s, length)
        for h in range(heads):
            pair = s * heads + h
            mixed = mm(reach_ref[pair], start_ref[pair]) + local_ref[pair]
            heads_ref[here, h * width : (h + 1) * width] = normed(mixed, gain).astype(bf16)

    into = stacked([slim_ref[core, :, left_at : left_at + cols] for core in range(2)])
    low = heads_ref[...]
    tail_src[...] = mt(low, into).astype(bf16)
    tail.start(0)
    loads[0].wait()
    loads[1].wait()

    def project(half, chunk):
        src[:, cube.columns(half, chunk)] = mm(
            heads_ref[...], wo_ref[half, :, part_of(chunk, cube.width)]
        ).astype(bf16)
        cube.start(half, chunk)

    cube.each(project)
    down_from = stacked([wide_ref[core, 7] for core in range(2)])
    for s in range(seqs):
        here = pl.ds(s * length, length)
        down_inner_ref[here, :] = (
            kept(lens_ref, s, c, length) * (SCALE * mt(grad_ref[here, :], down_from))
        ).astype(bf16)
    loads[2].wait()
    loads[3].wait()

    def activate(at):
        into_down = stacked([slim_ref[core, :, pl.ds(down_at + at.start, at.size)] for core in range(2)])
        part = mt(grad_ref[:, :half_model], wd_ref[0, at, :])
        part = part + mt(grad_ref[:, half_model:], wd_ref[1, at, :])
        part = part + mm(down_inner_ref[...], into_down)
        for s in range(seqs):
            active_ref[s * length : (s + 1) * length, at] = (
                kept(lens_ref, s, c, length) * part[s * length : (s + 1) * length]
            )

    unit_steps(units, activate)
    cube.middle()
    cube.finish(total_ref)
    inner = tail.total().astype(bf16)
    here = part_of(t, length)
    right = stacked([wide_ref[core, 6] for core in range(2)])
    resid = x_ref[here, :].astype(f32) + total_ref[...] + SCALE * mm(inner, right)
    resid_ref[...] = resid
    out_inner_ref[here, :] = inner
    n2_ref[here, :] = normed(resid, gain_ref[...]).astype(bf16)
    cube.spread()
    tail.start(1)
    cube.relay()
    tail.wait(1)
    cube.done()
    tail.done()

    @pl.when(c < ctx_size - 1)
    def _():
        @pl.loop(0, seqs)
        def _(s):
            remote(
                chain_out.at[s],
                start_ref.at[pl.ds(0, heads)],
                chain_send.at[s],
                chain_recv.at[s],
                {"ctx": c + 1},
            ).wait_send()


def feed_kernel(
    sizes,
    lens_ref,
    n2_ref,
    active_ref,
    resid_ref,
    gain_ref,
    wide_ref,
    slim_ref,
    down_grad_ref,
    grad_ref,
    wg_own,
    wg_other,
    wu_own,
    wu_other,
    wd_own,
    wd_other,
    low_ref,
    inner_grad_ref,
    gresid_ref,
    down_ref,
    down_tail_ref,
    gate_right_ref,
    up_right_ref,
    down_left_ref,
    wg_ref,
    wu_ref,
    wd_ref,
    act_ref,
    dgate_ref,
    dup_ref,
    inner_ref,
    back_gate,
    back_up,
    own_grad,
    load_sem,
    grad_sem,
    *scratch,
):
    seqs, length, cols, ctx_size, tp_size = sizes
    model = n2_ref.shape[1]
    half_model = model // 2
    units = active_ref.shape[1]
    gate_at = 4 * cols + LANES
    up_at = gate_at + units
    down_at = up_at + units
    f = lax.axis_index("fsdp")
    c = lax.axis_index("ctx")
    t = lax.axis_index("tp")
    loads = slot_loads(
        [(wg_own, wg_other, wg_ref), (wu_own, wu_other, wu_ref), (wd_own, wd_other, wd_ref)],
        f,
        load_sem,
    )
    here = part_of(t, length)
    own_load = pltpu.make_async_copy(grad_ref.at[here], own_grad, grad_sem)
    own_load.start()
    greet(pltpu.get_barrier_semaphore(), tp_peers(t, tp_size))
    src, first, second, held, total_ref, send_sem, recv_sem = scratch[:7]
    tail_src, tail_got, tail_send, tail_recv = scratch[7:]
    cube = Cube(t, src, low_ref, first, second, held, send_sem, recv_sem, CHUNKS)
    tail = Tail(t, tail_src, inner_grad_ref, tail_got, tail_send, tail_recv, tp_size)
    into = stacked([wide_ref[core, 4 + kind] for core in range(2) for kind in range(2)])
    blank = jnp.zeros((8, units), bf16)
    gates = [slim_ref[core, :, gate_at : gate_at + units] for core in range(2)]
    ups = [slim_ref[core, :, up_at : up_at + units] for core in range(2)]
    back_gate[...] = stacked([gates[0], blank, gates[1], blank])
    back_up[...] = stacked([blank, ups[0], blank, ups[1]])
    inner_ref[...] = mt(n2_ref[...], into).astype(bf16)
    for load in loads[:4]:
        load.wait()

    def forward(at):
        pre = []
        for weight, back in ((wg_ref, back_gate), (wu_ref, back_up)):
            part = mm(n2_ref[:, :half_model], weight[0, :, at])
            part = part + mm(n2_ref[:, half_model:], weight[1, :, at])
            pre.append(part + SCALE * mm(inner_ref[...], back[:, at]))
        gate, up = pre
        sigma = jax.nn.sigmoid(gate)
        silu = gate * sigma
        active = active_ref[:, at]
        act_ref[:, at] = (silu * up).astype(bf16)
        dgate_ref[:, at] = (active * up * (sigma * (1.0 + gate * (1.0 - sigma)))).astype(bf16)
        dup_ref[:, at] = (active * silu).astype(bf16)

    unit_steps(units, forward)
    tail_src[...] = (
        SCALE * (mt(dgate_ref[...], back_gate[...]) + mt(dup_ref[...], back_up[...]))
    ).astype(bf16)
    tail.start(0)

    def project(half, chunk):
        rows = part_of(chunk, cube.width)
        src[:, cube.columns(half, chunk)] = (
            mt(dgate_ref[...], wg_ref[half, rows, :]) + mt(dup_ref[...], wu_ref[half, rows, :])
        ).astype(bf16)
        cube.start(half, chunk)

    cube.each(project)
    cube.middle()
    for load in loads[4:]:
        load.wait()

    def descend(half, chunk):
        down_ref[:, cube.columns(half, chunk)] = mm(
            act_ref[...], wd_ref[half, :, part_of(chunk, cube.width)]
        ).astype(bf16)

    cube.each(descend)
    cube.finish(total_ref)
    own_load.wait()
    inner = tail.total().astype(bf16)
    grad_second = total_ref[...] + mm(inner, into)
    grad = own_grad[...].astype(f32) * kept(lens_ref, t, c, length) + norm_back(
        resid_ref[...], gain_ref[...], grad_second
    )
    gresid_ref[...] = grad
    low_ref[here, :] = grad.astype(bf16)
    inner_grad_ref[here, :] = inner
    cube.spread()
    tail.start(1)
    into_down = stacked([slim_ref[core, :, down_at : down_at + units] for core in range(2)])
    down_tail_ref[...] = mt(act_ref[...], into_down).astype(bf16)
    gate_right_ref[...] = SCALE * tm(inner_ref[...], dgate_ref[...])
    cube.relay()
    up_right_ref[...] = SCALE * tm(inner_ref[...], dup_ref[...])
    down_left_ref[...] = tm(down_grad_ref[...], act_ref[...])
    tail.wait(1)
    cube.done()
    tail.done()


def back_kernel(
    sizes,
    lens_ref,
    low_ref,
    head_gain_ref,
    start_ref,
    map_ref,
    reach_ref,
    local_ref,
    inv_ref,
    wkey_ref,
    wval_ref,
    ext_ref,
    qtaps_ref,
    ktaps_ref,
    vtaps_ref,
    rates_ref,
    wide_ref,
    slim_ref,
    wo_own,
    wo_other,
    heads_ref,
    out_inner_ref,
    src,
    tail_src,
    resid_ref,
    grad_ref,
    n2_ref,
    feed_grad_ref,
    pre_ref,
    block_ref,
    out_left_ref,
    out_right_ref,
    down_right_ref,
    feed_left_ref,
    wo_ref,
    dheads_ref,
    dmix_ref,
    after_ref,
    chain_out,
    gconv_ref,
    halo_out,
    halo_in,
    down_inner_ref,
    load_sem,
    chain_send,
    chain_recv,
    halo_send,
    halo_recv,
    *scratch,
):
    seqs, length, heads, width, ctx_size, tp_size = sizes
    cols = heads * width
    model = low_ref.shape[1]
    half_model = model // 2
    left_at = 3 * cols + LANES
    f = lax.axis_index("fsdp")
    c = lax.axis_index("ctx")
    t = lax.axis_index("tp")
    loads = slot_loads([(wo_own, wo_other, wo_ref)], f, load_sem)
    greet(
        pltpu.get_barrier_semaphore(),
        [({"ctx": c - 1}, c > 0), ({"ctx": c + 1}, c < ctx_size - 1)] + tp_peers(t, tp_size),
    )
    first, second, held, total_ref, send_sem, recv_sem = scratch[:6]
    tail_got, tail_send, tail_recv = scratch[6:]
    cube = Cube(t, src, block_ref, first, second, held, send_sem, recv_sem, CHUNKS)
    tail = Tail(t, tail_src, down_inner_ref, tail_got, tail_send, tail_recv, tp_size)
    cube.each(cube.start)
    tail.start(0)
    mine = part_of(t, length)
    gain = head_gain_ref[...]
    taps = jnp.concatenate([qtaps_ref[...], ktaps_ref[...], vtaps_ref[...]], axis=1)
    row_at, col_at = grid_of(length)
    gconv_ref[...] = jnp.zeros_like(gconv_ref)
    from_out = stacked([wide_ref[core, 6] for core in range(2)])
    into_out = stacked([slim_ref[core, :, left_at : left_at + cols] for core in range(2)])
    inner_grad = (SCALE * mt(low_ref[...], from_out)).astype(bf16)
    for load in loads:
        load.wait()
    dheads_ref[...] = (
        mt(low_ref[:, :half_model], wo_ref[0])
        + mt(low_ref[:, half_model:], wo_ref[1])
        + mm(inner_grad, into_out)
    )
    out_left_ref[...] = tm(inner_grad, heads_ref[...])

    @pl.loop(0, seqs)
    def _(s):
        here = part_of(s, length)
        pairs = pl.ds(s * heads, heads)
        hop = remote(
            chain_out.at[s], after_ref.at[pairs], chain_send.at[s], chain_recv.at[s], {"ctx": c - 1}
        )
        for h in range(heads):
            pair = s * heads + h
            mixed = mm(reach_ref[pair], start_ref[pair]) + local_ref[pair]
            dmix_ref[pair] = norm_back(mixed, gain, dheads_ref[here, h * width : (h + 1) * width])

        @pl.when(c < ctx_size - 1)
        def _():
            hop.wait_recv()

        @pl.when(c == ctx_size - 1)
        def _():
            after_ref[pairs] = jnp.zeros((heads, width, width), bf16)

        @pl.when(c > 0)
        def _():
            for h in range(heads):
                pair = s * heads + h
                chain_out[s, h] = (
                    tm(map_ref[pair], after_ref[pair]) + tm(reach_ref[pair], dmix_ref[pair])
                ).astype(bf16)
            hop.start()

    cube.middle()

    @pl.loop(0, seqs)
    def _(s):
        here = part_of(s, length)
        rate_block = rates_ref[here, :]
        rate_grads = jnp.zeros((length, LANES), f32)
        lane = lax.broadcasted_iota(jnp.int32, (length, LANES), 1)
        for h in range(heads):
            pair = s * heads + h
            at = h * width
            convs = [convolved(ext_ref, taps, s, length, i * cols + at, width) for i in range(3)]
            sigmas = [jax.nn.sigmoid(a) for a in convs]
            acts = [a * b for a, b in zip(convs, sigmas)]
            scales = [
                lax.rsqrt(jnp.sum(a * a, axis=-1, keepdims=True) + EPS) for a in acts[:2]
            ]
            query, key = [a * b for a, b in zip(acts, scales)]
            value = acts[2]
            rate = column(rate_block, RATE_AT + h)
            start, after = start_ref[pair], after_ref[pair]
            dmix = dmix_ref[pair]
            inverse = inv_ref[pair]
            fresh = wval_ref[pair] - mm(wkey_ref[pair], start)
            products = mt(key, key)
            scores = jnp.where(row_at >= col_at, mt(query, key), 0.0)
            dfresh = tm(scores, dmix) + mm(key, after)
            dvalue = tm(inverse, dfresh)
            dkey_in = -mt(dvalue, start)
            dscores = jnp.where(row_at >= col_at, mt(dmix, fresh), 0.0)
            dquery = mt(dmix, start) + mm(dscores, key)
            dstrict = jnp.where(row_at > col_at, -mt(dvalue, fresh), 0.0)
            dprod = rate * dstrict
            dkey = (
                tm(dscores, query)
                + mt(fresh, after)
                + rate * dkey_in
                + mm(dprod, key)
                + tm(dprod, key)
            )
            drate = jnp.sum(dstrict * products + dvalue * value + dkey_in * key, axis=-1, keepdims=True)
            grads = [
                scale * grad - act * (scale * scale * scale) * jnp.sum(act * grad, axis=-1, keepdims=True)
                for act, scale, grad in zip(acts, scales, (dquery, dkey))
            ] + [rate * dvalue]
            for i in range(3):
                slope = sigmas[i] * (1.0 + convs[i] * (1.0 - sigmas[i]))
                gconv_ref[pl.ds(HALO, length), pl.ds(i * cols + at, width)] = grads[i] * slope
            rate_grads = rate_grads + jnp.where(
                lane == RATE_AT + h, drate * rate * (1.0 - rate), 0.0
            )
        for i in range(3 * heads):
            at = i * width
            total = None
            spill = None
            for j in range(CONV):
                tap = taps[j : j + 1, at : at + width]
                term = tap * gconv_ref[pl.ds(HALO + CONV - 1 - j, length), pl.ds(at, width)]
                edge = tap * gconv_ref[pl.ds(CONV - 1 - j, HALO), pl.ds(at, width)]
                total = term if total is None else total + term
                spill = edge if spill is None else spill + edge
            pre_ref[here, at : at + width] = total.astype(bf16)
            halo_out[0, s, :, at : at + width] = total[length - HALO :, :]
            halo_out[1, s, :, at : at + width] = spill
        pre_ref[here, 3 * cols :] = rate_grads.astype(bf16)

        @pl.when(s == 1)
        def _():
            cube.finish(total_ref)
            inner = tail.total().astype(bf16)
            right = stacked([wide_ref[core, 7] for core in range(2)])
            final = resid_ref[...] + total_ref[...] + SCALE * mm(inner, right)
            block_ref[mine, :] = (kept(lens_ref, t, c, length) * final).astype(bf16)
            down_inner_ref[mine, :] = inner
            cube.spread()
            tail.start(1)

        @pl.when(s == 2)
        def _():
            cube.relay()

    halo_in[1] = halo_out[1].astype(bf16)
    halo = remote(halo_in.at[1], halo_in.at[0], halo_send, halo_recv, {"ctx": c - 1})

    @pl.when(c > 0)
    def _():
        halo.start()

    @pl.when(c < ctx_size - 1)
    def _():
        halo.wait_recv()
        for s in range(seqs):
            last = s * length + length - 16
            block = pre_ref[last : last + 16, : 3 * cols].astype(f32)
            edge = (halo_out[0, s] + halo_in[0, s].astype(f32))
            pre_ref[last : last + 16, : 3 * cols] = jnp.concatenate(
                [block[:HALO], edge], axis=0
            ).astype(bf16)

    @pl.when(c > 0)
    def _():
        halo.wait_send()

        @pl.loop(0, seqs)
        def _(s):
            remote(
                chain_out.at[s], after_ref.at[pl.ds(0, heads)], chain_send.at[s], chain_recv.at[s],
                {"ctx": c - 1},
            ).wait_send()
    out_right_ref[...] = SCALE * tm(out_inner_ref[...], low_ref[...])
    feed_left_ref[...] = tm(feed_grad_ref[...], n2_ref[...])
    tail.wait(1)
    masked = jnp.concatenate(
        [
            kept(lens_ref, s, c, length) * down_inner_ref[s * length : (s + 1) * length, :].astype(f32)
            for s in range(seqs)
        ],
        axis=0,
    )
    down_right_ref[...] = SCALE * tm(masked, grad_ref[...])
    cube.done()
    tail.done()


def first_kernel(
    sizes,
    pre_ref,
    w_ref,
    back_ref,
    into_ref,
    x_ref,
    gain_ref,
    gresid_ref,
    n1_ref,
    inner_ref,
    grad_ref,
    left_ref,
    right_ref,
    inner_grad_ref,
    *scratch,
):
    (tp_size,) = sizes
    t = lax.axis_index("tp")
    block = x_ref.shape[0] // tp_size
    half_model = x_ref.shape[1] // 2
    cols = w_ref.shape[2]
    greet(pltpu.get_barrier_semaphore(), tp_peers(t, tp_size))
    src, first, second, held, total_ref, send_sem, recv_sem = scratch[:7]
    tail_src, tail_got, tail_send, tail_recv = scratch[7:]
    cube = Cube(t, src, grad_ref, first, second, held, send_sem, recv_sem, CHUNKS)
    tail = Tail(t, tail_src, inner_grad_ref, tail_got, tail_send, tail_recv, tp_size)
    tail_src[...] = (SCALE * mt(pre_ref[...], back_ref[...])).astype(bf16)
    tail.start(0)

    def project(half, chunk):
        rows = cube.columns(half, chunk)
        part = mm(pre_ref[:, 3 * cols :], into_ref[:, rows])
        for i in range(3):
            part = part + mt(pre_ref[:, i * cols : (i + 1) * cols], w_ref[i, rows, :])
        src[:, rows] = part.astype(bf16)
        cube.start(half, chunk)

    cube.each(project)
    inner = tail.total().astype(bf16)
    here = part_of(t, block)
    inner_grad_ref[here, :] = inner
    tail.start(1)
    cube.middle()
    right_ref[...] = SCALE * tm(inner_ref[...], pre_ref[...])
    tail.wait(1)
    left_ref[...] = tm(inner_grad_ref[...], n1_ref[...])
    cube.finish(total_ref)
    grad_first = total_ref[...] + mm(inner, into_ref[...])
    grad = gresid_ref[...] + norm_back(x_ref[here, :].astype(f32), gain_ref[...], grad_first)
    grad_ref[here, :] = grad.astype(bf16)
    cube.spread()
    cube.relay()
    cube.done()
    tail.done()


def share_kernel(sizes, strips, *refs):
    ctx_size, wide = sizes
    count = len(refs) - 10
    ins, outs, (pack, mate_in, mine, recv, summed, send_sem, recv_sem, part_send, part_recv) = (
        refs[:count],
        refs[count : count + 1],
        refs[count + 1 :],
    )
    f = lax.axis_index("fsdp")
    c = lax.axis_index("ctx")
    mate = {"fsdp": 1 - f}
    others = [({"ctx": lax.rem(c + 1 + i, ctx_size)}, None) for i in range(ctx_size - 1)]
    greet(pltpu.get_barrier_semaphore(), [(mate, None)] + others)
    part = wide // ctx_size
    used = sum(strip[4] for strip in strips)
    for core in range(2):
        at = 0
        for index, row, step, col, width in strips:
            rows = row + core * step
            pack[core, :, at : at + width] = ins[index][rows : rows + 8, col : col + width].astype(bf16)
            at += width
        pack[core, :, used:] = jnp.zeros((8, wide - used), bf16)
    swap = remote(pack.at[1 - f], mate_in, send_sem, recv_sem, mate)
    swap.start()
    swap.wait()
    both = (pack[f].astype(f32) + mate_in[...].astype(f32)).astype(bf16)
    for j in range(ctx_size):
        mine[j] = both[:, j * part : (j + 1) * part]
    sends = []
    for i in range(ctx_size - 1):
        j = lax.rem(c + 1 + i, ctx_size)
        sends.append(
            remote(
                mine.at[j],
                recv.at[ctx_size - 2 - i],
                part_send.at[0, i],
                part_recv.at[0, ctx_size - 2 - i],
                {"ctx": j},
            )
        )
    for copy in sends:
        copy.start()
    for copy in sends:
        copy.wait_recv()
    total = mine[c].astype(f32)
    for i in range(ctx_size - 1):
        total = total + recv[i].astype(f32)
    summed[c] = total.astype(bf16)
    spreads = []
    for i in range(ctx_size - 1):
        j = lax.rem(c + 1 + i, ctx_size)
        spreads.append(
            remote(
                summed.at[c],
                summed.at[c],
                part_send.at[1, i],
                part_recv.at[1, ctx_size - 2 - i],
                {"ctx": j},
            )
        )
    for copy in spreads:
        copy.start()
    for copy in spreads:
        copy.wait_recv()
    for j in range(ctx_size):
        outs[0][:, j * part : (j + 1) * part] = summed[j].astype(f32)
    for copy in sends + spreads:
        copy.wait_send()


def deal_kernel(strips, packed_ref, *outs):
    at = 0
    for out, strip in zip(outs, strips):
        out[...] = packed_ref[:, at : at + strip[4]]
        at += strip[4]


def local(ctx_size, tp_size, *arguments):
    (
        hidden_in,
        seq_lengths,
        mixer_gain,
        feed_gain,
        query_weight,
        key_weight,
        value_weight,
        rate_weight,
        query_conv,
        key_conv,
        value_conv,
        head_gain,
        output_weight,
        gate_weight,
        up_weight,
        down_weight,
        query_left,
        query_right,
        key_left,
        key_right,
        value_left,
        value_right,
        rate_left,
        rate_right,
        output_left,
        output_right,
        gate_left,
        gate_right,
        up_left,
        up_right,
        down_left,
        down_right,
        output_grad,
    ) = arguments
    seqs, length, model = hidden_in.shape
    heads = rate_weight.shape[1]
    width = head_gain.shape[0]
    cols = heads * width
    rows = seqs * length
    units = gate_weight.shape[1]
    half = query_weight.shape[0]
    pairs = seqs * heads
    x = hidden_in.reshape(rows, model)
    grad_rows = output_grad.reshape(rows, model)
    rate_from = jnp.pad(rate_right, ((0, 0), (RATE_AT, LANES - RATE_AT - heads)))
    rate_rows = jnp.pad(rate_weight.T, ((0, 8 - heads), (0, 0)))
    wides = (
        query_left.T,
        key_left.T,
        value_left.T,
        rate_left.T,
        gate_left.T,
        up_left.T,
        output_right,
        down_right,
    )
    slims = (
        query_right,
        key_right,
        value_right,
        rate_from,
        output_left.T,
        gate_right,
        up_right,
        down_left.T,
    )
    slim_wide = sum(item.shape[1] for item in slims)
    gain1, gain2, gain3 = mixer_gain[None, :], feed_gain[None, :], head_gain[None, :]
    ext = length + HALO
    square = (pairs, width, width)
    tall = (pairs, length, width)
    block = rows // tp_size
    smem = pl.BlockSpec(memory_space=pltpu.SMEM)
    (
        n1,
        wqkv,
        wo,
        wg,
        wu,
        wd,
        wide_all,
        slim_all,
        into,
        back,
        pre_ext,
        inner,
        rates,
        inverse,
        wkey,
        wval,
        reach,
        local_out,
        step_map,
        end_state,
    ) = pl.pallas_call(
        functools.partial(mixer_kernel, (seqs, length, heads, width, ctx_size)),
        out_shape=(
            shape((rows, model), bf16),
            shape((3, model, cols), bf16),
            shape(output_weight.shape, bf16),
            shape(gate_weight.shape, bf16),
            shape(up_weight.shape, bf16),
            shape(down_weight.shape, bf16),
            shape((2, 8, 8, model), bf16),
            shape((2, 8, slim_wide), bf16),
            shape((LANES, model), bf16),
            shape((LANES, 3 * cols + LANES), bf16),
            shape((seqs, ext, 3 * cols), f32),
            shape((rows, LANES), bf16),
            shape((rows, LANES), f32),
            shape((pairs, length, length), bf16),
            shape(tall, bf16),
            shape(tall, f32),
            shape(tall, bf16),
            shape(tall, f32),
            shape(square, bf16),
            shape(square, f32),
        ),
        in_specs=[smem] + [VMEM] * 5 + [ANY] * 24,
        out_specs=(VMEM,) + (ANY,) * 5 + (VMEM,) * 14,
        scratch_shapes=[
            pltpu.VMEM((3, model, cols), bf16),
            pltpu.VMEM((8, model), bf16),
            pltpu.VMEM((seqs, HALO, 3 * cols), bf16),
            pltpu.VMEM((seqs, HALO, 3 * cols), bf16),
            pltpu.VMEM((LANES, 3 * cols + LANES), f32),
            pltpu.VMEM((LANES, model), f32),
            DMA((24,)),
            DMA((24,)),
            DMA((20,)),
            DMA((3,)),
            DMA,
            DMA,
        ],
        compiler_params=params(0),
        name="mixer",
    )(
        seq_lengths,
        x,
        gain1,
        query_conv,
        key_conv,
        value_conv,
        query_weight,
        key_weight,
        value_weight,
        rate_rows,
        *wides,
        *slims,
        output_weight,
        gate_weight,
        up_weight,
        down_weight,
    )
    mixer_sizes = (seqs, length, heads, width, ctx_size, tp_size)
    second, out_inner, residual, heads_low, start, active, down_grad = pl.pallas_call(
        functools.partial(attend_kernel, mixer_sizes),
        out_shape=(
            shape((rows, model), bf16),
            shape((rows, LANES), bf16),
            shape((block, model), f32),
            shape((rows, cols), bf16),
            shape(square, bf16),
            shape((rows, units), f32),
            shape((rows, LANES), bf16),
        ),
        in_specs=[smem] + [VMEM] * 10 + [ANY] * 4,
        out_specs=(VMEM,) * 7,
        scratch_shapes=[
            pltpu.VMEM((seqs, heads, width, width), bf16),
            pltpu.VMEM((2,) + output_weight.shape, bf16),
            pltpu.VMEM((2,) + down_weight.shape, bf16),
            DMA((2, 2)),
            DMA((seqs,)),
            DMA((seqs,)),
        ]
        + cube_scratch(rows, model)
        + tail_scratch(rows, tp_size),
        compiler_params=params(1),
        name="attend",
    )(
        seq_lengths,
        x,
        gain2,
        gain3,
        step_map,
        end_state,
        reach,
        local_out,
        wide_all,
        slim_all,
        grad_rows,
        output_weight,
        wo,
        down_weight,
        wd,
    )
    (
        resid_low,
        feed_grad,
        grad_residual,
        down_part,
        down_tail,
        gate_right_grad,
        up_right_grad,
        down_left_grad,
    ) = pl.pallas_call(
        functools.partial(feed_kernel, (seqs, length, cols, ctx_size, tp_size)),
        out_shape=(
            shape((rows, model), bf16),
            shape((rows, LANES), bf16),
            shape((block, model), f32),
            shape((rows, model), bf16),
            shape((rows, LANES), bf16),
            shape((LANES, units), f32),
            shape((LANES, units), f32),
            shape((LANES, units), f32),
        ),
        in_specs=[smem] + [VMEM] * 7 + [ANY] * 7,
        out_specs=(VMEM,) * 8,
        scratch_shapes=[
            pltpu.VMEM((2,) + gate_weight.shape, bf16),
            pltpu.VMEM((2,) + up_weight.shape, bf16),
            pltpu.VMEM((2,) + down_weight.shape, bf16),
            pltpu.VMEM((rows, units), bf16),
            pltpu.VMEM((rows, units), bf16),
            pltpu.VMEM((rows, units), bf16),
            pltpu.VMEM((rows, LANES), bf16),
            pltpu.VMEM((LANES, units), bf16),
            pltpu.VMEM((LANES, units), bf16),
            pltpu.VMEM((block, model), bf16),
            DMA((3, 2)),
            DMA,
        ]
        + cube_scratch(rows, model)
        + tail_scratch(rows, tp_size),
        compiler_params=params(2),
        name="feed",
    )(
        seq_lengths,
        second,
        active,
        residual,
        gain2,
        wide_all,
        slim_all,
        down_grad,
        grad_rows,
        gate_weight,
        wg,
        up_weight,
        wu,
        down_weight,
        wd,
    )
    grad_pre, block_out, out_left, out_right, down_right_grad, feed_left = pl.pallas_call(
        functools.partial(back_kernel, mixer_sizes),
        out_shape=(
            shape((rows, 3 * cols + LANES), bf16),
            shape((rows, model), bf16),
            shape((LANES, cols), f32),
            shape((LANES, model), f32),
            shape((LANES, model), f32),
            shape((LANES, model), f32),
        ),
        in_specs=[smem] + [VMEM] * 16 + [ANY] * 2 + [VMEM] * 8,
        out_specs=(VMEM,) * 6,
        scratch_shapes=[
            pltpu.VMEM((2,) + output_weight.shape, bf16),
            pltpu.VMEM((rows, cols), f32),
            pltpu.VMEM(tall, f32),
            pltpu.VMEM(square, bf16),
            pltpu.VMEM((seqs, heads, width, width), bf16),
            pltpu.VMEM((HALO + length + HALO, 3 * cols), f32),
            pltpu.VMEM((2, seqs, HALO, 3 * cols), f32),
            pltpu.VMEM((2, seqs, HALO, 3 * cols), bf16),
            pltpu.VMEM((rows, LANES), bf16),
            DMA((1, 2)),
            DMA((seqs,)),
            DMA((seqs,)),
            DMA,
            DMA,
        ]
        + cube_scratch(rows, model)[1:]
        + tail_scratch(rows, tp_size)[1:],
        compiler_params=params(3),
        name="back",
    )(
        seq_lengths,
        resid_low,
        gain3,
        start,
        step_map,
        reach,
        local_out,
        inverse,
        wkey,
        wval,
        pre_ext,
        query_conv,
        key_conv,
        value_conv,
        rates,
        wide_all,
        slim_all,
        output_weight,
        wo,
        heads_low,
        out_inner,
        down_part,
        down_tail,
        residual,
        grad_rows,
        second,
        feed_grad,
    )
    input_grad, mixer_left, mixer_right = pl.pallas_call(
        functools.partial(first_kernel, (tp_size,)),
        out_shape=(
            shape((rows, model), bf16),
            shape((LANES, model), f32),
            shape((LANES, 3 * cols + LANES), f32),
        ),
        in_specs=[VMEM] * 9,
        out_specs=(VMEM,) * 3,
        scratch_shapes=[pltpu.VMEM((rows, LANES), bf16)]
        + cube_scratch(rows, model)
        + tail_scratch(rows, tp_size),
        compiler_params=params(4),
        name="first",
    )(grad_pre, wqkv, back, into, x, gain1, grad_residual, n1, inner)
    sources = [
        mixer_left,
        mixer_right,
        feed_left,
        gate_right_grad,
        up_right_grad,
        out_left,
        out_right,
        down_left_grad,
        down_right_grad,
    ]
    strips = []
    for kind in range(4):
        strips.append((0, kind * 8, 32, 0, model))
        strips.append((1, kind * 8, 32, kind * cols, cols if kind < 3 else LANES))
    strips += [
        (5, 0, 8, 0, cols),
        (6, 0, 8, 0, model),
        (2, 0, 16, 0, model),
        (3, 0, 16, 0, units),
        (2, 8, 16, 0, model),
        (4, 8, 16, 0, units),
        (7, 0, 8, 0, units),
        (8, 0, 8, 0, model),
    ]
    strips = tuple(strips)
    used = sum(item[4] for item in strips)
    grain = LANES * ctx_size
    total_wide = -(-used // grain) * grain
    packed = pl.pallas_call(
        functools.partial(share_kernel, (ctx_size, total_wide), strips),
        out_shape=(shape((8, total_wide), f32),),
        in_specs=[VMEM] * len(sources),
        out_specs=(VMEM,),
        scratch_shapes=[
            pltpu.VMEM((2, 8, total_wide), bf16),
            pltpu.VMEM((8, total_wide), bf16),
            pltpu.VMEM((ctx_size, 8, total_wide // ctx_size), bf16),
            pltpu.VMEM((ctx_size - 1, 8, total_wide // ctx_size), bf16),
            pltpu.VMEM((ctx_size, 8, total_wide // ctx_size), bf16),
            DMA,
            DMA,
            DMA((2, ctx_size - 1)),
            DMA((2, ctx_size - 1)),
        ],
        compiler_params=params(5),
        name="share",
    )(*sources)[0]
    shares = list(
        pl.pallas_call(
            functools.partial(deal_kernel, strips),
            out_shape=tuple(shape((8, item[4]), f32) for item in strips),
            in_specs=[VMEM],
            out_specs=(VMEM,) * len(strips),
            name="deal",
        )(packed)
    )
    shares[7] = shares[7][:, RATE_AT : RATE_AT + heads]
    lefts = (0, 2, 4, 6, 8, 10, 12, 14)
    shares = [item.T if i in lefts else item for i, item in enumerate(shares)]
    return (
        block_out.reshape(seqs, length, model),
        input_grad.reshape(seqs, length, model),
    ) + tuple(shares)


def solution(mesh):
    placed = (
        P("fsdp", "ctx", None),
        P("fsdp"),
        P(),
        P(),
        P("fsdp", "tp"),
        P("fsdp", "tp"),
        P("fsdp", "tp"),
        P("fsdp", "tp"),
        P(None, "tp"),
        P(None, "tp"),
        P(None, "tp"),
        P(),
        P("tp", "fsdp"),
        P("fsdp", "tp"),
        P("fsdp", "tp"),
        P("tp", "fsdp"),
    )
    left_in, left_over, right_over, right_in = (
        P(None, "fsdp"),
        P("tp", "fsdp"),
        P("fsdp", None),
        P("fsdp", "tp"),
    )
    adapters = (left_in, right_in) * 4 + (left_over, right_over) + (left_in, right_in) * 2 + (
        left_over,
        right_over,
    )
    rows = P("fsdp", "ctx", None)
    return jax.shard_map(
        functools.partial(local, mesh.shape["ctx"], mesh.shape["tp"]),
        mesh=mesh,
        in_specs=placed + adapters + (rows,),
        out_specs=(rows, rows) + adapters,
        check_vma=False,
    )
```

```python
import functools

import jax
import jax.numpy as jnp
from jax import lax
from jax.experimental import pallas as pl
from jax.experimental.pallas import tpu as pltpu
from jax.sharding import PartitionSpec as P

MESH = pl.DeviceIdType.MESH
ANY = pl.BlockSpec(memory_space=pl.ANY)
VMEM = pl.BlockSpec(memory_space=pltpu.VMEM)
DMA = pltpu.SemaphoreType.DMA
f32, bf16 = jnp.float32, jnp.bfloat16

CONV = 4
SCALE = 0.5
EPS = 1e-06
LANES = 128
RATE_AT = 64
HALO = 8


def shape(dims, kind):
    return jax.ShapeDtypeStruct(tuple(dims), kind)


def product(left, right, dims):
    return lax.dot_general(
        left.astype(bf16), right.astype(bf16), (dims, ((), ())), preferred_element_type=f32
    )


def mm(left, right):
    return product(left, right, ((1,), (0,)))


def mt(left, right):
    return product(left, right, ((1,), (1,)))


def tm(left, right):
    return product(left, right, ((0,), (0,)))


def params(collective, limit=58 << 20):
    return pltpu.CompilerParams(
        collective_id=collective, has_side_effects=True, vmem_limit_bytes=limit
    )


def grid_of(size):
    rows = lax.broadcasted_iota(jnp.int32, (size, size), 0)
    cols = lax.broadcasted_iota(jnp.int32, (size, size), 1)
    return rows, cols


def halves(values):
    high = values.astype(bf16)
    return high, (values - high.astype(f32)).astype(bf16)


def finer(left, right, dims):
    lhigh, llow = halves(left)
    rhigh, rlow = halves(right)
    (la,), (ra,) = dims
    return lax.dot_general(
        jnp.concatenate([lhigh, llow, lhigh], axis=la),
        jnp.concatenate([rhigh, rhigh, rlow], axis=ra),
        (dims, ((), ())),
        preferred_element_type=f32,
    )


def unit_inverses(stricts):
    size = stricts[0].shape[0]
    rows, cols = grid_of(size)
    eye = jnp.where(rows == cols, 1.0, 0.0)
    found = [eye - jnp.where((rows >> 1) == (cols >> 1), item, 0.0) for item in stricts]
    level = 1
    while (1 << level) < size:
        joined = ((rows >> (level + 1)) == (cols >> (level + 1))) & ((rows >> level) != (cols >> level))
        lows = [item.astype(bf16) for item in found]
        inner = [mm(jnp.where(joined, item, 0.0), low) for item, low in zip(stricts, lows)]
        found = [item - mm(low, part) for item, low, part in zip(found, lows, inner)]
        level += 1
    lows = [item.astype(bf16) for item in found]
    errors = []
    for item, low in zip(stricts, lows):
        pair = jnp.concatenate(halves(item), axis=1)
        errors.append(eye - low.astype(f32) - mm(pair, jnp.concatenate([low, low], axis=0)))
    return [low.astype(f32) + mm(low, error) for low, error in zip(lows, errors)]


def normed(values, gain):
    return values * lax.rsqrt(jnp.mean(values * values, axis=-1, keepdims=True) + EPS) * gain


def norm_back(values, gain, grad):
    scale = lax.rsqrt(jnp.mean(values * values, axis=-1, keepdims=True) + EPS)
    weighted = gain * grad
    return scale * weighted - values * (scale * scale * scale) * jnp.mean(
        values * weighted, axis=-1, keepdims=True
    )


def greet(barrier, peers):
    count = 0
    for peer, condition in peers:

        def tell(peer=peer):
            pl.semaphore_signal(barrier, inc=1, device_id=peer, device_id_type=MESH)

        if condition is None:
            tell()
            count = count + 1
        else:
            pl.when(condition)(tell)
            count = count + jnp.where(condition, 1, 0)
    pl.semaphore_wait(barrier, count)


def remote(source, target, send_sem, recv_sem, peer):
    return pltpu.make_async_remote_copy(
        src_ref=source,
        dst_ref=target,
        send_sem=send_sem,
        recv_sem=recv_sem,
        device_id=peer,
        device_id_type=MESH,
    )


def column(block, lane):
    return block[:, lane : lane + 1]


def convolved(ext_ref, taps, s, length, at, width):
    total = None
    for i in range(CONV):
        rows = ext_ref[s, pl.ds(HALO - (CONV - 1) + i, length), pl.ds(at, width)]
        term = taps[i : i + 1, at : at + width] * rows
        total = term if total is None else total + term
    return total


def kept(lens_ref, s, c, length):
    place = c * length + lax.broadcasted_iota(jnp.int32, (length, 1), 0)
    return jnp.where(place < lens_ref[s], 1.0, 0.0)


def part_of(at, size):
    return pl.ds(pl.multiple_of(at * size, size), size)


class Cube:
    def __init__(self, t, src, out, first, second, held, send_sem, recv_sem, chunks):
        self.y, self.x = t // 2, lax.rem(t, 2)
        self.t, self.src, self.out = t, src, out
        self.first, self.second, self.held = first, second, held
        self.send_sem, self.recv_sem = send_sem, recv_sem
        self.chunks = chunks
        self.block = src.shape[0] // 4
        self.half_width = src.shape[1] // 2
        self.width = self.half_width // chunks
        self.beside = self.y * 2 + (1 - self.x)
        self.above = (1 - self.y) * 2 + self.x

    def peer(self, side):
        return {"tp": self.beside * (1 - side) + self.above * side}

    def columns(self, half, chunk):
        return pl.ds(
            pl.multiple_of(half * self.half_width + chunk * self.width, self.width), self.width
        )

    def copy(self, stage, half, chunk, j):
        wide = self.columns(half, chunk)
        slim = part_of(chunk, self.width)
        send, recv = self.send_sem.at[stage, half, chunk, j], self.recv_sem.at[stage, half, chunk, j]
        across = self.above * (1 - half) + self.beside * half
        if stage == 0:
            g = (1 - half) * (2 * j + 1 - self.x) + half * (2 * (1 - self.y) + j)
            source, target = self.src.at[part_of(g, self.block), wide], self.first.at[half, j, :, slim]
            side = half
        elif stage == 1:
            source, target = self.held.at[half, :, slim], self.second.at[half, :, slim]
            side = 1 - half
        else:
            g = self.t if j == 0 else across
            source = target = self.out.at[part_of(g, self.block), wide]
            side = 1 - half if stage == 2 else half
        return remote(source, target, send, recv, self.peer(side))

    def each(self, body):
        @pl.loop(0, 2 * self.chunks)
        def _(k):
            body(lax.rem(k, 2), k // 2)

    def start(self, half, chunk):
        self.copy(0, half, chunk, 0).start()
        self.copy(0, half, chunk, 1).start()

    def middle(self):
        def body(half, chunk):
            wide = self.columns(half, chunk)
            slim = part_of(chunk, self.width)
            for j in range(2):
                self.copy(0, half, chunk, j).wait_recv()
            across = self.above * (1 - half) + self.beside * half
            other = (1 - half) * (1 - self.y) + half * (1 - self.x)
            self.held[half, :, slim] = (
                self.src[part_of(across, self.block), wide].astype(f32)
                + self.first[half, other, :, slim].astype(f32)
            ).astype(bf16)
            self.copy(1, half, chunk, 0).start()

        self.each(body)

    def finish(self, total_ref):
        def body(half, chunk):
            wide = self.columns(half, chunk)
            slim = part_of(chunk, self.width)
            self.copy(1, half, chunk, 0).wait_recv()
            mine = (1 - half) * self.y + half * self.x
            total_ref[:, wide] = (
                self.src[part_of(self.t, self.block), wide].astype(f32)
                + self.first[half, mine, :, slim].astype(f32)
                + self.second[half, :, slim].astype(f32)
            )

        self.each(body)

    def spread(self):
        def body(half, chunk):
            self.copy(2, half, chunk, 0).start()
            self.copy(3, half, chunk, 0).start()

        self.each(body)

    def relay(self):
        def body(half, chunk):
            self.copy(2, half, chunk, 0).wait_recv()
            self.copy(3, half, chunk, 1).start()

        self.each(body)

    def done(self):
        def body(half, chunk):
            for j in range(2):
                self.copy(3, half, chunk, j).wait_recv()
            for stage in range(4):
                for j in range(2 if stage in (0, 3) else 1):
                    self.copy(stage, half, chunk, j).wait_send()

        self.each(body)


class Tail:
    def __init__(self, t, src, out, got, send_sem, recv_sem, size):
        self.t, self.src, self.out, self.got, self.size = t, src, out, got, size
        self.send_sem, self.recv_sem = send_sem, recv_sem
        self.block = src.shape[0] // size

    def copies(self, stage):
        found = []
        for i in range(self.size - 1):
            g = lax.rem(self.t + 1 + i, self.size)
            if stage == 0:
                source, target = self.src.at[part_of(g, self.block)], self.got.at[self.size - 2 - i]
            else:
                source = target = self.out.at[part_of(self.t, self.block)]
            found.append(
                remote(
                    source,
                    target,
                    self.send_sem.at[stage, i],
                    self.recv_sem.at[stage, self.size - 2 - i],
                    {"tp": g},
                )
            )
        return found

    def start(self, stage):
        for copy in self.copies(stage):
            copy.start()

    def wait(self, stage):
        for copy in self.copies(stage):
            copy.wait_recv()

    def total(self):
        self.wait(0)
        total = self.src[part_of(self.t, self.block), :].astype(f32)
        for i in range(self.size - 1):
            total = total + self.got[i].astype(f32)
        return total

    def done(self):
        for stage in range(2):
            for copy in self.copies(stage):
                copy.wait_send()


CHUNKS = 4


def cube_scratch(rows, model):
    block = rows // 4
    return [
        pltpu.VMEM((rows, model), bf16),
        pltpu.VMEM((2, 2, block, model // 2), bf16),
        pltpu.VMEM((2, block, model // 2), bf16),
        pltpu.VMEM((2, block, model // 2), bf16),
        pltpu.VMEM((block, model), f32),
        DMA((4, 2, CHUNKS, 2)),
        DMA((4, 2, CHUNKS, 2)),
    ]


def tail_scratch(rows, size):
    return [
        pltpu.VMEM((rows, LANES), bf16),
        pltpu.VMEM((size - 1, rows // size, LANES), bf16),
        DMA((2, size - 1)),
        DMA((2, size - 1)),
    ]


def tp_peers(t, size):
    return [({"tp": lax.rem(t + 1 + i, size)}, None) for i in range(size - 1)]


def stacked(pieces):
    rows = sum(piece.shape[0] for piece in pieces)
    fill = jnp.zeros((LANES - rows, pieces[0].shape[1]), f32)
    return jnp.concatenate([piece.astype(f32) for piece in pieces] + [fill], axis=0).astype(bf16)


def slot_loads(pairs, f, sems):
    loads = []
    for i, (own, other, scratch) in enumerate(pairs):
        loads.append(pltpu.make_async_copy(own, scratch.at[f], sems.at[i, 0]))
        loads.append(pltpu.make_async_copy(other, scratch.at[1 - f], sems.at[i, 1]))
    for load in loads:
        load.start()
    return loads


def unit_steps(units, body):
    step = 2 * LANES
    whole = units // step

    @pl.loop(0, whole)
    def _(k):
        body(part_of(k, step))

    if units % step:
        body(pl.ds(whole * step, units % step))


def mixer_kernel(
    sizes,
    lens_ref,
    x_ref,
    gain_ref,
    gain2_ref,
    head_gain_ref,
    qtaps_ref,
    ktaps_ref,
    vtaps_ref,
    wq_ref,
    wk_ref,
    wv_ref,
    wr_ref,
    wide0,
    wide1,
    wide2,
    wide3,
    wide4,
    wide5,
    wide6,
    wide7,
    slim0,
    slim1,
    slim2,
    slim3,
    slim4,
    slim5,
    slim6,
    slim7,
    wo_own,
    wg_own,
    wu_own,
    wd_own,
    grad_hbm,
    n2_ref,
    out_inner_ref,
    resid_ref,
    wo_other,
    wg_other,
    wu_other,
    wd_other,
    wqkv_out,
    n1_out,
    wide_hbm,
    slim_hbm,
    into_out,
    back_out,
    ext_out,
    inner_out,
    rates_out,
    inv_out,
    wkey_out,
    wval_out,
    reach_out,
    local_out,
    map_out,
    heads_out,
    start_out,
    active_out,
    down_inner_out,
    n1_ref,
    wide_out,
    slim_out,
    into_ref,
    back_ref,
    ext_ref,
    inner_ref,
    rates_ref,
    inv_ref,
    wkey_ref,
    wval_ref,
    reach_ref,
    local_ref,
    map_ref,
    heads_ref,
    start_ref,
    active_ref,
    down_inner_ref,
    end_ref,
    w_ref,
    wr_all,
    halo_out,
    halo_in,
    back_f32,
    into_f32,
    chain_out,
    wo_ref,
    wd_ref,
    grad_ref,
    send_sem,
    recv_sem,
    local_sem,
    store_sem,
    halo_send,
    halo_recv,
    load_sem,
    grad_sem,
    chain_send,
    chain_recv,
    *scratch,
):
    seqs, length, heads, width, ctx_size, tp_size = sizes
    cols = heads * width
    half = wq_ref.shape[0]
    model = 2 * half
    half_model = half
    units = active_ref.shape[1]
    left_at = 3 * cols + LANES
    down_at = left_at + cols + 2 * units
    f = lax.axis_index("fsdp")
    c = lax.axis_index("ctx")
    t = lax.axis_index("tp")
    mate = {"fsdp": 1 - f}
    greet(
        pltpu.get_barrier_semaphore(),
        [(mate, None), ({"ctx": c - 1}, c > 0), ({"ctx": c + 1}, c < ctx_size - 1)]
        + tp_peers(t, tp_size),
    )
    src, first, second, held, total_ref, cube_send, cube_recv = scratch[:7]
    tail_src, tail_got, tail_send, tail_recv = scratch[7:]
    cube = Cube(t, src, n2_ref, first, second, held, cube_send, cube_recv, CHUNKS)
    tail = Tail(t, tail_src, out_inner_ref, tail_got, tail_send, tail_recv, tp_size)
    stores = []

    def store(pairs):
        for source, target in pairs:
            copy = pltpu.make_async_copy(source, target, store_sem.at[len(stores)])
            copy.start()
            stores.append(copy)

    top = pl.ds(pl.multiple_of(f * half, half), half)
    moves = []
    for i, ref in enumerate((wide0, wide1, wide2, wide3, wide4, wide5, wide6, wide7)):
        moves.append((ref, wide_out.at[f, i]))
    at = 0
    for ref in (slim0, slim1, slim2, slim3, slim4, slim5, slim6, slim7):
        moves.append((ref, slim_out.at[f, :, at : at + ref.shape[1]]))
        at += ref.shape[1]
    moves += [
        (wr_ref, wr_all.at[:, top]),
        (wq_ref, w_ref.at[0, top]),
        (wk_ref, w_ref.at[1, top]),
        (wv_ref, w_ref.at[2, top]),
    ]
    near = [pltpu.make_async_copy(src, dst, local_sem.at[i]) for i, (src, dst) in enumerate(moves)]
    local_count = len(moves)
    moves += [(wo_own, wo_other), (wg_own, wg_other), (wu_own, wu_other), (wd_own, wd_other)]
    across = [
        remote(src, dst, send_sem.at[i], recv_sem.at[i], mate) for i, (src, dst) in enumerate(moves)
    ]
    for copy in across[:local_count] + near:
        copy.start()
    own_loads = [
        pltpu.make_async_copy(wo_own, wo_ref.at[f], load_sem.at[0]),
        pltpu.make_async_copy(wd_own, wd_ref.at[f], load_sem.at[2]),
        pltpu.make_async_copy(grad_hbm, grad_ref, grad_sem),
    ]

    @pl.loop(0, seqs)
    def _(s):
        here = pl.ds(pl.multiple_of(s * length, length), length)
        n1_ref[here, :] = normed(x_ref[here, :].astype(f32), gain_ref[...]).astype(bf16)

    for i in range(local_count):
        near[i].wait()
        across[i].wait_recv()
    for copy in across[local_count:] + own_loads:
        copy.start()
    kinds = 4
    into_f32[...] = jnp.zeros_like(into_f32)
    back_f32[...] = jnp.zeros_like(back_f32)
    for core in range(2):
        for kind in range(kinds):
            spot = core * 32 + kind * 8
            into_f32[spot : spot + 8, :] = wide_out[core, kind].astype(f32)
        for kind in range(kinds):
            at = kind * cols
            wide = cols if kind < 3 else LANES
            back_f32[core * 32 + kind * 8 : core * 32 + kind * 8 + 8, at : at + wide] = slim_out[
                core, :, at : at + wide
            ].astype(f32)
    into_f32[RATE_AT : RATE_AT + 8, :] = wr_all[...].astype(f32)
    into_ref[...] = into_f32[...].astype(bf16)
    back_ref[...] = back_f32[...].astype(bf16)
    store([(w_ref, wqkv_out), (n1_ref, n1_out), (wide_out, wide_hbm), (slim_out, slim_hbm)])
    store([(into_ref, into_out), (back_ref, back_out)])

    @pl.loop(0, seqs)
    def _(s):
        here = pl.ds(pl.multiple_of(s * length, length), length)
        block = n1_ref[here, :]
        tail = mt(block, into_ref[...])
        inner = tail.astype(bf16)
        inner_ref[here, :] = inner
        for i in range(3):
            pre = mm(block, w_ref[i]) + SCALE * mm(inner, back_ref[:, i * cols : (i + 1) * cols])
            ext_ref[s, HALO : HALO + length, i * cols : (i + 1) * cols] = pre
            halo_out[s, :, i * cols : (i + 1) * cols] = pre[length - HALO :, :].astype(bf16)
        pre_rate = tail + SCALE * mm(inner, back_ref[:, 3 * cols :])
        rates_ref[here, :] = jax.nn.sigmoid(pre_rate) * kept(lens_ref, s, c, length)

    halo = remote(halo_out, halo_in, halo_send, halo_recv, {"ctx": c + 1})

    @pl.when(c < ctx_size - 1)
    def _():
        halo.start()

    @pl.when(c > 0)
    def _():
        halo.wait_recv()
        ext_ref[:, 0:HALO, :] = halo_in[...].astype(f32)

    @pl.when(c == 0)
    def _():
        ext_ref[:, 0:HALO, :] = jnp.zeros((seqs, HALO, 3 * cols), f32)

    taps = jnp.concatenate([qtaps_ref[...], ktaps_ref[...], vtaps_ref[...]], axis=1)
    row_at, col_at = grid_of(length)

    def solve(s):
        here = pl.ds(pl.multiple_of(s * length, length), length)
        rate_block = rates_ref[here, :]
        queries, keys, values, rates, stricts = [], [], [], [], []
        for h in range(heads):
            at = h * width
            parts = [
                jax.nn.silu(convolved(ext_ref, taps, s, length, i * cols + at, width))
                for i in range(3)
            ]
            query, key = [
                a * lax.rsqrt(jnp.sum(a * a, axis=-1, keepdims=True) + EPS) for a in parts[:2]
            ]
            rate = column(rate_block, RATE_AT + h)
            queries.append(query)
            keys.append(key)
            values.append(parts[2])
            rates.append(rate)
            stricts.append(
                jnp.where(row_at > col_at, rate * finer(key, key, ((1,), (1,))), 0.0)
            )
        inverses = unit_inverses(stricts)
        for h in range(heads):
            pair = s * heads + h
            query, key, value, rate, inverse = queries[h], keys[h], values[h], rates[h], inverses[h]
            wkey = mm(inverse, rate * key)
            wval = mm(inverse, rate * value)
            scores = jnp.where(row_at >= col_at, finer(query, key, ((1,), (1,))), 0.0)
            inv_ref[pair] = inverse.astype(bf16)
            wkey_ref[pair] = wkey.astype(bf16)
            wval_ref[pair] = wval
            reach_ref[pair] = (query - mm(scores, wkey)).astype(bf16)
            local_ref[pair] = finer(scores, wval, ((1,), (0,)))
            map_ref[pair] = (jnp.where(row_at == col_at, 1.0, 0.0) - tm(key, wkey)).astype(bf16)
            end_ref[pair] = tm(key, wval)

    gain = head_gain_ref[...]

    def link(s):
        pairs = pl.ds(s * heads, heads)
        hop = remote(
            chain_out.at[s], start_ref.at[pairs], chain_send.at[s], chain_recv.at[s], {"ctx": c + 1}
        )

        @pl.when(c > 0)
        def _():
            hop.wait_recv()

        @pl.when(c == 0)
        def _():
            start_ref[pairs] = jnp.zeros((heads, width, width), bf16)

        @pl.when(c < ctx_size - 1)
        def _():
            for h in range(heads):
                pair = s * heads + h
                chain_out[s, h] = (mm(map_ref[pair], start_ref[pair]) + end_ref[pair]).astype(bf16)
            hop.start()

        here = part_of(s, length)
        for h in range(heads):
            pair = s * heads + h
            mixed = mm(reach_ref[pair], start_ref[pair]) + local_ref[pair]
            heads_ref[here, h * width : (h + 1) * width] = normed(mixed, gain).astype(bf16)

    @pl.loop(0, seqs + ctx_size - 1)
    def _(k):
        @pl.when(k < seqs)
        def _():
            solve(k)

        @pl.when((k >= c) & (k < c + seqs))
        def _():
            link(k - c)

    store(
        [
            (ext_ref, ext_out),
            (inner_ref, inner_out),
            (rates_ref, rates_out),
            (inv_ref, inv_out),
            (wkey_ref, wkey_out),
            (wval_ref, wval_out),
            (reach_ref, reach_out),
            (local_ref, local_out),
            (map_ref, map_out),
            (heads_ref, heads_out),
            (start_ref, start_out),
        ]
    )
    into = stacked([slim_out[core, :, left_at : left_at + cols] for core in range(2)])
    low = heads_ref[...]
    tail_src[...] = mt(low, into).astype(bf16)
    tail.start(0)
    across[local_count].wait_recv()
    wo_load = pltpu.make_async_copy(wo_other, wo_ref.at[1 - f], load_sem.at[1])
    wo_load.start()
    own_loads[0].wait()
    wo_load.wait()

    def project(half, chunk):
        src[:, cube.columns(half, chunk)] = mm(
            heads_ref[...], wo_ref[half, :, part_of(chunk, cube.width)]
        ).astype(bf16)
        cube.start(half, chunk)

    cube.each(project)
    for copy in across[local_count + 1 :]:
        copy.wait_recv()
    wd_load = pltpu.make_async_copy(wd_other, wd_ref.at[1 - f], load_sem.at[3])
    wd_load.start()
    own_loads[2].wait()
    down_from = stacked([wide_out[core, 7] for core in range(2)])
    for s in range(seqs):
        here = pl.ds(s * length, length)
        down_inner_ref[here, :] = (
            kept(lens_ref, s, c, length) * (SCALE * mt(grad_ref[here, :], down_from))
        ).astype(bf16)
    own_loads[1].wait()
    wd_load.wait()

    def activate(at):
        into_down = stacked([slim_out[core, :, pl.ds(down_at + at.start, at.size)] for core in range(2)])
        part = mt(grad_ref[:, :half_model], wd_ref[0, at, :])
        part = part + mt(grad_ref[:, half_model:], wd_ref[1, at, :])
        part = part + mm(down_inner_ref[...], into_down)
        for s in range(seqs):
            active_ref[s * length : (s + 1) * length, at] = (
                kept(lens_ref, s, c, length) * part[s * length : (s + 1) * length]
            )

    unit_steps(units, activate)
    store([(active_ref, active_out), (down_inner_ref, down_inner_out)])
    cube.middle()
    cube.finish(total_ref)
    inner = tail.total().astype(bf16)
    here = part_of(t, length)
    right = stacked([wide_out[core, 6] for core in range(2)])
    resid = x_ref[here, :].astype(f32) + total_ref[...] + SCALE * mm(inner, right)
    resid_ref[...] = resid
    out_inner_ref[here, :] = inner
    n2_ref[here, :] = normed(resid, gain2_ref[...]).astype(bf16)
    cube.spread()
    tail.start(1)
    cube.relay()
    tail.wait(1)
    cube.done()
    tail.done()
    for copy in across:
        copy.wait_send()
    for copy in stores:
        copy.wait()

    @pl.when(c < ctx_size - 1)
    def _():
        halo.wait_send()

        @pl.loop(0, seqs)
        def _(s):
            remote(
                chain_out.at[s],
                start_ref.at[pl.ds(0, heads)],
                chain_send.at[s],
                chain_recv.at[s],
                {"ctx": c + 1},
            ).wait_send()


def feed_kernel(
    sizes,
    lens_ref,
    n2_ref,
    active_ref,
    resid_ref,
    gain_ref,
    wide_ref,
    slim_ref,
    down_grad_ref,
    grad_ref,
    wg_own,
    wg_other,
    wu_own,
    wu_other,
    wd_own,
    wd_other,
    low_ref,
    inner_grad_ref,
    gresid_ref,
    down_ref,
    down_tail_ref,
    gate_right_ref,
    up_right_ref,
    down_left_ref,
    wg_ref,
    wu_ref,
    wd_ref,
    act_ref,
    dgate_ref,
    dup_ref,
    inner_ref,
    back_gate,
    back_up,
    own_grad,
    load_sem,
    grad_sem,
    *scratch,
):
    seqs, length, cols, ctx_size, tp_size = sizes
    model = n2_ref.shape[1]
    half_model = model // 2
    units = active_ref.shape[1]
    gate_at = 4 * cols + LANES
    up_at = gate_at + units
    down_at = up_at + units
    f = lax.axis_index("fsdp")
    c = lax.axis_index("ctx")
    t = lax.axis_index("tp")
    loads = slot_loads(
        [(wg_own, wg_other, wg_ref), (wu_own, wu_other, wu_ref), (wd_own, wd_other, wd_ref)],
        f,
        load_sem,
    )
    here = part_of(t, length)
    own_load = pltpu.make_async_copy(grad_ref.at[here], own_grad, grad_sem)
    own_load.start()
    greet(pltpu.get_barrier_semaphore(), tp_peers(t, tp_size))
    src, first, second, held, total_ref, send_sem, recv_sem = scratch[:7]
    tail_src, tail_got, tail_send, tail_recv = scratch[7:]
    cube = Cube(t, src, low_ref, first, second, held, send_sem, recv_sem, CHUNKS)
    tail = Tail(t, tail_src, inner_grad_ref, tail_got, tail_send, tail_recv, tp_size)
    into = stacked([wide_ref[core, 4 + kind] for core in range(2) for kind in range(2)])
    blank = jnp.zeros((8, units), bf16)
    gates = [slim_ref[core, :, gate_at : gate_at + units] for core in range(2)]
    ups = [slim_ref[core, :, up_at : up_at + units] for core in range(2)]
    back_gate[...] = stacked([gates[0], blank, gates[1], blank])
    back_up[...] = stacked([blank, ups[0], blank, ups[1]])
    inner_ref[...] = mt(n2_ref[...], into).astype(bf16)
    for load in loads[:4]:
        load.wait()

    def forward(at):
        pre = []
        for weight, back in ((wg_ref, back_gate), (wu_ref, back_up)):
            part = mm(n2_ref[:, :half_model], weight[0, :, at])
            part = part + mm(n2_ref[:, half_model:], weight[1, :, at])
            pre.append(part + SCALE * mm(inner_ref[...], back[:, at]))
        gate, up = pre
        sigma = jax.nn.sigmoid(gate)
        silu = gate * sigma
        active = active_ref[:, at]
        act_ref[:, at] = (silu * up).astype(bf16)
        dgate_ref[:, at] = (active * up * (sigma * (1.0 + gate * (1.0 - sigma)))).astype(bf16)
        dup_ref[:, at] = (active * silu).astype(bf16)

    unit_steps(units, forward)
    tail_src[...] = (
        SCALE * (mt(dgate_ref[...], back_gate[...]) + mt(dup_ref[...], back_up[...]))
    ).astype(bf16)
    tail.start(0)

    def project(half, chunk):
        rows = part_of(chunk, cube.width)
        src[:, cube.columns(half, chunk)] = (
            mt(dgate_ref[...], wg_ref[half, rows, :]) + mt(dup_ref[...], wu_ref[half, rows, :])
        ).astype(bf16)
        cube.start(half, chunk)

    cube.each(project)
    cube.middle()
    for load in loads[4:]:
        load.wait()

    def descend(half, chunk):
        down_ref[:, cube.columns(half, chunk)] = mm(
            act_ref[...], wd_ref[half, :, part_of(chunk, cube.width)]
        ).astype(bf16)

    cube.each(descend)
    cube.finish(total_ref)
    own_load.wait()
    inner = tail.total().astype(bf16)
    grad_second = total_ref[...] + mm(inner, into)
    grad = own_grad[...].astype(f32) * kept(lens_ref, t, c, length) + norm_back(
        resid_ref[...], gain_ref[...], grad_second
    )
    gresid_ref[...] = grad
    low_ref[here, :] = grad.astype(bf16)
    inner_grad_ref[here, :] = inner
    cube.spread()
    tail.start(1)
    into_down = stacked([slim_ref[core, :, down_at : down_at + units] for core in range(2)])
    down_tail_ref[...] = mt(act_ref[...], into_down).astype(bf16)
    gate_right_ref[...] = SCALE * tm(inner_ref[...], dgate_ref[...])[:32]
    cube.relay()
    up_right_ref[...] = SCALE * tm(inner_ref[...], dup_ref[...])[:32]
    down_left_ref[...] = tm(down_grad_ref[...], act_ref[...])[:32]
    tail.wait(1)
    cube.done()
    tail.done()


def strip_plan(cols, model, units):
    widths = (
        ("ql", model), ("qr", cols), ("kl", model), ("kr", cols), ("vl", model), ("vr", cols),
        ("rl", model), ("rr", LANES), ("ol", cols), ("or", model), ("gl", model), ("gr", units),
        ("ul", model), ("ur", units), ("dl", units), ("dr", model),
    )
    plan, at = {}, 0
    for name, wide in widths:
        plan[name] = (at, wide)
        at += wide
    return plan, at


BACK_LOADS = 24


def back_kernel(
    sizes,
    lens_ref,
    low_ref,
    head_gain_ref,
    gain_ref,
    qtaps_ref,
    ktaps_ref,
    vtaps_ref,
    wide_ref,
    slim_ref,
    tail_src,
    feed_grad_ref,
    out_inner_ref,
    inner_ref,
    gate_right_ref,
    up_right_ref,
    down_left_ref,
    start_hbm,
    map_hbm,
    reach_hbm,
    local_hbm,
    inv_hbm,
    wkey_hbm,
    wval_hbm,
    ext_hbm,
    rates_hbm,
    heads_hbm,
    down_hbm,
    resid_hbm,
    grad_hbm,
    n2_hbm,
    n1_hbm,
    x_hbm,
    gresid_hbm,
    w_hbm,
    back_hbm,
    into_hbm,
    wo_own,
    wo_other,
    block_hbm,
    input_grad_hbm,
    packed_ref,
    start_ref,
    map_ref,
    reach_ref,
    local_ref,
    inv_ref,
    wkey_ref,
    wval_ref,
    ext_ref,
    rates_ref,
    heads_ref,
    src,
    resid_ref,
    grad_ref,
    normed_ref,
    x_ref,
    gresid_ref,
    w_ref,
    back_ref,
    into_ref,
    wo_ref,
    out_ref,
    pre_ref,
    dmix_ref,
    after_ref,
    chain_out,
    gconv_ref,
    halo_out,
    halo_in,
    down_inner_ref,
    keys_ref,
    slopes_ref,
    values_ref,
    vslopes_ref,
    dfresh_ref,
    dkeys_ref,
    fresh_ref,
    tail2_src,
    inner_grad_ref,
    pack,
    mate_in,
    mine_ref,
    got,
    summed,
    load_sem,
    store_sem,
    chain_send,
    chain_recv,
    halo_send,
    halo_recv,
    swap_send,
    swap_recv,
    part_send,
    part_recv,
    first,
    second,
    held,
    total_ref,
    cube_send,
    cube_recv,
    cube2_send,
    cube2_recv,
    tail_got,
    tail_send,
    tail_recv,
    tail2_got,
    tail2_send,
    tail2_recv,
):
    seqs, length, heads, width, ctx_size, tp_size = sizes
    cols = heads * width
    model = low_ref.shape[1]
    half_model = model // 2
    units = gate_right_ref.shape[1]
    left_at = 3 * cols + LANES
    plan, used = strip_plan(cols, model, units)
    f = lax.axis_index("fsdp")
    c = lax.axis_index("ctx")
    t = lax.axis_index("tp")
    mate = {"fsdp": 1 - f}
    mine = part_of(t, length)
    loads = {}

    def fetch(name, source, target):
        loads[name] = pltpu.make_async_copy(source, target, load_sem.at[len(loads)])
        loads[name].start()

    fetch("wo_own", wo_own, wo_ref.at[f])
    fetch("wo_other", wo_other, wo_ref.at[1 - f])
    fetch("src", down_hbm, src)
    fetch("reach", reach_hbm, reach_ref)
    fetch("start", start_hbm, start_ref)
    fetch("local", local_hbm, local_ref)
    fetch("map", map_hbm, map_ref)
    fetch("ext", ext_hbm, ext_ref)
    fetch("rates", rates_hbm, rates_ref)
    fetch("wkey", wkey_hbm, wkey_ref)
    fetch("wval", wval_hbm, wval_ref)
    fetch("inv", inv_hbm, inv_ref)
    fetch("heads", heads_hbm, heads_ref)
    fetch("resid", resid_hbm, resid_ref)
    fetch("n2", n2_hbm, normed_ref)
    fetch("grad", grad_hbm, grad_ref)
    greet(
        pltpu.get_barrier_semaphore(),
        [(mate, None)]
        + [({"ctx": lax.rem(c + 1 + i, ctx_size)}, None) for i in range(ctx_size - 1)]
        + tp_peers(t, tp_size),
    )
    cube = Cube(t, src, out_ref, first, second, held, cube_send, cube_recv, CHUNKS)
    tail = Tail(t, tail_src, down_inner_ref, tail_got, tail_send, tail_recv, tp_size)
    cube2 = Cube(t, src, out_ref, first, second, held, cube2_send, cube2_recv, CHUNKS)
    tail2 = Tail(t, tail2_src, inner_grad_ref, tail2_got, tail2_send, tail2_recv, tp_size)

    def put(name, core, rows):
        at, wide = plan[name]
        pack[core, :, at : at + wide] = rows.astype(bf16)

    tail.start(0)
    gain = head_gain_ref[...]
    taps = jnp.concatenate([qtaps_ref[...], ktaps_ref[...], vtaps_ref[...]], axis=1)
    row_at, col_at = grid_of(length)
    gconv_ref[...] = jnp.zeros_like(gconv_ref)
    from_out = stacked([wide_ref[core, 6] for core in range(2)])
    into_out = stacked([slim_ref[core, :, left_at : left_at + cols] for core in range(2)])
    out_grad = (SCALE * mt(low_ref[...], from_out)).astype(bf16)
    loads["wo_own"].wait()
    loads["wo_other"].wait()
    dheads = (
        mt(low_ref[:, :half_model], wo_ref[0])
        + mt(low_ref[:, half_model:], wo_ref[1])
        + mm(out_grad, into_out)
    )
    for s in range(seqs):
        for h in range(heads):
            dmix_ref[s * heads + h] = dheads[
                s * length : (s + 1) * length, h * width : (h + 1) * width
            ]
    loads["src"].wait()
    cube.each(cube.start)
    for name in ("reach", "start", "local", "map"):
        loads[name].wait()

    @pl.loop(0, seqs)
    def _(s):
        for h in range(heads):
            pair = s * heads + h
            mixed = mm(reach_ref[pair], start_ref[pair]) + local_ref[pair]
            dmix_ref[pair] = norm_back(mixed, gain, dmix_ref[pair])

    for name in ("ext", "rates", "wkey", "wval", "inv"):
        loads[name].wait()
    fetch("w", w_hbm, w_ref)
    fetch("back", back_hbm, back_ref)
    fetch("into", into_hbm, into_ref)
    fetch("x", x_hbm.at[mine], x_ref)
    fetch("gresid", gresid_hbm, gresid_ref)

    def hop_of(s):
        pairs = pl.ds(s * heads, heads)
        return remote(
            chain_out.at[s], after_ref.at[pairs], chain_send.at[s], chain_recv.at[s], {"ctx": c - 1}
        )

    def link(s):
        pairs = pl.ds(s * heads, heads)

        @pl.when(c < ctx_size - 1)
        def _():
            hop_of(s).wait_recv()

        @pl.when(c == ctx_size - 1)
        def _():
            after_ref[pairs] = jnp.zeros((heads, width, width), bf16)

        @pl.when(c > 0)
        def _():
            for h in range(heads):
                pair = s * heads + h
                chain_out[s, h] = (
                    tm(map_ref[pair], after_ref[pair]) + tm(reach_ref[pair], dmix_ref[pair])
                ).astype(bf16)
            hop_of(s).start()

    def unconvolve(s, kind):
        here = part_of(s, length)
        for h in range(heads):
            at = kind * cols + h * width
            total = None
            spill = None
            for j in range(CONV):
                tap = taps[j : j + 1, at : at + width]
                term = tap * gconv_ref[pl.ds(HALO + CONV - 1 - j, length), pl.ds(at, width)]
                edge = tap * gconv_ref[pl.ds(CONV - 1 - j, HALO), pl.ds(at, width)]
                total = term if total is None else total + term
                spill = edge if spill is None else spill + edge
            pre_ref[here, at : at + width] = total.astype(bf16)
            halo_out[0, s, :, at : at + width] = total[length - HALO :, :]
            halo_out[1, s, :, at : at + width] = spill

    def early(s):
        for h in range(heads):
            pair = s * heads + h
            at = h * width
            convs = [convolved(ext_ref, taps, s, length, i * cols + at, width) for i in range(3)]
            sigmas = [jax.nn.sigmoid(a) for a in convs]
            slopes = [b * (1.0 + a * (1.0 - b)) for a, b in zip(convs, sigmas)]
            acts = [a * b for a, b in zip(convs, sigmas)]
            scales = [lax.rsqrt(jnp.sum(a * a, axis=-1, keepdims=True) + EPS) for a in acts[:2]]
            query, key = [a * b for a, b in zip(acts, scales)]
            start, dmix = start_ref[pair], dmix_ref[pair]
            fresh = wval_ref[pair] - mm(wkey_ref[pair], start)
            scores = jnp.where(row_at >= col_at, finer(query, key, ((1,), (1,))), 0.0)
            dscores = jnp.where(row_at >= col_at, finer(dmix, fresh, ((1,), (1,))), 0.0)
            dquery = mt(dmix, start) + mm(dscores, key)
            keys_ref[pair] = key
            slopes_ref[pair] = slopes[1] * scales[1]
            values_ref[pair] = acts[2]
            vslopes_ref[pair] = slopes[2]
            dfresh_ref[pair] = tm(scores, dmix)
            dkeys_ref[pair] = tm(dscores, query)
            fresh_ref[pair] = fresh.astype(bf16)
            along = jnp.sum(query * dquery, axis=-1, keepdims=True)
            gconv_ref[pl.ds(HALO, length), pl.ds(at, width)] = (
                slopes[0] * scales[0] * (dquery - query * along)
            )
        unconvolve(s, 0)

    def late(s):
        here = part_of(s, length)
        rate_block = rates_ref[here, :]
        rate_grads = jnp.zeros((length, LANES), f32)
        lane = lax.broadcasted_iota(jnp.int32, (length, LANES), 1)
        for h in range(heads):
            pair = s * heads + h
            at = h * width
            rate = column(rate_block, RATE_AT + h)
            start, after, key, fresh = start_ref[pair], after_ref[pair], keys_ref[pair], fresh_ref[pair]
            dfresh = dfresh_ref[pair] + mm(key, after)
            dvalue = tm(inv_ref[pair], dfresh)
            dkey_in = -mt(dvalue, start)
            dstrict = jnp.where(row_at > col_at, -mt(dvalue, fresh), 0.0)
            dprod = rate * dstrict
            dkey = (
                dkeys_ref[pair] + mt(fresh, after) + rate * dkey_in + mm(dprod, key) + tm(dprod, key)
            )
            drate = jnp.sum(
                dstrict * mt(key, key) + dvalue * values_ref[pair] + dkey_in * key,
                axis=-1,
                keepdims=True,
            )
            along = jnp.sum(key * dkey, axis=-1, keepdims=True)
            gconv_ref[pl.ds(HALO, length), pl.ds(cols + at, width)] = slopes_ref[pair] * (
                dkey - key * along
            )
            gconv_ref[pl.ds(HALO, length), pl.ds(2 * cols + at, width)] = (
                rate * dvalue * vslopes_ref[pair]
            )
            rate_grads = rate_grads + jnp.where(
                lane == RATE_AT + h, drate * rate * (1.0 - rate), 0.0
            )
        unconvolve(s, 1)
        unconvolve(s, 2)
        pre_ref[here, 3 * cols :] = rate_grads.astype(bf16)

    ends = c == ctx_size - 1
    starts = c == 0
    inside = (c > 0) & (c < ctx_size - 1)
    begins = (ctx_size - 1 - c) // (ctx_size - 1)

    final = c // (ctx_size - 1)

    @pl.loop(0, 3 * seqs)
    def _(k):
        part = k // seqs
        s = lax.rem(k, seqs)
        odd = lax.rem(k, 2) == seqs % 2
        later = (1 - begins) * s + begins * lax.rem((k + seqs) // 2, seqs)

        @pl.when(k == 2 + 3 * final)
        def _():
            cube.middle()

        @pl.when(k == 4 + 4 * final)
        def _():
            cube.finish(total_ref)
            loads["resid"].wait()
            inner = tail.total().astype(bf16)
            right = stacked([wide_ref[core, 7] for core in range(2)])
            rows = resid_ref[...] + total_ref[...] + SCALE * mm(inner, right)
            out_ref[mine, :] = (kept(lens_ref, t, c, length) * rows).astype(bf16)
            down_inner_ref[mine, :] = inner
            cube.spread()
            tail.start(1)

        @pl.when(k == 6 + 4 * final)
        def _():
            cube.relay()

        @pl.when((ends & (part == 1)) | ((starts | inside) & (part == 0)))
        def _():
            early(s)

        @pl.when((ends & (part == 0)) | (inside & (part == 1)) | (starts & (part > 0) & odd))
        def _():
            link(later)

        @pl.when(((ends | inside) & (part == 2)) | (starts & (part > 0) & jnp.logical_not(odd)))
        def _():
            late(later)

    halo_in[1] = halo_out[1].astype(bf16)
    halo = remote(halo_in.at[1], halo_in.at[0], halo_send, halo_recv, {"ctx": c - 1})

    @pl.when(c > 0)
    def _():
        halo.start()

    @pl.when(c < ctx_size - 1)
    def _():
        halo.wait_recv()
        for s in range(seqs):
            last = s * length + length - 16
            block = pre_ref[last : last + 16, : 3 * cols].astype(f32)
            edge = (halo_out[0, s] + halo_in[0, s].astype(f32))
            pre_ref[last : last + 16, : 3 * cols] = jnp.concatenate(
                [block[:HALO], edge], axis=0
            ).astype(bf16)

    @pl.when(c > 0)
    def _():
        halo.wait_send()

        @pl.loop(0, seqs)
        def _(s):
            remote(
                chain_out.at[s], after_ref.at[pl.ds(0, heads)], chain_send.at[s], chain_recv.at[s],
                {"ctx": c - 1},
            ).wait_send()

    for name in ("w", "back", "into"):
        loads[name].wait()
    cube.done()
    block_store = pltpu.make_async_copy(out_ref, block_hbm, store_sem.at[0])
    block_store.start()
    tail2_src[...] = (SCALE * mt(pre_ref[...], back_ref[...])).astype(bf16)
    tail2.start(0)

    def project(half, chunk):
        rows = cube2.columns(half, chunk)
        part = mm(pre_ref[:, 3 * cols :], into_ref[:, rows])
        for i in range(3):
            part = part + mt(pre_ref[:, i * cols : (i + 1) * cols], w_ref[i, rows, :])
        src[:, rows] = part.astype(bf16)
        cube2.start(half, chunk)

    cube2.each(project)
    inner = tail2.total().astype(bf16)
    inner_grad_ref[mine, :] = inner
    tail2.start(1)
    loads["n2"].wait()
    feed_left = tm(feed_grad_ref[...], normed_ref[...])
    fetch("n1", n1_hbm, normed_ref)
    pack[:, :, used:] = jnp.zeros((2, 8, pack.shape[2] - used), bf16)
    loads["heads"].wait()
    out_left = tm(out_grad, heads_ref[...])
    out_right = SCALE * tm(out_inner_ref[...], low_ref[...])
    right = SCALE * tm(inner_ref[...], pre_ref[...])
    tail.wait(1)
    masked = jnp.concatenate(
        [
            kept(lens_ref, s, c, length) * down_inner_ref[s * length : (s + 1) * length, :].astype(f32)
            for s in range(seqs)
        ],
        axis=0,
    )
    loads["grad"].wait()
    down_right = SCALE * tm(masked, grad_ref[...])
    for core in range(2):
        at = core * 8
        put("ol", core, out_left[at : at + 8])
        put("or", core, out_right[at : at + 8])
        put("dr", core, down_right[at : at + 8])
        put("dl", core, down_left_ref[at : at + 8, :])
        at = core * 16
        put("gl", core, feed_left[at : at + 8])
        put("ul", core, feed_left[at + 8 : at + 16])
        put("gr", core, gate_right_ref[at : at + 8, :])
        put("ur", core, up_right_ref[at + 8 : at + 16, :])
        for kind, name in enumerate(("qr", "kr", "vr", "rr")):
            at = core * 32 + kind * 8
            put(name, core, right[at : at + 8, kind * cols : kind * cols + plan[name][1]])
    block_store.wait()
    cube2.middle()
    loads["n1"].wait()
    tail2.wait(1)
    left = tm(inner_grad_ref[...], normed_ref[...])
    for core in range(2):
        for kind, name in enumerate(("ql", "kl", "vl", "rl")):
            at = core * 32 + kind * 8
            put(name, core, left[at : at + 8])
    swap = remote(pack.at[1 - f], mate_in, swap_send, swap_recv, mate)
    swap.start()
    cube2.finish(total_ref)
    swap.wait_recv()
    both = (pack[f].astype(f32) + mate_in[...].astype(f32)).astype(bf16)
    piece = both.shape[1] // ctx_size
    for j in range(ctx_size):
        mine_ref[j] = both[:, j * piece : (j + 1) * piece]
    sends = []
    spreads = []
    for i in range(ctx_size - 1):
        peer = {"ctx": lax.rem(c + 1 + i, ctx_size)}
        back = ctx_size - 2 - i
        sends.append(
            remote(
                mine_ref.at[lax.rem(c + 1 + i, ctx_size)],
                got.at[back],
                part_send.at[0, i],
                part_recv.at[0, back],
                peer,
            )
        )
        spreads.append(
            remote(summed.at[c], summed.at[c], part_send.at[1, i], part_recv.at[1, back], peer)
        )
    for copy in sends:
        copy.start()
    loads["x"].wait()
    loads["gresid"].wait()
    grad_first = total_ref[...] + mm(inner, into_ref[...])
    grad = gresid_ref[...] + norm_back(x_ref[...].astype(f32), gain_ref[...], grad_first)
    out_ref[mine, :] = grad.astype(bf16)
    cube2.spread()
    for copy in sends:
        copy.wait_recv()
    total = mine_ref[c].astype(f32)
    for i in range(ctx_size - 1):
        total = total + got[i].astype(f32)
    summed[c] = total.astype(bf16)
    for copy in spreads:
        copy.start()
    cube2.relay()
    for copy in spreads:
        copy.wait_recv()
    for j in range(ctx_size):
        packed_ref[:, j * piece : (j + 1) * piece] = summed[j].astype(f32)
    cube2.done()
    grad_store = pltpu.make_async_copy(out_ref, input_grad_hbm, store_sem.at[1])
    grad_store.start()
    swap.wait_send()
    for copy in sends + spreads:
        copy.wait_send()
    tail.done()
    tail2.done()
    grad_store.wait()


def deal_kernel(strips, packed_ref, *outs):
    for out, (at, wide) in zip(outs, strips):
        out[...] = packed_ref[:, at : at + wide]


def local(ctx_size, tp_size, *arguments):
    (
        hidden_in,
        seq_lengths,
        mixer_gain,
        feed_gain,
        query_weight,
        key_weight,
        value_weight,
        rate_weight,
        query_conv,
        key_conv,
        value_conv,
        head_gain,
        output_weight,
        gate_weight,
        up_weight,
        down_weight,
        query_left,
        query_right,
        key_left,
        key_right,
        value_left,
        value_right,
        rate_left,
        rate_right,
        output_left,
        output_right,
        gate_left,
        gate_right,
        up_left,
        up_right,
        down_left,
        down_right,
        output_grad,
    ) = arguments
    seqs, length, model = hidden_in.shape
    heads = rate_weight.shape[1]
    width = head_gain.shape[0]
    cols = heads * width
    rows = seqs * length
    units = gate_weight.shape[1]
    half = query_weight.shape[0]
    pairs = seqs * heads
    x = hidden_in.reshape(rows, model)
    grad_rows = output_grad.reshape(rows, model)
    rate_from = jnp.pad(rate_right, ((0, 0), (RATE_AT, LANES - RATE_AT - heads)))
    rate_rows = jnp.pad(rate_weight.T, ((0, 8 - heads), (0, 0)))
    wides = (
        query_left.T,
        key_left.T,
        value_left.T,
        rate_left.T,
        gate_left.T,
        up_left.T,
        output_right,
        down_right,
    )
    slims = (
        query_right,
        key_right,
        value_right,
        rate_from,
        output_left.T,
        gate_right,
        up_right,
        down_left.T,
    )
    slim_wide = sum(item.shape[1] for item in slims)
    gain1, gain2, gain3 = mixer_gain[None, :], feed_gain[None, :], head_gain[None, :]
    ext = length + HALO
    square = (pairs, width, width)
    tall = (pairs, length, width)
    block = rows // tp_size
    smem = pl.BlockSpec(memory_space=pltpu.SMEM)
    mixer_sizes = (seqs, length, heads, width, ctx_size, tp_size)
    kept_shapes = (
        shape((rows, model), bf16),
        shape((2, 8, 8, model), bf16),
        shape((2, 8, slim_wide), bf16),
        shape((LANES, model), bf16),
        shape((LANES, 3 * cols + LANES), bf16),
        shape((seqs, ext, 3 * cols), f32),
        shape((rows, LANES), bf16),
        shape((rows, LANES), f32),
        shape((pairs, length, length), bf16),
        shape(tall, bf16),
        shape(tall, f32),
        shape(tall, bf16),
        shape(tall, f32),
        shape(square, bf16),
        shape((rows, cols), bf16),
        shape(square, bf16),
        shape((rows, units), f32),
        shape((rows, LANES), bf16),
    )
    (
        second,
        out_inner,
        residual,
        wo,
        wg,
        wu,
        wd,
        wqkv,
        n1,
        wide_all,
        slim_all,
        into,
        back,
        pre_ext,
        inner,
        rates,
        inverse,
        wkey,
        wval,
        reach,
        local_out,
        step_map,
        heads_low,
        start,
        active,
        down_grad,
    ) = pl.pallas_call(
        functools.partial(mixer_kernel, mixer_sizes),
        out_shape=(
            shape((rows, model), bf16),
            shape((rows, LANES), bf16),
            shape((block, model), f32),
            shape(output_weight.shape, bf16),
            shape(gate_weight.shape, bf16),
            shape(up_weight.shape, bf16),
            shape(down_weight.shape, bf16),
            shape((3, model, cols), bf16),
        )
        + kept_shapes,
        in_specs=[smem] + [VMEM] * 7 + [ANY] * 25,
        out_specs=(VMEM,) * 3 + (ANY,) * (5 + len(kept_shapes)),
        scratch_shapes=[pltpu.VMEM(item.shape, item.dtype) for item in kept_shapes]
        + [
            pltpu.VMEM(square, f32),
            pltpu.VMEM((3, model, cols), bf16),
            pltpu.VMEM((8, model), bf16),
            pltpu.VMEM((seqs, HALO, 3 * cols), bf16),
            pltpu.VMEM((seqs, HALO, 3 * cols), bf16),
            pltpu.VMEM((LANES, 3 * cols + LANES), f32),
            pltpu.VMEM((LANES, model), f32),
            pltpu.VMEM((seqs, heads, width, width), bf16),
            pltpu.VMEM((2,) + output_weight.shape, bf16),
            pltpu.VMEM((2,) + down_weight.shape, bf16),
            pltpu.VMEM((rows, model), bf16),
            DMA((24,)),
            DMA((24,)),
            DMA((20,)),
            DMA((19,)),
            DMA,
            DMA,
            DMA((4,)),
            DMA,
            DMA((seqs,)),
            DMA((seqs,)),
        ]
        + cube_scratch(rows, model)
        + tail_scratch(rows, tp_size),
        compiler_params=params(0),
        name="mixer",
    )(
        seq_lengths,
        x,
        gain1,
        gain2,
        gain3,
        query_conv,
        key_conv,
        value_conv,
        query_weight,
        key_weight,
        value_weight,
        rate_rows,
        *wides,
        *slims,
        output_weight,
        gate_weight,
        up_weight,
        down_weight,
        grad_rows,
    )
    (
        resid_low,
        feed_grad,
        grad_residual,
        down_part,
        down_tail,
        gate_right_grad,
        up_right_grad,
        down_left_grad,
    ) = pl.pallas_call(
        functools.partial(feed_kernel, (seqs, length, cols, ctx_size, tp_size)),
        out_shape=(
            shape((rows, model), bf16),
            shape((rows, LANES), bf16),
            shape((block, model), f32),
            shape((rows, model), bf16),
            shape((rows, LANES), bf16),
            shape((32, units), f32),
            shape((32, units), f32),
            shape((32, units), f32),
        ),
        in_specs=[smem] + [VMEM] * 7 + [ANY] * 7,
        out_specs=(VMEM,) * 8,
        scratch_shapes=[
            pltpu.VMEM((2,) + gate_weight.shape, bf16),
            pltpu.VMEM((2,) + up_weight.shape, bf16),
            pltpu.VMEM((2,) + down_weight.shape, bf16),
            pltpu.VMEM((rows, units), bf16),
            pltpu.VMEM((rows, units), bf16),
            pltpu.VMEM((rows, units), bf16),
            pltpu.VMEM((rows, LANES), bf16),
            pltpu.VMEM((LANES, units), bf16),
            pltpu.VMEM((LANES, units), bf16),
            pltpu.VMEM((block, model), bf16),
            DMA((3, 2)),
            DMA,
        ]
        + cube_scratch(rows, model)
        + tail_scratch(rows, tp_size),
        compiler_params=params(2),
        name="feed",
    )(
        seq_lengths,
        second,
        active,
        residual,
        gain2,
        wide_all,
        slim_all,
        down_grad,
        grad_rows,
        gate_weight,
        wg,
        up_weight,
        wu,
        down_weight,
        wd,
    )
    plan, used = strip_plan(cols, model, units)
    grain = LANES * ctx_size
    total_wide = -(-used // grain) * grain
    piece = total_wide // ctx_size
    block_out, input_grad, packed = pl.pallas_call(
        functools.partial(back_kernel, mixer_sizes),
        out_shape=(
            shape((rows, model), bf16),
            shape((rows, model), bf16),
            shape((8, total_wide), f32),
        ),
        in_specs=[smem] + [VMEM] * 15 + [ANY] * 22,
        out_specs=(ANY, ANY, VMEM),
        scratch_shapes=[
            pltpu.VMEM(square, bf16),
            pltpu.VMEM(square, bf16),
            pltpu.VMEM(tall, bf16),
            pltpu.VMEM(tall, f32),
            pltpu.VMEM((pairs, length, length), bf16),
            pltpu.VMEM(tall, bf16),
            pltpu.VMEM(tall, f32),
            pltpu.VMEM((seqs, ext, 3 * cols), f32),
            pltpu.VMEM((rows, LANES), f32),
            pltpu.VMEM((rows, cols), bf16),
            pltpu.VMEM((rows, model), bf16),
            pltpu.VMEM((block, model), f32),
            pltpu.VMEM((rows, model), bf16),
            pltpu.VMEM((rows, model), bf16),
            pltpu.VMEM((block, model), bf16),
            pltpu.VMEM((block, model), f32),
            pltpu.VMEM((3, model, cols), bf16),
            pltpu.VMEM((LANES, 3 * cols + LANES), bf16),
            pltpu.VMEM((LANES, model), bf16),
            pltpu.VMEM((2,) + output_weight.shape, bf16),
            pltpu.VMEM((rows, model), bf16),
            pltpu.VMEM((rows, 3 * cols + LANES), bf16),
            pltpu.VMEM(tall, f32),
            pltpu.VMEM(square, bf16),
            pltpu.VMEM((seqs, heads, width, width), bf16),
            pltpu.VMEM((HALO + length + HALO, 3 * cols), f32),
            pltpu.VMEM((2, seqs, HALO, 3 * cols), f32),
            pltpu.VMEM((2, seqs, HALO, 3 * cols), bf16),
            pltpu.VMEM((rows, LANES), bf16),
            pltpu.VMEM(tall, f32),
            pltpu.VMEM(tall, f32),
            pltpu.VMEM(tall, f32),
            pltpu.VMEM(tall, f32),
            pltpu.VMEM(tall, f32),
            pltpu.VMEM(tall, f32),
            pltpu.VMEM(tall, bf16),
            pltpu.VMEM((rows, LANES), bf16),
            pltpu.VMEM((rows, LANES), bf16),
            pltpu.VMEM((2, 8, total_wide), bf16),
            pltpu.VMEM((8, total_wide), bf16),
            pltpu.VMEM((ctx_size, 8, piece), bf16),
            pltpu.VMEM((ctx_size - 1, 8, piece), bf16),
            pltpu.VMEM((ctx_size, 8, piece), bf16),
            DMA((BACK_LOADS,)),
            DMA((2,)),
            DMA((seqs,)),
            DMA((seqs,)),
            DMA,
            DMA,
            DMA,
            DMA,
            DMA((2, ctx_size - 1)),
            DMA((2, ctx_size - 1)),
        ]
        + cube_scratch(rows, model)[1:]
        + [DMA((4, 2, CHUNKS, 2)), DMA((4, 2, CHUNKS, 2))]
        + tail_scratch(rows, tp_size)[1:] * 2,
        compiler_params=params(3),
        name="back",
    )(
        seq_lengths,
        resid_low,
        gain3,
        gain1,
        query_conv,
        key_conv,
        value_conv,
        wide_all,
        slim_all,
        down_tail,
        feed_grad,
        out_inner,
        inner,
        gate_right_grad,
        up_right_grad,
        down_left_grad,
        start,
        step_map,
        reach,
        local_out,
        inverse,
        wkey,
        wval,
        pre_ext,
        rates,
        heads_low,
        down_part,
        residual,
        grad_rows,
        second,
        n1,
        x,
        grad_residual,
        wqkv,
        back,
        into,
        output_weight,
        wo,
    )
    strips = tuple(plan.values())
    shares = list(
        pl.pallas_call(
            functools.partial(deal_kernel, strips),
            out_shape=tuple(shape((8, wide), f32) for _, wide in strips),
            in_specs=[VMEM],
            out_specs=(VMEM,) * len(strips),
            name="deal",
        )(packed)
    )
    shares[7] = shares[7][:, RATE_AT : RATE_AT + heads]
    lefts = (0, 2, 4, 6, 8, 10, 12, 14)
    shares = [item.T if i in lefts else item for i, item in enumerate(shares)]
    return (
        block_out.reshape(seqs, length, model),
        input_grad.reshape(seqs, length, model),
    ) + tuple(shares)


def solution(mesh):
    placed = (
        P("fsdp", "ctx", None),
        P("fsdp"),
        P(),
        P(),
        P("fsdp", "tp"),
        P("fsdp", "tp"),
        P("fsdp", "tp"),
        P("fsdp", "tp"),
        P(None, "tp"),
        P(None, "tp"),
        P(None, "tp"),
        P(),
        P("tp", "fsdp"),
        P("fsdp", "tp"),
        P("fsdp", "tp"),
        P("tp", "fsdp"),
    )
    left_in, left_over, right_over, right_in = (
        P(None, "fsdp"),
        P("tp", "fsdp"),
        P("fsdp", None),
        P("fsdp", "tp"),
    )
    adapters = (left_in, right_in) * 4 + (left_over, right_over) + (left_in, right_in) * 2 + (
        left_over,
        right_over,
    )
    rows = P("fsdp", "ctx", None)
    return jax.shard_map(
        functools.partial(local, mesh.shape["ctx"], mesh.shape["tp"]),
        mesh=mesh,
        in_specs=placed + adapters + (rows,),
        out_specs=(rows, rows) + adapters,
        check_vma=False,
    )
```

```python
import functools

import jax
import jax.numpy as jnp
from jax import lax
from jax.experimental import pallas as pl
from jax.experimental.pallas import tpu as pltpu
from jax.sharding import PartitionSpec as P

MESH = pl.DeviceIdType.MESH
ANY = pl.BlockSpec(memory_space=pl.ANY)
VMEM = pl.BlockSpec(memory_space=pltpu.VMEM)
DMA = pltpu.SemaphoreType.DMA
f32, bf16 = jnp.float32, jnp.bfloat16

CONV = 4
SCALE = 0.5
EPS = 1e-06
LANES = 128
RATE_AT = 64
HALO = 8


def shape(dims, kind):
    return jax.ShapeDtypeStruct(tuple(dims), kind)


def product(left, right, dims):
    return lax.dot_general(
        left.astype(bf16), right.astype(bf16), (dims, ((), ())), preferred_element_type=f32
    )


def mm(left, right):
    return product(left, right, ((1,), (0,)))


def mt(left, right):
    return product(left, right, ((1,), (1,)))


def tm(left, right):
    return product(left, right, ((0,), (0,)))


def params(collective, limit=58 << 20):
    return pltpu.CompilerParams(
        collective_id=collective, has_side_effects=True, vmem_limit_bytes=limit
    )


def grid_of(size):
    rows = lax.broadcasted_iota(jnp.int32, (size, size), 0)
    cols = lax.broadcasted_iota(jnp.int32, (size, size), 1)
    return rows, cols


def halves(values):
    high = values.astype(bf16)
    return high, (values - high.astype(f32)).astype(bf16)


def finer(left, right, dims):
    lhigh, llow = halves(left)
    rhigh, rlow = halves(right)
    (la,), (ra,) = dims
    return lax.dot_general(
        jnp.concatenate([lhigh, llow, lhigh], axis=la),
        jnp.concatenate([rhigh, rhigh, rlow], axis=ra),
        (dims, ((), ())),
        preferred_element_type=f32,
    )


def unit_inverses(stricts):
    size = stricts[0].shape[0]
    rows, cols = grid_of(size)
    eye = jnp.where(rows == cols, 1.0, 0.0)
    found = [eye - jnp.where((rows >> 1) == (cols >> 1), item, 0.0) for item in stricts]
    level = 1
    while (1 << level) < size:
        joined = ((rows >> (level + 1)) == (cols >> (level + 1))) & ((rows >> level) != (cols >> level))
        lows = [item.astype(bf16) for item in found]
        inner = [mm(jnp.where(joined, item, 0.0), low) for item, low in zip(stricts, lows)]
        found = [item - mm(low, part) for item, low, part in zip(found, lows, inner)]
        level += 1
    lows = [item.astype(bf16) for item in found]
    errors = []
    for item, low in zip(stricts, lows):
        pair = jnp.concatenate(halves(item), axis=1)
        errors.append(eye - low.astype(f32) - mm(pair, jnp.concatenate([low, low], axis=0)))
    return [low.astype(f32) + mm(low, error) for low, error in zip(lows, errors)]


def normed(values, gain):
    return values * lax.rsqrt(jnp.mean(values * values, axis=-1, keepdims=True) + EPS) * gain


def norm_back(values, gain, grad):
    scale = lax.rsqrt(jnp.mean(values * values, axis=-1, keepdims=True) + EPS)
    weighted = gain * grad
    return scale * weighted - values * (scale * scale * scale) * jnp.mean(
        values * weighted, axis=-1, keepdims=True
    )


def greet(barrier, peers):
    count = 0
    for peer, condition in peers:

        def tell(peer=peer):
            pl.semaphore_signal(barrier, inc=1, device_id=peer, device_id_type=MESH)

        if condition is None:
            tell()
            count = count + 1
        else:
            pl.when(condition)(tell)
            count = count + jnp.where(condition, 1, 0)
    pl.semaphore_wait(barrier, count)


def remote(source, target, send_sem, recv_sem, peer):
    return pltpu.make_async_remote_copy(
        src_ref=source,
        dst_ref=target,
        send_sem=send_sem,
        recv_sem=recv_sem,
        device_id=peer,
        device_id_type=MESH,
    )


def column(block, lane):
    return block[:, lane : lane + 1]


def convolved(ext_ref, taps, s, length, at, width):
    total = None
    for i in range(CONV):
        rows = ext_ref[s, pl.ds(HALO - (CONV - 1) + i, length), pl.ds(at, width)]
        term = taps[i : i + 1, at : at + width] * rows
        total = term if total is None else total + term
    return total


def kept(lens_ref, s, c, length):
    place = c * length + lax.broadcasted_iota(jnp.int32, (length, 1), 0)
    return jnp.where(place < lens_ref[s], 1.0, 0.0)


def part_of(at, size):
    return pl.ds(pl.multiple_of(at * size, size), size)


class Cube:
    def __init__(self, t, src, out, first, second, held, send_sem, recv_sem, chunks):
        self.y, self.x = t // 2, lax.rem(t, 2)
        self.t, self.src, self.out = t, src, out
        self.first, self.second, self.held = first, second, held
        self.send_sem, self.recv_sem = send_sem, recv_sem
        self.chunks = chunks
        self.block = src.shape[0] // 4
        self.half_width = src.shape[1] // 2
        self.width = self.half_width // chunks
        self.beside = self.y * 2 + (1 - self.x)
        self.above = (1 - self.y) * 2 + self.x

    def peer(self, side):
        return {"tp": self.beside * (1 - side) + self.above * side}

    def columns(self, half, chunk):
        return pl.ds(
            pl.multiple_of(half * self.half_width + chunk * self.width, self.width), self.width
        )

    def copy(self, stage, half, chunk, j):
        wide = self.columns(half, chunk)
        slim = part_of(chunk, self.width)
        send, recv = self.send_sem.at[stage, half, chunk, j], self.recv_sem.at[stage, half, chunk, j]
        across = self.above * (1 - half) + self.beside * half
        if stage == 0:
            g = (1 - half) * (2 * j + 1 - self.x) + half * (2 * (1 - self.y) + j)
            source, target = self.src.at[part_of(g, self.block), wide], self.first.at[half, j, :, slim]
            side = half
        elif stage == 1:
            source, target = self.held.at[half, :, slim], self.second.at[half, :, slim]
            side = 1 - half
        else:
            g = self.t if j == 0 else across
            source = target = self.out.at[part_of(g, self.block), wide]
            side = 1 - half if stage == 2 else half
        return remote(source, target, send, recv, self.peer(side))

    def each(self, body):
        @pl.loop(0, 2 * self.chunks)
        def _(k):
            body(lax.rem(k, 2), k // 2)

    def start(self, half, chunk):
        self.copy(0, half, chunk, 0).start()
        self.copy(0, half, chunk, 1).start()

    def block_at(self, i):
        flip_x, flip_y = (3 - i) // 2, lax.rem(i + 1, 2)
        y = self.y + flip_y * (1 - 2 * self.y)
        return y * 2 + self.x + flip_x * (1 - 2 * self.x)

    def send_block(self, i):
        def go(half, j):
            for chunk in range(self.chunks):
                self.copy(0, half, chunk, j).start()

        @pl.when(i == 0)
        def _():
            go(0, 1 - self.y)
            go(1, 1 - self.x)

        @pl.when(i == 1)
        def _():
            go(0, self.y)

        @pl.when(i == 2)
        def _():
            go(1, self.x)

    def pass_on(self, half, chunk):
        wide = self.columns(half, chunk)
        slim = part_of(chunk, self.width)
        across = self.above * (1 - half) + self.beside * half
        other = (1 - half) * (1 - self.y) + half * (1 - self.x)
        self.copy(0, half, chunk, other).wait_recv()
        self.held[half, :, slim] = (
            self.src[part_of(across, self.block), wide].astype(f32)
            + self.first[half, other, :, slim].astype(f32)
        ).astype(bf16)
        self.copy(1, half, chunk, 0).start()

    def middle(self):
        self.each(self.pass_on)

    def middle_half(self, half):
        @pl.loop(0, self.chunks)
        def _(chunk):
            self.pass_on(half, chunk)

    def finish(self, total_ref):
        def body(half, chunk):
            wide = self.columns(half, chunk)
            slim = part_of(chunk, self.width)
            mine = (1 - half) * self.y + half * self.x
            self.copy(0, half, chunk, mine).wait_recv()
            self.copy(1, half, chunk, 0).wait_recv()
            total_ref[:, wide] = (
                self.src[part_of(self.t, self.block), wide].astype(f32)
                + self.first[half, mine, :, slim].astype(f32)
                + self.second[half, :, slim].astype(f32)
            )

        self.each(body)

    def spread(self):
        def body(half, chunk):
            self.copy(2, half, chunk, 0).start()
            self.copy(3, half, chunk, 0).start()

        self.each(body)

    def relay(self):
        def body(half, chunk):
            self.copy(2, half, chunk, 0).wait_recv()
            self.copy(3, half, chunk, 1).start()

        self.each(body)

    def done(self):
        def body(half, chunk):
            for j in range(2):
                self.copy(3, half, chunk, j).wait_recv()
            for stage in range(4):
                for j in range(2 if stage in (0, 3) else 1):
                    self.copy(stage, half, chunk, j).wait_send()

        self.each(body)


class Tail:
    def __init__(self, t, src, out, got, send_sem, recv_sem, size):
        self.t, self.src, self.out, self.got, self.size = t, src, out, got, size
        self.send_sem, self.recv_sem = send_sem, recv_sem
        self.block = src.shape[0] // size

    def copies(self, stage):
        found = []
        for i in range(self.size - 1):
            g = lax.rem(self.t + 1 + i, self.size)
            if stage == 0:
                source, target = self.src.at[part_of(g, self.block)], self.got.at[self.size - 2 - i]
            else:
                source = target = self.out.at[part_of(self.t, self.block)]
            found.append(
                remote(
                    source,
                    target,
                    self.send_sem.at[stage, i],
                    self.recv_sem.at[stage, self.size - 2 - i],
                    {"tp": g},
                )
            )
        return found

    def start(self, stage):
        for copy in self.copies(stage):
            copy.start()

    def send_block(self, g):
        i = lax.rem(g - self.t - 1 + self.size, self.size)
        back = self.size - 2 - i
        remote(
            self.src.at[part_of(g, self.block)],
            self.got.at[back],
            self.send_sem.at[0, i],
            self.recv_sem.at[0, back],
            {"tp": g},
        ).start()

    def wait(self, stage):
        for copy in self.copies(stage):
            copy.wait_recv()

    def total(self):
        self.wait(0)
        total = self.src[part_of(self.t, self.block), :].astype(f32)
        for i in range(self.size - 1):
            total = total + self.got[i].astype(f32)
        return total

    def done(self):
        for stage in range(2):
            for copy in self.copies(stage):
                copy.wait_send()


CHUNKS = 4


def cube_scratch(rows, model):
    block = rows // 4
    return [
        pltpu.VMEM((rows, model), bf16),
        pltpu.VMEM((2, 2, block, model // 2), bf16),
        pltpu.VMEM((2, block, model // 2), bf16),
        pltpu.VMEM((2, block, model // 2), bf16),
        pltpu.VMEM((block, model), f32),
        DMA((4, 2, CHUNKS, 2)),
        DMA((4, 2, CHUNKS, 2)),
    ]


def tail_scratch(rows, size):
    return [
        pltpu.VMEM((rows, LANES), bf16),
        pltpu.VMEM((size - 1, rows // size, LANES), bf16),
        DMA((2, size - 1)),
        DMA((2, size - 1)),
    ]


def tp_peers(t, size):
    return [({"tp": lax.rem(t + 1 + i, size)}, None) for i in range(size - 1)]


def stacked(pieces):
    rows = sum(piece.shape[0] for piece in pieces)
    fill = jnp.zeros((LANES - rows, pieces[0].shape[1]), f32)
    return jnp.concatenate([piece.astype(f32) for piece in pieces] + [fill], axis=0).astype(bf16)


def slot_loads(pairs, f, sems):
    loads = []
    for i, (own, other, scratch) in enumerate(pairs):
        loads.append(pltpu.make_async_copy(own, scratch.at[f], sems.at[i, 0]))
        loads.append(pltpu.make_async_copy(other, scratch.at[1 - f], sems.at[i, 1]))
    for load in loads:
        load.start()
    return loads


def unit_steps(units, body):
    step = 2 * LANES
    whole = units // step

    @pl.loop(0, whole)
    def _(k):
        body(part_of(k, step))

    if units % step:
        body(pl.ds(whole * step, units % step))


def mixer_kernel(
    sizes,
    lens_ref,
    x_ref,
    gain_ref,
    gain2_ref,
    head_gain_ref,
    qtaps_ref,
    ktaps_ref,
    vtaps_ref,
    wq_ref,
    wk_ref,
    wv_ref,
    wr_ref,
    wide0,
    wide1,
    wide2,
    wide3,
    wide4,
    wide5,
    wide6,
    wide7,
    slim0,
    slim1,
    slim2,
    slim3,
    slim4,
    slim5,
    slim6,
    slim7,
    wo_own,
    wg_own,
    wu_own,
    wd_own,
    grad_hbm,
    n2_ref,
    out_inner_ref,
    resid_ref,
    wo_other,
    wg_other,
    wu_other,
    wd_other,
    wqkv_out,
    n1_out,
    wide_hbm,
    slim_hbm,
    into_out,
    back_out,
    ext_out,
    inner_out,
    rates_out,
    inv_out,
    wkey_out,
    wval_out,
    reach_out,
    local_out,
    map_out,
    heads_out,
    start_out,
    active_out,
    down_inner_out,
    n1_ref,
    wide_out,
    slim_out,
    into_ref,
    back_ref,
    ext_ref,
    inner_ref,
    rates_ref,
    inv_ref,
    wkey_ref,
    wval_ref,
    reach_ref,
    local_ref,
    map_ref,
    heads_ref,
    start_ref,
    active_ref,
    down_inner_ref,
    end_ref,
    w_ref,
    wr_all,
    halo_out,
    halo_in,
    back_f32,
    into_f32,
    chain_out,
    wo_ref,
    wd_ref,
    grad_ref,
    send_sem,
    recv_sem,
    local_sem,
    store_sem,
    halo_send,
    halo_recv,
    load_sem,
    grad_sem,
    chain_send,
    chain_recv,
    *scratch,
):
    seqs, length, heads, width, ctx_size, tp_size = sizes
    cols = heads * width
    half = wq_ref.shape[0]
    model = 2 * half
    half_model = half
    units = active_ref.shape[1]
    left_at = 3 * cols + LANES
    down_at = left_at + cols + 2 * units
    f = lax.axis_index("fsdp")
    c = lax.axis_index("ctx")
    t = lax.axis_index("tp")
    mate = {"fsdp": 1 - f}
    greet(
        pltpu.get_barrier_semaphore(),
        [(mate, None), ({"ctx": c - 1}, c > 0), ({"ctx": c + 1}, c < ctx_size - 1)]
        + tp_peers(t, tp_size),
    )
    src, first, second, held, total_ref, cube_send, cube_recv = scratch[:7]
    tail_src, tail_got, tail_send, tail_recv = scratch[7:]
    cube = Cube(t, src, n2_ref, first, second, held, cube_send, cube_recv, CHUNKS)
    tail = Tail(t, tail_src, out_inner_ref, tail_got, tail_send, tail_recv, tp_size)
    stores = []

    def store(pairs):
        for source, target in pairs:
            copy = pltpu.make_async_copy(source, target, store_sem.at[len(stores)])
            copy.start()
            stores.append(copy)

    top = pl.ds(pl.multiple_of(f * half, half), half)
    moves = []
    for i, ref in enumerate((wide0, wide1, wide2, wide3, wide4, wide5, wide6, wide7)):
        moves.append((ref, wide_out.at[f, i]))
    at = 0
    for ref in (slim0, slim1, slim2, slim3, slim4, slim5, slim6, slim7):
        moves.append((ref, slim_out.at[f, :, at : at + ref.shape[1]]))
        at += ref.shape[1]
    moves += [
        (wr_ref, wr_all.at[:, top]),
        (wq_ref, w_ref.at[0, top]),
        (wk_ref, w_ref.at[1, top]),
        (wv_ref, w_ref.at[2, top]),
    ]
    near = [pltpu.make_async_copy(src, dst, local_sem.at[i]) for i, (src, dst) in enumerate(moves)]
    local_count = len(moves)
    moves += [(wo_own, wo_ref.at[f]), (wg_own, wg_other), (wu_own, wu_other), (wd_own, wd_other)]
    across = [
        remote(src, dst, send_sem.at[i], recv_sem.at[i], mate) for i, (src, dst) in enumerate(moves)
    ]
    for copy in across[:local_count] + near:
        copy.start()
    own_loads = [
        pltpu.make_async_copy(wo_own, wo_ref.at[f], load_sem.at[0]),
        pltpu.make_async_copy(wd_own, wd_ref.at[f], load_sem.at[2]),
        pltpu.make_async_copy(grad_hbm, grad_ref, grad_sem),
    ]

    @pl.loop(0, seqs)
    def _(s):
        here = pl.ds(pl.multiple_of(s * length, length), length)
        n1_ref[here, :] = normed(x_ref[here, :].astype(f32), gain_ref[...]).astype(bf16)

    for i in range(local_count):
        near[i].wait()
        across[i].wait_recv()
    for copy in across[local_count:] + own_loads:
        copy.start()
    kinds = 4
    into_f32[...] = jnp.zeros_like(into_f32)
    back_f32[...] = jnp.zeros_like(back_f32)
    for core in range(2):
        for kind in range(kinds):
            spot = core * 32 + kind * 8
            into_f32[spot : spot + 8, :] = wide_out[core, kind].astype(f32)
        for kind in range(kinds):
            at = kind * cols
            wide = cols if kind < 3 else LANES
            back_f32[core * 32 + kind * 8 : core * 32 + kind * 8 + 8, at : at + wide] = slim_out[
                core, :, at : at + wide
            ].astype(f32)
    into_f32[RATE_AT : RATE_AT + heads, :] = wr_all[...].astype(f32)
    into_ref[...] = into_f32[...].astype(bf16)
    back_ref[...] = back_f32[...].astype(bf16)
    store([(w_ref, wqkv_out), (n1_ref, n1_out), (wide_out, wide_hbm), (slim_out, slim_hbm)])
    store([(into_ref, into_out), (back_ref, back_out)])

    def halo_of(s):
        return remote(
            halo_out.at[s], halo_in.at[s], halo_send.at[s], halo_recv.at[s], {"ctx": c + 1}
        )

    @pl.loop(0, seqs)
    def _(k):
        s = cube.block_at(k)
        here = pl.ds(pl.multiple_of(s * length, length), length)
        block = n1_ref[here, :]
        tail = mt(block, into_ref[...])
        inner = tail.astype(bf16)
        inner_ref[here, :] = inner
        for i in range(3):
            pre = mm(block, w_ref[i]) + SCALE * mm(inner, back_ref[:, i * cols : (i + 1) * cols])
            ext_ref[s, HALO : HALO + length, i * cols : (i + 1) * cols] = pre
            halo_out[s, :, i * cols : (i + 1) * cols] = pre[length - HALO :, :].astype(bf16)
        pre_rate = tail + SCALE * mm(inner, back_ref[:, 3 * cols :])
        rates_ref[here, :] = jax.nn.sigmoid(pre_rate) * kept(lens_ref, s, c, length)

        @pl.when(c < ctx_size - 1)
        def _():
            halo_of(s).start()

    taps = jnp.concatenate([qtaps_ref[...], ktaps_ref[...], vtaps_ref[...]], axis=1)
    row_at, col_at = grid_of(length)

    def solve(s):
        @pl.when(c > 0)
        def _():
            halo_of(s).wait_recv()
            ext_ref[s, 0:HALO, :] = halo_in[s].astype(f32)

        @pl.when(c == 0)
        def _():
            ext_ref[s, 0:HALO, :] = jnp.zeros((HALO, 3 * cols), f32)

        here = pl.ds(pl.multiple_of(s * length, length), length)
        rate_block = rates_ref[here, :]
        queries, keys, values, rates, stricts = [], [], [], [], []
        for h in range(heads):
            at = h * width
            parts = [
                jax.nn.silu(convolved(ext_ref, taps, s, length, i * cols + at, width))
                for i in range(3)
            ]
            query, key = [
                a * lax.rsqrt(jnp.sum(a * a, axis=-1, keepdims=True) + EPS) for a in parts[:2]
            ]
            rate = column(rate_block, RATE_AT + h)
            queries.append(query)
            keys.append(key)
            values.append(parts[2])
            rates.append(rate)
            stricts.append(
                jnp.where(row_at > col_at, rate * finer(key, key, ((1,), (1,))), 0.0)
            )
        inverses = unit_inverses(stricts)
        for h in range(heads):
            pair = s * heads + h
            query, key, value, rate, inverse = queries[h], keys[h], values[h], rates[h], inverses[h]
            wkey = mm(inverse, rate * key)
            wval = mm(inverse, rate * value)
            scores = jnp.where(row_at >= col_at, finer(query, key, ((1,), (1,))), 0.0)
            inv_ref[pair] = inverse.astype(bf16)
            wkey_ref[pair] = wkey.astype(bf16)
            wval_ref[pair] = wval
            reach_ref[pair] = (query - mm(scores, wkey)).astype(bf16)
            local_ref[pair] = finer(scores, wval, ((1,), (0,)))
            map_ref[pair] = (jnp.where(row_at == col_at, 1.0, 0.0) - tm(key, wkey)).astype(bf16)
            end_ref[pair] = tm(key, wval)

    gain = head_gain_ref[...]

    def hop_of(pair):
        return remote(
            chain_out.at[pair],
            start_ref.at[pair],
            chain_send.at[pair],
            chain_recv.at[pair],
            {"ctx": c + 1},
        )

    def link(s):
        for h in range(heads):
            pair = s * heads + h

            @pl.when(c > 0)
            def _(pair=pair):
                hop_of(pair).wait_recv()

            @pl.when(c == 0)
            def _(pair=pair):
                start_ref[pair] = jnp.zeros((width, width), bf16)

            @pl.when(c < ctx_size - 1)
            def _(pair=pair):
                chain_out[pair] = (mm(map_ref[pair], start_ref[pair]) + end_ref[pair]).astype(bf16)
                hop_of(pair).start()

        here = part_of(s, length)
        for h in range(heads):
            pair = s * heads + h
            mixed = mm(reach_ref[pair], start_ref[pair]) + local_ref[pair]
            heads_ref[here, h * width : (h + 1) * width] = normed(mixed, gain).astype(bf16)

    into = stacked([slim_out[core, :, left_at : left_at + cols] for core in range(2)])
    across[local_count].wait_recv()
    own_loads[0].wait()
    store([(wo_ref.at[1 - f], wo_other)])

    def project(i):
        here = part_of(cube.block_at(i), length)
        low = heads_ref[here, :]
        for side in range(2):
            src[here, side * half_model : (side + 1) * half_model] = mm(low, wo_ref[side]).astype(bf16)
        tail_src[here, :] = mt(low, into).astype(bf16)
        cube.send_block(i)

        @pl.when(i < 3)
        def _():
            tail.send_block(cube.block_at(i))

        @pl.when(i == 2)
        def _():
            cube.middle_half(1)

        @pl.when(i == 3)
        def _():
            cube.middle_half(0)

    @pl.loop(0, seqs + ctx_size - 1)
    def _(k):
        @pl.when(k < seqs)
        def _():
            solve(cube.block_at(k))

        @pl.when((k >= c) & (k < c + seqs))
        def _():
            link(cube.block_at(k - c))
            project(k - c)

    store(
        [
            (ext_ref, ext_out),
            (inner_ref, inner_out),
            (rates_ref, rates_out),
            (inv_ref, inv_out),
            (wkey_ref, wkey_out),
            (wval_ref, wval_out),
            (reach_ref, reach_out),
            (local_ref, local_out),
            (map_ref, map_out),
            (heads_ref, heads_out),
            (start_ref, start_out),
        ]
    )
    cube.finish(total_ref)
    inner = tail.total().astype(bf16)
    here = part_of(t, length)
    right = stacked([wide_out[core, 6] for core in range(2)])
    resid = x_ref[here, :].astype(f32) + total_ref[...] + SCALE * mm(inner, right)
    resid_ref[...] = resid
    out_inner_ref[here, :] = inner
    n2_ref[here, :] = normed(resid, gain2_ref[...]).astype(bf16)
    cube.spread()
    tail.start(1)
    for copy in across[local_count + 1 :]:
        copy.wait_recv()
    wd_load = pltpu.make_async_copy(wd_other, wd_ref.at[1 - f], load_sem.at[3])
    wd_load.start()
    own_loads[2].wait()
    down_from = stacked([wide_out[core, 7] for core in range(2)])
    for s in range(seqs):
        here = pl.ds(s * length, length)
        down_inner_ref[here, :] = (
            kept(lens_ref, s, c, length) * (SCALE * mt(grad_ref[here, :], down_from))
        ).astype(bf16)
    own_loads[1].wait()
    wd_load.wait()

    def activate(at):
        into_down = stacked([slim_out[core, :, pl.ds(down_at + at.start, at.size)] for core in range(2)])
        part = mt(grad_ref[:, :half_model], wd_ref[0, at, :])
        part = part + mt(grad_ref[:, half_model:], wd_ref[1, at, :])
        part = part + mm(down_inner_ref[...], into_down)
        for s in range(seqs):
            active_ref[s * length : (s + 1) * length, at] = (
                kept(lens_ref, s, c, length) * part[s * length : (s + 1) * length]
            )

    cube.relay()
    unit_steps(units, activate)
    store([(active_ref, active_out), (down_inner_ref, down_inner_out)])
    tail.wait(1)
    cube.done()
    tail.done()
    for copy in across:
        copy.wait_send()
    for copy in stores:
        copy.wait()

    @pl.when(c < ctx_size - 1)
    def _():
        @pl.loop(0, seqs)
        def _(s):
            halo_of(s).wait_send()

        @pl.loop(0, seqs * heads)
        def _(pair):
            hop_of(pair).wait_send()


def feed_kernel(
    sizes,
    lens_ref,
    n2_ref,
    gain_ref,
    wide_ref,
    slim_ref,
    down_grad_ref,
    grad_ref,
    wg_own,
    wg_other,
    wu_own,
    wu_other,
    wd_own,
    wd_other,
    active_hbm,
    resid_hbm,
    low_ref,
    inner_grad_ref,
    gresid_hbm,
    down_hbm,
    down_tail_ref,
    gate_right_ref,
    up_right_ref,
    down_left_ref,
    wg_ref,
    wu_ref,
    wd_ref,
    act_ref,
    dgate_ref,
    dup_ref,
    inner_ref,
    back_gate,
    back_up,
    own_grad,
    active_ref,
    resid_ref,
    gresid_ref,
    down_ref,
    load_sem,
    piece_sem,
    store_sem,
    grad_sem,
    *scratch,
):
    seqs, length, cols, ctx_size, tp_size = sizes
    model = n2_ref.shape[1]
    half_model = model // 2
    units = active_ref.shape[1]
    gate_at = 4 * cols + LANES
    up_at = gate_at + units
    down_at = up_at + units
    f = lax.axis_index("fsdp")
    c = lax.axis_index("ctx")
    t = lax.axis_index("tp")
    step = 2 * LANES
    spans = [pl.ds(at, min(step, units - at)) for at in range(0, units, step)]
    whole = [
        pltpu.make_async_copy(wd_own, wd_ref.at[f], load_sem.at[0]),
        pltpu.make_async_copy(wd_other, wd_ref.at[1 - f], load_sem.at[1]),
        pltpu.make_async_copy(resid_hbm, resid_ref, load_sem.at[2]),
    ]

    def piece_loads(at, k):
        return [
            pltpu.make_async_copy(source.at[:, at], target.at[:, at], piece_sem.at[k, i])
            for i, (source, target) in enumerate(
                (
                    (wg_own, wg_ref.at[f]),
                    (wg_other, wg_ref.at[1 - f]),
                    (wu_own, wu_ref.at[f]),
                    (wu_other, wu_ref.at[1 - f]),
                    (active_hbm, active_ref),
                )
            )
        ]

    for k, at in enumerate(spans):
        for load in piece_loads(at, k):
            load.start()
    for load in whole:
        load.start()
    here = part_of(t, length)
    own_load = pltpu.make_async_copy(grad_ref.at[here], own_grad, grad_sem)
    own_load.start()
    greet(pltpu.get_barrier_semaphore(), tp_peers(t, tp_size))
    src, first, second, held, total_ref, send_sem, recv_sem = scratch[:7]
    tail_src, tail_got, tail_send, tail_recv = scratch[7:]
    cube = Cube(t, src, low_ref, first, second, held, send_sem, recv_sem, CHUNKS)
    tail = Tail(t, tail_src, inner_grad_ref, tail_got, tail_send, tail_recv, tp_size)
    into = stacked([wide_ref[core, 4 + kind] for core in range(2) for kind in range(2)])
    blank = jnp.zeros((8, units), bf16)
    gates = [slim_ref[core, :, gate_at : gate_at + units] for core in range(2)]
    ups = [slim_ref[core, :, up_at : up_at + units] for core in range(2)]
    back_gate[...] = stacked([gates[0], blank, gates[1], blank])
    back_up[...] = stacked([blank, ups[0], blank, ups[1]])
    inner_ref[...] = mt(n2_ref[...], into).astype(bf16)
    def forward(at, k):
        for load in piece_loads(at, k):
            load.wait()
        pre = []
        for weight, back in ((wg_ref, back_gate), (wu_ref, back_up)):
            part = mm(n2_ref[:, :half_model], weight[0, :, at])
            part = part + mm(n2_ref[:, half_model:], weight[1, :, at])
            pre.append(part + SCALE * mm(inner_ref[...], back[:, at]))
        gate, up = pre
        sigma = jax.nn.sigmoid(gate)
        silu = gate * sigma
        active = active_ref[:, at]
        act_ref[:, at] = (silu * up).astype(bf16)
        dgate_ref[:, at] = (active * up * (sigma * (1.0 + gate * (1.0 - sigma)))).astype(bf16)
        dup_ref[:, at] = (active * silu).astype(bf16)

    full = units // step

    @pl.loop(0, full)
    def _(k):
        forward(part_of(k, step), k)

    if units % step:
        forward(spans[-1], full)
    tail_src[...] = (
        SCALE * (mt(dgate_ref[...], back_gate[...]) + mt(dup_ref[...], back_up[...]))
    ).astype(bf16)
    tail.start(0)

    def project(half, chunk):
        rows = part_of(chunk, cube.width)
        src[:, cube.columns(half, chunk)] = (
            mt(dgate_ref[...], wg_ref[half, rows, :]) + mt(dup_ref[...], wu_ref[half, rows, :])
        ).astype(bf16)
        cube.start(half, chunk)

    cube.each(project)
    cube.middle()
    for load in whole:
        load.wait()

    def descend(half, chunk):
        down_ref[:, cube.columns(half, chunk)] = mm(
            act_ref[...], wd_ref[half, :, part_of(chunk, cube.width)]
        ).astype(bf16)

    cube.each(descend)
    down_store = pltpu.make_async_copy(down_ref, down_hbm, store_sem.at[0])
    down_store.start()
    cube.finish(total_ref)
    own_load.wait()
    inner = tail.total().astype(bf16)
    grad_second = total_ref[...] + mm(inner, into)
    grad = own_grad[...].astype(f32) * kept(lens_ref, t, c, length) + norm_back(
        resid_ref[...], gain_ref[...], grad_second
    )
    gresid_ref[...] = grad
    grad_store = pltpu.make_async_copy(gresid_ref, gresid_hbm, store_sem.at[1])
    grad_store.start()
    low_ref[here, :] = grad.astype(bf16)
    inner_grad_ref[here, :] = inner
    cube.spread()
    tail.start(1)
    into_down = stacked([slim_ref[core, :, down_at : down_at + units] for core in range(2)])
    down_tail_ref[...] = mt(act_ref[...], into_down).astype(bf16)
    gate_right_ref[...] = SCALE * tm(inner_ref[...], dgate_ref[...])[:32]
    cube.relay()
    up_right_ref[...] = SCALE * tm(inner_ref[...], dup_ref[...])[:32]
    down_left_ref[...] = tm(down_grad_ref[...], act_ref[...])[:32]
    tail.wait(1)
    cube.done()
    tail.done()
    down_store.wait()
    grad_store.wait()


def strip_plan(cols, model, units):
    widths = (
        ("ql", model), ("qr", cols), ("kl", model), ("kr", cols), ("vl", model), ("vr", cols),
        ("rl", model), ("rr", LANES), ("ol", cols), ("or", model), ("gl", model), ("gr", units),
        ("ul", model), ("ur", units), ("dl", units), ("dr", model),
    )
    plan, at = {}, 0
    for name, wide in widths:
        plan[name] = (at, wide)
        at += wide
    return plan, at


BACK_LOADS = 24


def back_kernel(
    sizes,
    lens_ref,
    low_ref,
    head_gain_ref,
    gain_ref,
    qtaps_ref,
    ktaps_ref,
    vtaps_ref,
    wide_ref,
    slim_ref,
    tail_src,
    feed_grad_ref,
    out_inner_ref,
    inner_ref,
    gate_right_ref,
    up_right_ref,
    down_left_ref,
    start_hbm,
    map_hbm,
    reach_hbm,
    local_hbm,
    inv_hbm,
    wkey_hbm,
    wval_hbm,
    ext_hbm,
    rates_hbm,
    heads_hbm,
    down_hbm,
    resid_hbm,
    grad_hbm,
    n2_hbm,
    n1_hbm,
    x_hbm,
    gresid_hbm,
    w_hbm,
    back_hbm,
    into_hbm,
    wo_own,
    wo_other,
    block_hbm,
    input_grad_hbm,
    packed_ref,
    start_ref,
    map_ref,
    reach_ref,
    local_ref,
    inv_ref,
    wkey_ref,
    wval_ref,
    ext_ref,
    rates_ref,
    heads_ref,
    src,
    resid_ref,
    grad_ref,
    normed_ref,
    x_ref,
    gresid_ref,
    w_ref,
    back_ref,
    into_ref,
    wo_ref,
    out_ref,
    pre_ref,
    dmix_ref,
    after_ref,
    chain_out,
    gconv_ref,
    halo_out,
    halo_in,
    down_inner_ref,
    keys_ref,
    slopes_ref,
    values_ref,
    vslopes_ref,
    dfresh_ref,
    dkeys_ref,
    fresh_ref,
    tail2_src,
    inner_grad_ref,
    pack,
    mate_in,
    mine_ref,
    got,
    summed,
    load_sem,
    store_sem,
    chain_send,
    chain_recv,
    halo_send,
    halo_recv,
    swap_send,
    swap_recv,
    part_send,
    part_recv,
    first,
    second,
    held,
    total_ref,
    cube_send,
    cube_recv,
    cube2_send,
    cube2_recv,
    src2,
    first2,
    second2,
    held2,
    tail_got,
    tail_send,
    tail_recv,
    tail2_got,
    tail2_send,
    tail2_recv,
):
    seqs, length, heads, width, ctx_size, tp_size = sizes
    cols = heads * width
    model = low_ref.shape[1]
    half_model = model // 2
    units = gate_right_ref.shape[1]
    left_at = 3 * cols + LANES
    pairs = seqs * heads
    plan, used = strip_plan(cols, model, units)
    f = lax.axis_index("fsdp")
    c = lax.axis_index("ctx")
    t = lax.axis_index("tp")
    mate = {"fsdp": 1 - f}
    mine = part_of(t, length)
    loads = {}

    def fetch(name, source, target):
        loads[name] = pltpu.make_async_copy(source, target, load_sem.at[len(loads)])
        loads[name].start()

    fetch("wo_own", wo_own, wo_ref.at[f])
    fetch("wo_other", wo_other, wo_ref.at[1 - f])
    fetch("src", down_hbm, src)
    fetch("reach", reach_hbm, reach_ref)
    fetch("start", start_hbm, start_ref)
    fetch("local", local_hbm, local_ref)
    fetch("map", map_hbm, map_ref)
    fetch("ext", ext_hbm, ext_ref)
    fetch("rates", rates_hbm, rates_ref)
    fetch("wkey", wkey_hbm, wkey_ref)
    fetch("wval", wval_hbm, wval_ref)
    fetch("inv", inv_hbm, inv_ref)
    fetch("heads", heads_hbm, heads_ref)
    fetch("resid", resid_hbm, resid_ref)
    fetch("n2", n2_hbm, normed_ref)
    fetch("grad", grad_hbm, grad_ref)
    greet(
        pltpu.get_barrier_semaphore(),
        [(mate, None)]
        + [({"ctx": lax.rem(c + 1 + i, ctx_size)}, None) for i in range(ctx_size - 1)]
        + tp_peers(t, tp_size),
    )
    cube = Cube(t, src, out_ref, first, second, held, cube_send, cube_recv, CHUNKS)
    tail = Tail(t, tail_src, down_inner_ref, tail_got, tail_send, tail_recv, tp_size)
    cube2 = Cube(t, src2, out_ref, first2, second2, held2, cube2_send, cube2_recv, CHUNKS)
    tail2 = Tail(t, tail2_src, inner_grad_ref, tail2_got, tail2_send, tail2_recv, tp_size)

    def put(name, core, rows):
        at, wide = plan[name]
        pack[core, :, at : at + wide] = rows.astype(bf16)

    tail.start(0)
    gain = head_gain_ref[...]
    taps = jnp.concatenate([qtaps_ref[...], ktaps_ref[...], vtaps_ref[...]], axis=1)
    row_at, col_at = grid_of(length)
    gconv_ref[...] = jnp.zeros_like(gconv_ref)
    from_out = stacked([wide_ref[core, 6] for core in range(2)])
    into_out = stacked([slim_ref[core, :, left_at : left_at + cols] for core in range(2)])
    out_grad = (SCALE * mt(low_ref[...], from_out)).astype(bf16)
    loads["wo_own"].wait()
    loads["wo_other"].wait()
    dheads = (
        mt(low_ref[:, :half_model], wo_ref[0])
        + mt(low_ref[:, half_model:], wo_ref[1])
        + mm(out_grad, into_out)
    )
    for s in range(seqs):
        for h in range(heads):
            dmix_ref[s * heads + h] = dheads[
                s * length : (s + 1) * length, h * width : (h + 1) * width
            ]
    loads["src"].wait()
    cube.each(cube.start)
    for name in ("reach", "start", "local", "map"):
        loads[name].wait()

    @pl.loop(0, seqs)
    def _(s):
        for h in range(heads):
            pair = s * heads + h
            mixed = mm(reach_ref[pair], start_ref[pair]) + local_ref[pair]
            dmix_ref[pair] = norm_back(mixed, gain, dmix_ref[pair])

    for name in ("ext", "rates", "wkey", "wval", "inv"):
        loads[name].wait()
    fetch("w", w_hbm, w_ref)
    fetch("back", back_hbm, back_ref)
    fetch("into", into_hbm, into_ref)
    fetch("x", x_hbm.at[mine], x_ref)
    fetch("gresid", gresid_hbm, gresid_ref)

    def hop_of(pair):
        return remote(
            chain_out.at[pair],
            after_ref.at[pair],
            chain_send.at[pair],
            chain_recv.at[pair],
            {"ctx": c - 1},
        )

    def link(s):
        for h in range(heads):
            pair = s * heads + h

            @pl.when(c == ctx_size - 1)
            def _(pair=pair):
                after_ref[pair] = jnp.zeros((width, width), bf16)

            @pl.when(c < ctx_size - 1)
            def _(pair=pair):
                hop_of(pair).wait_recv()

            @pl.when(c > 0)
            def _(pair=pair):
                chain_out[pair] = (
                    tm(map_ref[pair], after_ref[pair]) + tm(reach_ref[pair], dmix_ref[pair])
                ).astype(bf16)
                hop_of(pair).start()

    def unconvolve(s, kind):
        here = part_of(s, length)
        for h in range(heads):
            at = kind * cols + h * width
            total = None
            spill = None
            for j in range(CONV):
                tap = taps[j : j + 1, at : at + width]
                term = tap * gconv_ref[pl.ds(HALO + CONV - 1 - j, length), pl.ds(at, width)]
                edge = tap * gconv_ref[pl.ds(CONV - 1 - j, HALO), pl.ds(at, width)]
                total = term if total is None else total + term
                spill = edge if spill is None else spill + edge
            pre_ref[here, at : at + width] = total.astype(bf16)
            halo_out[0, s, :, at : at + width] = total[length - HALO :, :]
            halo_out[1, s, :, at : at + width] = spill

    def early(s):
        every = range(heads)
        at = [h * width for h in every]
        convs = [
            [convolved(ext_ref, taps, s, length, i * cols + at[h], width) for i in range(3)]
            for h in every
        ]
        starts_in = [start_ref[s * heads + h] for h in every]
        grads_in = [dmix_ref[s * heads + h] for h in every]
        wkeys = [wkey_ref[s * heads + h] for h in every]
        wvals = [wval_ref[s * heads + h] for h in every]
        fresh = [wval - mm(wkey, start) for wval, wkey, start in zip(wvals, wkeys, starts_in)]
        sigmas = [[jax.nn.sigmoid(a) for a in row] for row in convs]
        slopes = [
            [b * (1.0 + a * (1.0 - b)) for a, b in zip(row, sig)] for row, sig in zip(convs, sigmas)
        ]
        acts = [[a * b for a, b in zip(row, sig)] for row, sig in zip(convs, sigmas)]
        scales = [
            [lax.rsqrt(jnp.sum(a * a, axis=-1, keepdims=True) + EPS) for a in row[:2]] for row in acts
        ]
        query = [acts[h][0] * scales[h][0] for h in every]
        key = [acts[h][1] * scales[h][1] for h in every]
        lower = row_at >= col_at
        scores = [jnp.where(lower, finer(q, k, ((1,), (1,))), 0.0) for q, k in zip(query, key)]
        dscores = [
            jnp.where(lower, finer(g, v, ((1,), (1,))), 0.0) for g, v in zip(grads_in, fresh)
        ]
        dquery = [
            mt(g, start) + mm(d, k) for g, start, d, k in zip(grads_in, starts_in, dscores, key)
        ]
        dfresh = [tm(p, g) for p, g in zip(scores, grads_in)]
        dkeys = [tm(d, q) for d, q in zip(dscores, query)]
        along = [jnp.sum(q * g, axis=-1, keepdims=True) for q, g in zip(query, dquery)]
        for h in every:
            pair = s * heads + h
            keys_ref[pair] = key[h]
            slopes_ref[pair] = slopes[h][1] * scales[h][1]
            values_ref[pair] = acts[h][2]
            vslopes_ref[pair] = slopes[h][2]
            dfresh_ref[pair] = dfresh[h]
            dkeys_ref[pair] = dkeys[h]
            fresh_ref[pair] = fresh[h].astype(bf16)
            gconv_ref[pl.ds(HALO, length), pl.ds(at[h], width)] = (
                slopes[h][0] * scales[h][0] * (dquery[h] - query[h] * along[h])
            )
        unconvolve(s, 0)

    def late(s):
        every = range(heads)
        here = part_of(s, length)
        rate_block = rates_ref[here, :]
        lane = lax.broadcasted_iota(jnp.int32, (length, LANES), 1)
        rate = [column(rate_block, RATE_AT + h) for h in every]
        start = [start_ref[s * heads + h] for h in every]
        after = [after_ref[s * heads + h] for h in every]
        key = [keys_ref[s * heads + h] for h in every]
        fresh = [fresh_ref[s * heads + h] for h in every]
        before = [dfresh_ref[s * heads + h] for h in every]
        inverse = [inv_ref[s * heads + h] for h in every]
        dkeys = [dkeys_ref[s * heads + h] for h in every]
        values = [values_ref[s * heads + h] for h in every]
        keyed = [slopes_ref[s * heads + h] for h in every]
        valued = [vslopes_ref[s * heads + h] for h in every]
        low = [item.astype(bf16) for item in key]
        dfresh = [b + mm(k, a) for b, k, a in zip(before, low, after)]
        dvalue = [tm(inv, d) for inv, d in zip(inverse, dfresh)]
        dvalue_low = [item.astype(bf16) for item in dvalue]
        products = [mt(k, k) for k in low]
        outer = [mt(v, a) for v, a in zip(fresh, after)]
        dkey_in = [-mt(d, st) for d, st in zip(dvalue_low, start)]
        dstrict = [
            jnp.where(row_at > col_at, -mt(d, v), 0.0) for d, v in zip(dvalue_low, fresh)
        ]
        dprod = [(r * d).astype(bf16) for r, d in zip(rate, dstrict)]
        forth = [mm(d, k) for d, k in zip(dprod, low)]
        back = [tm(d, k) for d, k in zip(dprod, low)]
        dkey = [
            dkeys[h] + outer[h] + rate[h] * dkey_in[h] + forth[h] + back[h] for h in every
        ]
        drate = [
            jnp.sum(
                dstrict[h] * products[h] + dvalue[h] * values[h] + dkey_in[h] * key[h],
                axis=-1,
                keepdims=True,
            )
            for h in every
        ]
        along = [jnp.sum(k * d, axis=-1, keepdims=True) for k, d in zip(key, dkey)]
        rate_grads = jnp.zeros((length, LANES), f32)
        for h in every:
            at = h * width
            gconv_ref[pl.ds(HALO, length), pl.ds(cols + at, width)] = keyed[h] * (
                dkey[h] - key[h] * along[h]
            )
            gconv_ref[pl.ds(HALO, length), pl.ds(2 * cols + at, width)] = (
                rate[h] * dvalue[h] * valued[h]
            )
            rate_grads = rate_grads + jnp.where(
                lane == RATE_AT + h, drate[h] * rate[h] * (1.0 - rate[h]), 0.0
            )
        unconvolve(s, 1)
        unconvolve(s, 2)
        pre_ref[here, 3 * cols :] = rate_grads.astype(bf16)

    ends = c == ctx_size - 1
    starts = c == 0
    inside = (c > 0) & (c < ctx_size - 1)
    begins = (ctx_size - 1 - c) // (ctx_size - 1)

    final = c // (ctx_size - 1)
    block_store = pltpu.make_async_copy(out_ref, block_hbm, store_sem.at[0])

    def halo_of(s):
        return remote(
            halo_in.at[1, s], halo_in.at[0, s], halo_send.at[s], halo_recv.at[s], {"ctx": c - 1}
        )

    def project(i):
        s = cube2.block_at(i)
        here = part_of(s, length)

        @pl.when(c < ctx_size - 1)
        def _():
            halo_of(s).wait_recv()
            last = pl.ds(pl.multiple_of(s * length + length - 16, 16), 16)
            rows = pre_ref[last, : 3 * cols].astype(f32)
            edge = halo_out[0, s] + halo_in[0, s].astype(f32)
            pre_ref[last, : 3 * cols] = jnp.concatenate([rows[:HALO], edge], axis=0).astype(bf16)

        @pl.when(i == 0)
        def _():
            for name in ("w", "back", "into"):
                loads[name].wait()

        part = mm(pre_ref[here, 3 * cols :], into_ref[...])
        for kind in range(3):
            part = part + mt(pre_ref[here, kind * cols : (kind + 1) * cols], w_ref[kind])
        src2[here, :] = part.astype(bf16)
        tail2_src[here, :] = (SCALE * mt(pre_ref[here, :], back_ref[...])).astype(bf16)
        cube2.send_block(i)

        @pl.when(i < 3)
        def _():
            tail2.send_block(s)

        @pl.when(i == 1)
        def _():
            cube.done()
            block_store.start()

        @pl.when(i == 2)
        def _():
            block_store.wait()
            cube2.middle_half(1)

        @pl.when(i == 3)
        def _():
            cube2.middle_half(0)

    @pl.loop(0, 3 * seqs + 2)
    def _(k):
        part = k // seqs
        odd = lax.rem(k, 2) == seqs % 2
        s = cube2.block_at(lax.rem(k, seqs))
        later = cube2.block_at(
            (1 - begins) * lax.rem(k, seqs) + begins * lax.rem((k + seqs) // 2, seqs)
        )
        ready = (1 - begins) * (k - 2 * seqs - 1) + begins * ((k + seqs - 3) // 2 - seqs)

        @pl.when(k == 2 + 3 * final)
        def _():
            cube.middle()

        @pl.when(k == 4 + 3 * final)
        def _():
            cube.finish(total_ref)
            loads["resid"].wait()
            inner = tail.total().astype(bf16)
            right = stacked([wide_ref[core, 7] for core in range(2)])
            rows = resid_ref[...] + total_ref[...] + SCALE * mm(inner, right)
            out_ref[mine, :] = (kept(lens_ref, t, c, length) * rows).astype(bf16)
            down_inner_ref[mine, :] = inner
            cube.spread()
            tail.start(1)

        @pl.when(k == 6 + 2 * final)
        def _():
            cube.relay()

        @pl.when((ends & (part == 1)) | ((starts | inside) & (part == 0)))
        def _():
            early(s)

        @pl.when(
            (ends & (part == 0)) | (inside & (part == 1)) | (starts & (part > 0) & (part < 3) & odd)
        )
        def _():
            link(later)

        @pl.when(
            ((ends | inside) & (part == 2))
            | (starts & (part > 0) & (part < 3) & jnp.logical_not(odd))
        )
        def _():
            late(later)
            halo_in[1, later] = halo_out[1, later].astype(bf16)

            @pl.when(c > 0)
            def _():
                halo_of(later).start()

        @pl.when(
            ((ends | inside) & (k > 2 * seqs) & (k < 3 * seqs + 1))
            | (starts & (k > seqs + 2) & jnp.logical_not(odd))
        )
        def _():
            project(ready)


    @pl.when(c > 0)
    def _():
        @pl.loop(0, seqs)
        def _(s):
            halo_of(s).wait_send()

        @pl.loop(0, pairs)
        def _(pair):
            hop_of(pair).wait_send()

    inner = tail2.total().astype(bf16)
    inner_grad_ref[mine, :] = inner
    tail2.start(1)
    loads["n2"].wait()
    feed_left = tm(feed_grad_ref[...], normed_ref[...])
    fetch("n1", n1_hbm, normed_ref)
    pack[:, :, used:] = jnp.zeros((2, 8, pack.shape[2] - used), bf16)
    loads["heads"].wait()
    out_left = tm(out_grad, heads_ref[...])
    out_right = SCALE * tm(out_inner_ref[...], low_ref[...])
    right = SCALE * tm(inner_ref[...], pre_ref[...])
    tail.wait(1)
    masked = jnp.concatenate(
        [
            kept(lens_ref, s, c, length) * down_inner_ref[s * length : (s + 1) * length, :].astype(f32)
            for s in range(seqs)
        ],
        axis=0,
    )
    loads["grad"].wait()
    down_right = SCALE * tm(masked, grad_ref[...])
    for core in range(2):
        at = core * 8
        put("ol", core, out_left[at : at + 8])
        put("or", core, out_right[at : at + 8])
        put("dr", core, down_right[at : at + 8])
        put("dl", core, down_left_ref[at : at + 8, :])
        at = core * 16
        put("gl", core, feed_left[at : at + 8])
        put("ul", core, feed_left[at + 8 : at + 16])
        put("gr", core, gate_right_ref[at : at + 8, :])
        put("ur", core, up_right_ref[at + 8 : at + 16, :])
        for kind, name in enumerate(("qr", "kr", "vr", "rr")):
            at = core * 32 + kind * 8
            put(name, core, right[at : at + 8, kind * cols : kind * cols + plan[name][1]])
    loads["n1"].wait()
    tail2.wait(1)
    left = tm(inner_grad_ref[...], normed_ref[...])
    for core in range(2):
        for kind, name in enumerate(("ql", "kl", "vl", "rl")):
            at = core * 32 + kind * 8
            put(name, core, left[at : at + 8])
    swap = remote(pack.at[1 - f], mate_in, swap_send, swap_recv, mate)
    swap.start()
    cube2.finish(total_ref)
    loads["x"].wait()
    loads["gresid"].wait()
    grad_first = total_ref[...] + mm(inner, into_ref[...])
    grad = gresid_ref[...] + norm_back(x_ref[...].astype(f32), gain_ref[...], grad_first)
    out_ref[mine, :] = grad.astype(bf16)
    cube2.spread()
    swap.wait_recv()
    both = (pack[f].astype(f32) + mate_in[...].astype(f32)).astype(bf16)
    piece = both.shape[1] // ctx_size
    for j in range(ctx_size):
        mine_ref[j] = both[:, j * piece : (j + 1) * piece]
    sends = []
    spreads = []
    for i in range(ctx_size - 1):
        peer = {"ctx": lax.rem(c + 1 + i, ctx_size)}
        back = ctx_size - 2 - i
        sends.append(
            remote(
                mine_ref.at[lax.rem(c + 1 + i, ctx_size)],
                got.at[back],
                part_send.at[0, i],
                part_recv.at[0, back],
                peer,
            )
        )
        spreads.append(
            remote(summed.at[c], summed.at[c], part_send.at[1, i], part_recv.at[1, back], peer)
        )
    for copy in sends:
        copy.start()
    cube2.relay()
    for copy in sends:
        copy.wait_recv()
    total = mine_ref[c].astype(f32)
    for i in range(ctx_size - 1):
        total = total + got[i].astype(f32)
    summed[c] = total.astype(bf16)
    for copy in spreads:
        copy.start()
    for copy in spreads:
        copy.wait_recv()
    for j in range(ctx_size):
        packed_ref[:, j * piece : (j + 1) * piece] = summed[j].astype(f32)
    cube2.done()
    grad_store = pltpu.make_async_copy(out_ref, input_grad_hbm, store_sem.at[1])
    grad_store.start()
    swap.wait_send()
    for copy in sends + spreads:
        copy.wait_send()
    tail.done()
    tail2.done()
    grad_store.wait()


def deal_kernel(strips, heads, packed_ref, block_in, grad_in, block_out, grad_out, *refs):
    outs, (block_ref, grad_ref, load_sem, store_sem) = refs[:-4], refs[-4:]
    count = load_sem.shape[1]
    size = block_ref.shape[0] // count
    moves = []
    for i, (source, middle, target) in enumerate(
        ((block_in, block_ref, block_out), (grad_in, grad_ref, grad_out))
    ):
        for k in range(count):
            here = pl.ds(k * size, size)
            load = pltpu.make_async_copy(source.at[here], middle.at[here], load_sem.at[i, k])
            load.start()
            moves.append(
                (load, pltpu.make_async_copy(middle.at[here], target.at[here], store_sem.at[i, k]))
            )
    for load, store in moves:
        load.wait()
        store.start()
    for index, (out, (at, wide)) in enumerate(zip(outs, strips)):
        if index == 7:
            lanes = lax.broadcasted_iota(jnp.int32, (heads, LANES), 1)
            rows = lax.broadcasted_iota(jnp.int32, (heads, LANES), 0)
            pick = jnp.where(lanes == rows + RATE_AT, 1.0, 0.0)
            out[...] = mt(pick, packed_ref[:, at : at + wide])
        else:
            out[...] = packed_ref[:, at : at + wide]
    for _, store in moves:
        store.wait()


def local(ctx_size, tp_size, *arguments):
    (
        hidden_in,
        seq_lengths,
        mixer_gain,
        feed_gain,
        query_weight,
        key_weight,
        value_weight,
        rate_weight,
        query_conv,
        key_conv,
        value_conv,
        head_gain,
        output_weight,
        gate_weight,
        up_weight,
        down_weight,
        query_left,
        query_right,
        key_left,
        key_right,
        value_left,
        value_right,
        rate_left,
        rate_right,
        output_left,
        output_right,
        gate_left,
        gate_right,
        up_left,
        up_right,
        down_left,
        down_right,
        output_grad,
    ) = arguments
    seqs, length, model = hidden_in.shape
    heads = rate_weight.shape[1]
    width = head_gain.shape[0]
    cols = heads * width
    rows = seqs * length
    units = gate_weight.shape[1]
    half = query_weight.shape[0]
    pairs = seqs * heads
    x = hidden_in.reshape(rows, model)
    grad_rows = output_grad.reshape(rows, model)
    rate_from = jnp.pad(rate_right, ((0, 0), (RATE_AT, LANES - RATE_AT - heads)))
    rate_rows = rate_weight.T
    wides = (
        query_left.T,
        key_left.T,
        value_left.T,
        rate_left.T,
        gate_left.T,
        up_left.T,
        output_right,
        down_right,
    )
    slims = (
        query_right,
        key_right,
        value_right,
        rate_from,
        output_left.T,
        gate_right,
        up_right,
        down_left.T,
    )
    slim_wide = sum(item.shape[1] for item in slims)
    gain1, gain2, gain3 = mixer_gain[None, :], feed_gain[None, :], head_gain[None, :]
    ext = length + HALO
    square = (pairs, width, width)
    tall = (pairs, length, width)
    block = rows // tp_size
    smem = pl.BlockSpec(memory_space=pltpu.SMEM)
    mixer_sizes = (seqs, length, heads, width, ctx_size, tp_size)
    kept_shapes = (
        shape((rows, model), bf16),
        shape((2, 8, 8, model), bf16),
        shape((2, 8, slim_wide), bf16),
        shape((LANES, model), bf16),
        shape((LANES, 3 * cols + LANES), bf16),
        shape((seqs, ext, 3 * cols), f32),
        shape((rows, LANES), bf16),
        shape((rows, LANES), f32),
        shape((pairs, length, length), bf16),
        shape(tall, bf16),
        shape(tall, f32),
        shape(tall, bf16),
        shape(tall, f32),
        shape(square, bf16),
        shape((rows, cols), bf16),
        shape(square, bf16),
        shape((rows, units), f32),
        shape((rows, LANES), bf16),
    )
    (
        second,
        out_inner,
        residual,
        wo,
        wg,
        wu,
        wd,
        wqkv,
        n1,
        wide_all,
        slim_all,
        into,
        back,
        pre_ext,
        inner,
        rates,
        inverse,
        wkey,
        wval,
        reach,
        local_out,
        step_map,
        heads_low,
        start,
        active,
        down_grad,
    ) = pl.pallas_call(
        functools.partial(mixer_kernel, mixer_sizes),
        out_shape=(
            shape((rows, model), bf16),
            shape((rows, LANES), bf16),
            shape((block, model), f32),
            shape(output_weight.shape, bf16),
            shape(gate_weight.shape, bf16),
            shape(up_weight.shape, bf16),
            shape(down_weight.shape, bf16),
            shape((3, model, cols), bf16),
        )
        + kept_shapes,
        in_specs=[smem] + [VMEM] * 7 + [ANY] * 25,
        out_specs=(VMEM,) * 3 + (ANY,) * (5 + len(kept_shapes)),
        scratch_shapes=[pltpu.VMEM(item.shape, item.dtype) for item in kept_shapes]
        + [
            pltpu.VMEM(square, f32),
            pltpu.VMEM((3, model, cols), bf16),
            pltpu.VMEM((heads, model), bf16),
            pltpu.VMEM((seqs, HALO, 3 * cols), bf16),
            pltpu.VMEM((seqs, HALO, 3 * cols), bf16),
            pltpu.VMEM((LANES, 3 * cols + LANES), f32),
            pltpu.VMEM((LANES, model), f32),
            pltpu.VMEM(square, bf16),
            pltpu.VMEM((2,) + output_weight.shape, bf16),
            pltpu.VMEM((2,) + down_weight.shape, bf16),
            pltpu.VMEM((rows, model), bf16),
            DMA((24,)),
            DMA((24,)),
            DMA((20,)),
            DMA((20,)),
            DMA((seqs,)),
            DMA((seqs,)),
            DMA((4,)),
            DMA,
            DMA((pairs,)),
            DMA((pairs,)),
        ]
        + cube_scratch(rows, model)
        + tail_scratch(rows, tp_size),
        compiler_params=params(0),
        name="mixer",
    )(
        seq_lengths,
        x,
        gain1,
        gain2,
        gain3,
        query_conv,
        key_conv,
        value_conv,
        query_weight,
        key_weight,
        value_weight,
        rate_rows,
        *wides,
        *slims,
        output_weight,
        gate_weight,
        up_weight,
        down_weight,
        grad_rows,
    )
    (
        resid_low,
        feed_grad,
        grad_residual,
        down_part,
        down_tail,
        gate_right_grad,
        up_right_grad,
        down_left_grad,
    ) = pl.pallas_call(
        functools.partial(feed_kernel, (seqs, length, cols, ctx_size, tp_size)),
        out_shape=(
            shape((rows, model), bf16),
            shape((rows, LANES), bf16),
            shape((block, model), f32),
            shape((rows, model), bf16),
            shape((rows, LANES), bf16),
            shape((32, units), f32),
            shape((32, units), f32),
            shape((32, units), f32),
        ),
        in_specs=[smem] + [VMEM] * 5 + [ANY] * 9,
        out_specs=(VMEM, VMEM, ANY, ANY) + (VMEM,) * 4,
        scratch_shapes=[
            pltpu.VMEM((2,) + gate_weight.shape, bf16),
            pltpu.VMEM((2,) + up_weight.shape, bf16),
            pltpu.VMEM((2,) + down_weight.shape, bf16),
            pltpu.VMEM((rows, units), bf16),
            pltpu.VMEM((rows, units), bf16),
            pltpu.VMEM((rows, units), bf16),
            pltpu.VMEM((rows, LANES), bf16),
            pltpu.VMEM((LANES, units), bf16),
            pltpu.VMEM((LANES, units), bf16),
            pltpu.VMEM((block, model), bf16),
            pltpu.VMEM((rows, units), f32),
            pltpu.VMEM((block, model), f32),
            pltpu.VMEM((block, model), f32),
            pltpu.VMEM((rows, model), bf16),
            DMA((3,)),
            DMA((-(-units // (2 * LANES)), 5)),
            DMA((2,)),
            DMA,
        ]
        + cube_scratch(rows, model)
        + tail_scratch(rows, tp_size),
        compiler_params=params(2),
        name="feed",
    )(
        seq_lengths,
        second,
        gain2,
        wide_all,
        slim_all,
        down_grad,
        grad_rows,
        gate_weight,
        wg,
        up_weight,
        wu,
        down_weight,
        wd,
        active,
        residual,
    )
    plan, used = strip_plan(cols, model, units)
    grain = LANES * ctx_size
    total_wide = -(-used // grain) * grain
    piece = total_wide // ctx_size
    block_out, input_grad, packed = pl.pallas_call(
        functools.partial(back_kernel, mixer_sizes),
        out_shape=(
            shape((rows, model), bf16),
            shape((rows, model), bf16),
            shape((8, total_wide), f32),
        ),
        in_specs=[smem] + [VMEM] * 15 + [ANY] * 22,
        out_specs=(ANY, ANY, VMEM),
        scratch_shapes=[
            pltpu.VMEM(square, bf16),
            pltpu.VMEM(square, bf16),
            pltpu.VMEM(tall, bf16),
            pltpu.VMEM(tall, f32),
            pltpu.VMEM((pairs, length, length), bf16),
            pltpu.VMEM(tall, bf16),
            pltpu.VMEM(tall, f32),
            pltpu.VMEM((seqs, ext, 3 * cols), f32),
            pltpu.VMEM((rows, LANES), f32),
            pltpu.VMEM((rows, cols), bf16),
            pltpu.VMEM((rows, model), bf16),
            pltpu.VMEM((block, model), f32),
            pltpu.VMEM((rows, model), bf16),
            pltpu.VMEM((rows, model), bf16),
            pltpu.VMEM((block, model), bf16),
            pltpu.VMEM((block, model), f32),
            pltpu.VMEM((3, model, cols), bf16),
            pltpu.VMEM((LANES, 3 * cols + LANES), bf16),
            pltpu.VMEM((LANES, model), bf16),
            pltpu.VMEM((2,) + output_weight.shape, bf16),
            pltpu.VMEM((rows, model), bf16),
            pltpu.VMEM((rows, 3 * cols + LANES), bf16),
            pltpu.VMEM(tall, f32),
            pltpu.VMEM(square, bf16),
            pltpu.VMEM(square, bf16),
            pltpu.VMEM((HALO + length + HALO, 3 * cols), f32),
            pltpu.VMEM((2, seqs, HALO, 3 * cols), f32),
            pltpu.VMEM((2, seqs, HALO, 3 * cols), bf16),
            pltpu.VMEM((rows, LANES), bf16),
            pltpu.VMEM(tall, f32),
            pltpu.VMEM(tall, f32),
            pltpu.VMEM(tall, f32),
            pltpu.VMEM(tall, f32),
            pltpu.VMEM(tall, f32),
            pltpu.VMEM(tall, f32),
            pltpu.VMEM(tall, bf16),
            pltpu.VMEM((rows, LANES), bf16),
            pltpu.VMEM((rows, LANES), bf16),
            pltpu.VMEM((2, 8, total_wide), bf16),
            pltpu.VMEM((8, total_wide), bf16),
            pltpu.VMEM((ctx_size, 8, piece), bf16),
            pltpu.VMEM((ctx_size - 1, 8, piece), bf16),
            pltpu.VMEM((ctx_size, 8, piece), bf16),
            DMA((BACK_LOADS,)),
            DMA((2,)),
            DMA((pairs,)),
            DMA((pairs,)),
            DMA((seqs,)),
            DMA((seqs,)),
            DMA,
            DMA,
            DMA((2, ctx_size - 1)),
            DMA((2, ctx_size - 1)),
        ]
        + cube_scratch(rows, model)[1:]
        + [DMA((4, 2, CHUNKS, 2)), DMA((4, 2, CHUNKS, 2))]
        + cube_scratch(rows, model)[:4]
        + tail_scratch(rows, tp_size)[1:] * 2,
        compiler_params=params(3, 60 << 20),
        name="back",
    )(
        seq_lengths,
        resid_low,
        gain3,
        gain1,
        query_conv,
        key_conv,
        value_conv,
        wide_all,
        slim_all,
        down_tail,
        feed_grad,
        out_inner,
        inner,
        gate_right_grad,
        up_right_grad,
        down_left_grad,
        start,
        step_map,
        reach,
        local_out,
        inverse,
        wkey,
        wval,
        pre_ext,
        rates,
        heads_low,
        down_part,
        residual,
        grad_rows,
        second,
        n1,
        x,
        grad_residual,
        wqkv,
        back,
        into,
        output_weight,
        wo,
    )
    strips = tuple(plan.values())
    dealt = pl.pallas_call(
        functools.partial(deal_kernel, strips, heads),
        out_shape=(shape((rows, model), bf16),) * 2
        + tuple(
            shape((heads, 8) if i == 7 else (8, wide), f32) for i, (_, wide) in enumerate(strips)
        ),
        in_specs=[VMEM, ANY, ANY],
        out_specs=(ANY, ANY) + (VMEM,) * len(strips),
        scratch_shapes=[
            pltpu.VMEM((rows, model), bf16),
            pltpu.VMEM((rows, model), bf16),
            DMA((2, 4)),
            DMA((2, 4)),
        ],
        name="deal",
    )(packed, block_out, input_grad)
    block_out, input_grad = dealt[:2]
    shares = list(dealt[2:])
    lefts = (0, 2, 4, 6, 7, 8, 10, 12, 14)
    shares = [item.T if i in lefts else item for i, item in enumerate(shares)]
    return (
        block_out.reshape(seqs, length, model),
        input_grad.reshape(seqs, length, model),
    ) + tuple(shares)


def solution(mesh):
    placed = (
        P("fsdp", "ctx", None),
        P("fsdp"),
        P(),
        P(),
        P("fsdp", "tp"),
        P("fsdp", "tp"),
        P("fsdp", "tp"),
        P("fsdp", "tp"),
        P(None, "tp"),
        P(None, "tp"),
        P(None, "tp"),
        P(),
        P("tp", "fsdp"),
        P("fsdp", "tp"),
        P("fsdp", "tp"),
        P("tp", "fsdp"),
    )
    left_in, left_over, right_over, right_in = (
        P(None, "fsdp"),
        P("tp", "fsdp"),
        P("fsdp", None),
        P("fsdp", "tp"),
    )
    adapters = (left_in, right_in) * 4 + (left_over, right_over) + (left_in, right_in) * 2 + (
        left_over,
        right_over,
    )
    rows = P("fsdp", "ctx", None)
    return jax.shard_map(
        functools.partial(local, mesh.shape["ctx"], mesh.shape["tp"]),
        mesh=mesh,
        in_specs=placed + adapters + (rows,),
        out_specs=(rows, rows) + adapters,
        check_vma=False,
    )
```

```python
import functools

import jax
import jax.numpy as jnp
from jax import lax
from jax.experimental import pallas as pl
from jax.experimental.pallas import tpu as pltpu
from jax.sharding import PartitionSpec as P

MESH = pl.DeviceIdType.MESH
ANY = pl.BlockSpec(memory_space=pl.ANY)
VMEM = pl.BlockSpec(memory_space=pltpu.VMEM)
DMA = pltpu.SemaphoreType.DMA
f32, bf16 = jnp.float32, jnp.bfloat16

CONV = 4
SCALE = 0.5
EPS = 1e-06
LANES = 128
RATE_AT = 64
HALO = 8


def shape(dims, kind):
    return jax.ShapeDtypeStruct(tuple(dims), kind)


def product(left, right, dims):
    return lax.dot_general(
        left.astype(bf16), right.astype(bf16), (dims, ((), ())), preferred_element_type=f32
    )


def mm(left, right):
    return product(left, right, ((1,), (0,)))


def mt(left, right):
    return product(left, right, ((1,), (1,)))


def tm(left, right):
    return product(left, right, ((0,), (0,)))


def params(collective, limit=58 << 20):
    return pltpu.CompilerParams(
        collective_id=collective, has_side_effects=True, vmem_limit_bytes=limit
    )


def grid_of(size):
    rows = lax.broadcasted_iota(jnp.int32, (size, size), 0)
    cols = lax.broadcasted_iota(jnp.int32, (size, size), 1)
    return rows, cols


def halves(values):
    high = values.astype(bf16)
    return high, (values - high.astype(f32)).astype(bf16)


def finer(left, right, dims):
    lhigh, llow = halves(left)
    rhigh, rlow = halves(right)
    (la,), (ra,) = dims
    return lax.dot_general(
        jnp.concatenate([lhigh, llow, lhigh], axis=la),
        jnp.concatenate([rhigh, rhigh, rlow], axis=ra),
        (dims, ((), ())),
        preferred_element_type=f32,
    )


def unit_inverses(stricts):
    size = stricts[0].shape[0]
    rows, cols = grid_of(size)
    eye = jnp.where(rows == cols, 1.0, 0.0)
    found = [eye - jnp.where((rows >> 1) == (cols >> 1), item, 0.0) for item in stricts]
    level = 1
    while (1 << level) < size:
        joined = ((rows >> (level + 1)) == (cols >> (level + 1))) & ((rows >> level) != (cols >> level))
        lows = [item.astype(bf16) for item in found]
        inner = [mm(jnp.where(joined, item, 0.0), low) for item, low in zip(stricts, lows)]
        found = [item - mm(low, part) for item, low, part in zip(found, lows, inner)]
        level += 1
    lows = [item.astype(bf16) for item in found]
    errors = []
    for item, low in zip(stricts, lows):
        pair = jnp.concatenate(halves(item), axis=1)
        errors.append(eye - low.astype(f32) - mm(pair, jnp.concatenate([low, low], axis=0)))
    return [low.astype(f32) + mm(low, error) for low, error in zip(lows, errors)]


def normed(values, gain):
    return values * lax.rsqrt(jnp.mean(values * values, axis=-1, keepdims=True) + EPS) * gain


def norm_back(values, gain, grad):
    scale = lax.rsqrt(jnp.mean(values * values, axis=-1, keepdims=True) + EPS)
    weighted = gain * grad
    return scale * weighted - values * (scale * scale * scale) * jnp.mean(
        values * weighted, axis=-1, keepdims=True
    )


def greet(barrier, peers, later=(), expected=0):
    count = expected
    for peer, condition in list(peers) + list(later):

        def tell(peer=peer):
            pl.semaphore_signal(barrier, inc=1, device_id=peer, device_id_type=MESH)

        if condition is None:
            tell()
        else:
            pl.when(condition)(tell)
    for peer, condition in peers:
        count = count + (1 if condition is None else jnp.where(condition, 1, 0))
    pl.semaphore_wait(barrier, count)


def remote(source, target, send_sem, recv_sem, peer):
    return pltpu.make_async_remote_copy(
        src_ref=source,
        dst_ref=target,
        send_sem=send_sem,
        recv_sem=recv_sem,
        device_id=peer,
        device_id_type=MESH,
    )


def column(block, lane):
    return block[:, lane : lane + 1]


def convolved(ext_ref, taps, s, length, at, width):
    total = None
    for i in range(CONV):
        rows = ext_ref[s, pl.ds(HALO - (CONV - 1) + i, length), pl.ds(at, width)]
        term = taps[i : i + 1, at : at + width] * rows
        total = term if total is None else total + term
    return total


def kept(lens_ref, s, c, length):
    place = c * length + lax.broadcasted_iota(jnp.int32, (length, 1), 0)
    return jnp.where(place < lens_ref[s], 1.0, 0.0)


def part_of(at, size):
    return pl.ds(pl.multiple_of(at * size, size), size)


class Cube:
    def __init__(self, t, src, out, first, second, held, send_sem, recv_sem, chunks):
        self.y, self.x = t // 2, lax.rem(t, 2)
        self.t, self.src, self.out = t, src, out
        self.first, self.second, self.held = first, second, held
        self.send_sem, self.recv_sem = send_sem, recv_sem
        self.chunks = chunks
        self.block = src.shape[0] // 4
        self.half_width = src.shape[1] // 2
        self.width = self.half_width // chunks
        self.beside = self.y * 2 + (1 - self.x)
        self.above = (1 - self.y) * 2 + self.x

    def peer(self, side):
        return {"tp": self.beside * (1 - side) + self.above * side}

    def columns(self, half, chunk):
        return pl.ds(
            pl.multiple_of(half * self.half_width + chunk * self.width, self.width), self.width
        )

    def copy(self, stage, half, chunk, j):
        wide = self.columns(half, chunk)
        slim = part_of(chunk, self.width)
        send, recv = self.send_sem.at[stage, half, chunk, j], self.recv_sem.at[stage, half, chunk, j]
        across = self.above * (1 - half) + self.beside * half
        if stage == 0:
            g = (1 - half) * (2 * j + 1 - self.x) + half * (2 * (1 - self.y) + j)
            source, target = self.src.at[part_of(g, self.block), wide], self.first.at[half, j, :, slim]
            side = half
        elif stage == 1:
            source, target = self.held.at[half, :, slim], self.second.at[half, :, slim]
            side = 1 - half
        else:
            g = self.t if j == 0 else across
            source = target = self.out.at[part_of(g, self.block), wide]
            side = 1 - half if stage == 2 else half
        return remote(source, target, send, recv, self.peer(side))

    def each(self, body):
        @pl.loop(0, 2 * self.chunks)
        def _(k):
            body(lax.rem(k, 2), k // 2)

    def start(self, half, chunk):
        self.copy(0, half, chunk, 0).start()
        self.copy(0, half, chunk, 1).start()

    def block_at(self, i):
        flip_x, flip_y = (3 - i) // 2, lax.rem(i + 1, 2)
        y = self.y + flip_y * (1 - 2 * self.y)
        return y * 2 + self.x + flip_x * (1 - 2 * self.x)

    def send_block(self, i):
        def go(half, j):
            for chunk in range(self.chunks):
                self.copy(0, half, chunk, j).start()

        @pl.when(i == 0)
        def _():
            go(0, 1 - self.y)
            go(1, 1 - self.x)

        @pl.when(i == 1)
        def _():
            go(0, self.y)

        @pl.when(i == 2)
        def _():
            go(1, self.x)

    def pass_on(self, half, chunk):
        wide = self.columns(half, chunk)
        slim = part_of(chunk, self.width)
        across = self.above * (1 - half) + self.beside * half
        other = (1 - half) * (1 - self.y) + half * (1 - self.x)
        self.copy(0, half, chunk, other).wait_recv()
        self.held[half, :, slim] = (
            self.src[part_of(across, self.block), wide].astype(f32)
            + self.first[half, other, :, slim].astype(f32)
        ).astype(bf16)
        self.copy(1, half, chunk, 0).start()

    def middle(self):
        self.each(self.pass_on)

    def middle_half(self, half):
        @pl.loop(0, self.chunks)
        def _(chunk):
            self.pass_on(half, chunk)

    def finish(self, total_ref):
        def body(half, chunk):
            wide = self.columns(half, chunk)
            slim = part_of(chunk, self.width)
            mine = (1 - half) * self.y + half * self.x
            self.copy(0, half, chunk, mine).wait_recv()
            self.copy(1, half, chunk, 0).wait_recv()
            total_ref[:, wide] = (
                self.src[part_of(self.t, self.block), wide].astype(f32)
                + self.first[half, mine, :, slim].astype(f32)
                + self.second[half, :, slim].astype(f32)
            )

        self.each(body)

    def spread(self):
        def body(half, chunk):
            self.copy(2, half, chunk, 0).start()
            self.copy(3, half, chunk, 0).start()

        self.each(body)

    def relay(self):
        def body(half, chunk):
            self.copy(2, half, chunk, 0).wait_recv()
            self.copy(3, half, chunk, 1).start()

        self.each(body)

    def first_sent(self):
        def body(half, chunk):
            for j in range(2):
                self.copy(0, half, chunk, j).wait_send()

        self.each(body)

    def done(self, since=0):
        def body(half, chunk):
            for j in range(2):
                self.copy(3, half, chunk, j).wait_recv()
            for stage in range(since, 4):
                for j in range(2 if stage in (0, 3) else 1):
                    self.copy(stage, half, chunk, j).wait_send()

        self.each(body)


class Tail:
    def __init__(self, t, src, out, got, send_sem, recv_sem, size):
        self.t, self.src, self.out, self.got, self.size = t, src, out, got, size
        self.send_sem, self.recv_sem = send_sem, recv_sem
        self.block = src.shape[0] // size

    def copies(self, stage):
        found = []
        for i in range(self.size - 1):
            g = lax.rem(self.t + 1 + i, self.size)
            if stage == 0:
                source, target = self.src.at[part_of(g, self.block)], self.got.at[self.size - 2 - i]
            else:
                source = target = self.out.at[part_of(self.t, self.block)]
            found.append(
                remote(
                    source,
                    target,
                    self.send_sem.at[stage, i],
                    self.recv_sem.at[stage, self.size - 2 - i],
                    {"tp": g},
                )
            )
        return found

    def start(self, stage):
        for copy in self.copies(stage):
            copy.start()

    def send_block(self, g):
        i = lax.rem(g - self.t - 1 + self.size, self.size)
        back = self.size - 2 - i
        remote(
            self.src.at[part_of(g, self.block)],
            self.got.at[back],
            self.send_sem.at[0, i],
            self.recv_sem.at[0, back],
            {"tp": g},
        ).start()

    def wait(self, stage):
        for copy in self.copies(stage):
            copy.wait_recv()

    def total(self):
        self.wait(0)
        total = self.src[part_of(self.t, self.block), :].astype(f32)
        for i in range(self.size - 1):
            total = total + self.got[i].astype(f32)
        return total

    def done(self):
        for stage in range(2):
            for copy in self.copies(stage):
                copy.wait_send()


CHUNKS = 4


def cube_scratch(rows, model):
    block = rows // 4
    return [
        pltpu.VMEM((rows, model), bf16),
        pltpu.VMEM((2, 2, block, model // 2), bf16),
        pltpu.VMEM((2, block, model // 2), bf16),
        pltpu.VMEM((2, block, model // 2), bf16),
        pltpu.VMEM((block, model), f32),
        DMA((4, 2, CHUNKS, 2)),
        DMA((4, 2, CHUNKS, 2)),
    ]


def tail_scratch(rows, size):
    return [
        pltpu.VMEM((rows, LANES), bf16),
        pltpu.VMEM((size - 1, rows // size, LANES), bf16),
        DMA((2, size - 1)),
        DMA((2, size - 1)),
    ]


def tp_peers(t, size):
    return [({"tp": lax.rem(t + 1 + i, size)}, None) for i in range(size - 1)]


def stacked(pieces):
    rows = sum(piece.shape[0] for piece in pieces)
    fill = jnp.zeros((LANES - rows, pieces[0].shape[1]), f32)
    return jnp.concatenate([piece.astype(f32) for piece in pieces] + [fill], axis=0).astype(bf16)


def slot_loads(pairs, f, sems):
    loads = []
    for i, (own, other, scratch) in enumerate(pairs):
        loads.append(pltpu.make_async_copy(own, scratch.at[f], sems.at[i, 0]))
        loads.append(pltpu.make_async_copy(other, scratch.at[1 - f], sems.at[i, 1]))
    for load in loads:
        load.start()
    return loads


def unit_steps(units, body):
    step = 2 * LANES
    whole = units // step

    @pl.loop(0, whole)
    def _(k):
        body(part_of(k, step))

    if units % step:
        body(pl.ds(whole * step, units % step))


def mixer_kernel(
    sizes,
    lens_ref,
    x_ref,
    gain_ref,
    gain2_ref,
    head_gain_ref,
    qtaps_ref,
    ktaps_ref,
    vtaps_ref,
    rate_from_ref,
    wq_ref,
    wk_ref,
    wv_ref,
    wr_ref,
    wide0,
    wide1,
    wide2,
    wide3,
    wide4,
    wide5,
    wide6,
    wide7,
    slim0,
    slim1,
    slim2,
    slim4,
    slim5,
    slim6,
    slim7,
    wo_own,
    wg_own,
    wu_own,
    wd_own,
    grad_hbm,
    n2_ref,
    out_inner_ref,
    resid_ref,
    wo_other,
    wg_other,
    wu_other,
    wd_other,
    wqkv_out,
    n1_out,
    wide_hbm,
    slim_hbm,
    into_out,
    back_out,
    ext_out,
    inner_out,
    rates_out,
    inv_out,
    wkey_out,
    wval_out,
    reach_out,
    local_out,
    map_out,
    heads_out,
    start_out,
    active_out,
    down_inner_out,
    n1_ref,
    wide_out,
    slim_out,
    into_ref,
    back_ref,
    ext_ref,
    inner_ref,
    rates_ref,
    inv_ref,
    wkey_ref,
    wval_ref,
    reach_ref,
    local_ref,
    map_ref,
    heads_ref,
    start_ref,
    active_ref,
    down_inner_ref,
    end_ref,
    w_ref,
    wr_all,
    halo_out,
    halo_in,
    back_f32,
    into_f32,
    chain_out,
    wo_ref,
    wd_ref,
    grad_ref,
    slim3,
    send_sem,
    recv_sem,
    local_sem,
    store_sem,
    halo_send,
    halo_recv,
    load_sem,
    grad_sem,
    chain_send,
    chain_recv,
    *scratch,
):
    seqs, length, heads, width, ctx_size, tp_size = sizes
    cols = heads * width
    half = wq_ref.shape[0]
    model = 2 * half
    half_model = half
    units = active_ref.shape[1]
    left_at = 3 * cols + LANES
    down_at = left_at + cols + 2 * units
    f = lax.axis_index("fsdp")
    c = lax.axis_index("ctx")
    t = lax.axis_index("tp")
    mate = {"fsdp": 1 - f}
    greet(
        pltpu.get_barrier_semaphore(),
        [(mate, None), ({"ctx": c - 1}, c > 0), ({"ctx": c + 1}, c < ctx_size - 1)]
        + tp_peers(t, tp_size),
    )
    src, first, second, held, total_ref, cube_send, cube_recv = scratch[:7]
    tail_src, tail_got, tail_send, tail_recv = scratch[7:]
    cube = Cube(t, src, n2_ref, first, second, held, cube_send, cube_recv, CHUNKS)
    tail = Tail(t, tail_src, out_inner_ref, tail_got, tail_send, tail_recv, tp_size)
    stores = []

    def store(pairs):
        for source, target in pairs:
            copy = pltpu.make_async_copy(source, target, store_sem.at[len(stores)])
            copy.start()
            stores.append(copy)

    top = pl.ds(pl.multiple_of(f * half, half), half)
    rows, lanes = grid_of(8)
    wide_lanes = lax.broadcasted_iota(jnp.int32, (8, LANES), 1)
    spread = jnp.zeros((8, LANES), f32)
    for h in range(heads):
        row = jnp.broadcast_to(rate_from_ref[h : h + 1, :].astype(f32), (8, 8))
        turned = jnp.sum(jnp.where(rows == lanes, row, 0.0), axis=1, keepdims=True)
        spread = spread + jnp.where(wide_lanes == RATE_AT + h, turned, 0.0)
    slim3[...] = spread.astype(bf16)
    moves = []
    for i, ref in enumerate((wide0, wide1, wide2, wide3, wide4, wide5, wide6, wide7)):
        moves.append((ref, wide_out.at[f, i]))
    at = 0
    for ref in (slim0, slim1, slim2, slim3, slim4, slim5, slim6, slim7):
        moves.append((ref, slim_out.at[f, :, at : at + ref.shape[1]]))
        at += ref.shape[1]
    moves += [
        (wr_ref, wr_all.at[:, top]),
        (wq_ref, w_ref.at[0, top]),
        (wk_ref, w_ref.at[1, top]),
        (wv_ref, w_ref.at[2, top]),
    ]
    near = [pltpu.make_async_copy(src, dst, local_sem.at[i]) for i, (src, dst) in enumerate(moves)]
    local_count = len(moves)
    moves += [(wo_own, wo_ref.at[f]), (wg_own, wg_other), (wu_own, wu_other), (wd_own, wd_other)]
    across = [
        remote(src, dst, send_sem.at[i], recv_sem.at[i], mate) for i, (src, dst) in enumerate(moves)
    ]
    for copy in across[:local_count] + near:
        copy.start()
    own_loads = [
        pltpu.make_async_copy(wo_own, wo_ref.at[f], load_sem.at[0]),
        pltpu.make_async_copy(wd_own, wd_ref.at[f], load_sem.at[2]),
        pltpu.make_async_copy(grad_hbm, grad_ref, grad_sem),
    ]

    @pl.loop(0, seqs)
    def _(s):
        here = pl.ds(pl.multiple_of(s * length, length), length)
        n1_ref[here, :] = normed(x_ref[here, :].astype(f32), gain_ref[...]).astype(bf16)

    for i in range(local_count):
        near[i].wait()
        across[i].wait_recv()
    for copy in across[local_count:] + own_loads:
        copy.start()
    kinds = 4
    into_f32[...] = jnp.zeros_like(into_f32)
    back_f32[...] = jnp.zeros_like(back_f32)
    for core in range(2):
        for kind in range(kinds):
            spot = core * 32 + kind * 8
            into_f32[spot : spot + 8, :] = wide_out[core, kind].astype(f32)
        for kind in range(kinds):
            at = kind * cols
            wide = cols if kind < 3 else LANES
            back_f32[core * 32 + kind * 8 : core * 32 + kind * 8 + 8, at : at + wide] = slim_out[
                core, :, at : at + wide
            ].astype(f32)
    into_f32[RATE_AT : RATE_AT + heads, :] = wr_all[...].astype(f32)
    into_ref[...] = into_f32[...].astype(bf16)
    back_ref[...] = back_f32[...].astype(bf16)
    store([(w_ref, wqkv_out), (n1_ref, n1_out), (wide_out, wide_hbm), (slim_out, slim_hbm)])
    store([(into_ref, into_out), (back_ref, back_out)])

    def halo_of(s):
        return remote(
            halo_out.at[s], halo_in.at[s], halo_send.at[s], halo_recv.at[s], {"ctx": c + 1}
        )

    @pl.loop(0, seqs)
    def _(k):
        s = cube.block_at(k)
        here = pl.ds(pl.multiple_of(s * length, length), length)
        block = n1_ref[here, :]
        tail = mt(block, into_ref[...])
        inner = tail.astype(bf16)
        inner_ref[here, :] = inner
        for i in range(3):
            pre = mm(block, w_ref[i]) + SCALE * mm(inner, back_ref[:, i * cols : (i + 1) * cols])
            ext_ref[s, HALO : HALO + length, i * cols : (i + 1) * cols] = pre
            halo_out[s, :, i * cols : (i + 1) * cols] = pre[length - HALO :, :].astype(bf16)
        pre_rate = tail + SCALE * mm(inner, back_ref[:, 3 * cols :])
        rates_ref[here, :] = jax.nn.sigmoid(pre_rate) * kept(lens_ref, s, c, length)

        @pl.when(c < ctx_size - 1)
        def _():
            halo_of(s).start()

    taps = jnp.concatenate([qtaps_ref[...], ktaps_ref[...], vtaps_ref[...]], axis=1)
    row_at, col_at = grid_of(length)

    def solve(s):
        @pl.when(c > 0)
        def _():
            halo_of(s).wait_recv()
            ext_ref[s, 0:HALO, :] = halo_in[s].astype(f32)

        @pl.when(c == 0)
        def _():
            ext_ref[s, 0:HALO, :] = jnp.zeros((HALO, 3 * cols), f32)

        here = pl.ds(pl.multiple_of(s * length, length), length)
        rate_block = rates_ref[here, :]
        queries, keys, values, rates, stricts = [], [], [], [], []
        for h in range(heads):
            at = h * width
            parts = [
                jax.nn.silu(convolved(ext_ref, taps, s, length, i * cols + at, width))
                for i in range(3)
            ]
            query, key = [
                a * lax.rsqrt(jnp.sum(a * a, axis=-1, keepdims=True) + EPS) for a in parts[:2]
            ]
            rate = column(rate_block, RATE_AT + h)
            queries.append(query)
            keys.append(key)
            values.append(parts[2])
            rates.append(rate)
            stricts.append(
                jnp.where(row_at > col_at, rate * finer(key, key, ((1,), (1,))), 0.0)
            )
        inverses = unit_inverses(stricts)
        for h in range(heads):
            pair = s * heads + h
            query, key, value, rate, inverse = queries[h], keys[h], values[h], rates[h], inverses[h]
            wkey = mm(inverse, rate * key)
            wval = mm(inverse, rate * value)
            scores = jnp.where(row_at >= col_at, finer(query, key, ((1,), (1,))), 0.0)
            inv_ref[pair] = inverse.astype(bf16)
            wkey_ref[pair] = wkey.astype(bf16)
            wval_ref[pair] = wval
            reach_ref[pair] = (query - mm(scores, wkey)).astype(bf16)
            local_ref[pair] = finer(scores, wval, ((1,), (0,)))
            map_ref[pair] = (jnp.where(row_at == col_at, 1.0, 0.0) - tm(key, wkey)).astype(bf16)
            end_ref[pair] = tm(key, wval)

    gain = head_gain_ref[...]

    def hop_of(pair):
        return remote(
            chain_out.at[pair],
            start_ref.at[pair],
            chain_send.at[pair],
            chain_recv.at[pair],
            {"ctx": c + 1},
        )

    def link(s):
        for h in range(heads):
            pair = s * heads + h

            @pl.when(c > 0)
            def _(pair=pair):
                hop_of(pair).wait_recv()

            @pl.when(c == 0)
            def _(pair=pair):
                start_ref[pair] = jnp.zeros((width, width), bf16)

            @pl.when(c < ctx_size - 1)
            def _(pair=pair):
                chain_out[pair] = (mm(map_ref[pair], start_ref[pair]) + end_ref[pair]).astype(bf16)
                hop_of(pair).start()

        here = part_of(s, length)
        for h in range(heads):
            pair = s * heads + h
            mixed = mm(reach_ref[pair], start_ref[pair]) + local_ref[pair]
            heads_ref[here, h * width : (h + 1) * width] = normed(mixed, gain).astype(bf16)

    into = stacked([slim_out[core, :, left_at : left_at + cols] for core in range(2)])
    across[local_count].wait_recv()
    own_loads[0].wait()
    store([(wo_ref.at[1 - f], wo_other)])

    def project(i):
        here = part_of(cube.block_at(i), length)
        low = heads_ref[here, :]
        for side in range(2):
            src[here, side * half_model : (side + 1) * half_model] = mm(low, wo_ref[side]).astype(bf16)
        tail_src[here, :] = mt(low, into).astype(bf16)
        cube.send_block(i)

        @pl.when(i < 3)
        def _():
            tail.send_block(cube.block_at(i))

        @pl.when(i == 2)
        def _():
            cube.middle_half(1)

        @pl.when(i == 3)
        def _():
            cube.middle_half(0)

    @pl.loop(0, seqs + ctx_size - 1)
    def _(k):
        @pl.when(k < seqs)
        def _():
            solve(cube.block_at(k))

        @pl.when((k >= c) & (k < c + seqs))
        def _():
            link(cube.block_at(k - c))
            project(k - c)

    store(
        [
            (ext_ref, ext_out),
            (inner_ref, inner_out),
            (rates_ref, rates_out),
            (inv_ref, inv_out),
            (wkey_ref, wkey_out),
            (wval_ref, wval_out),
            (reach_ref, reach_out),
            (local_ref, local_out),
            (map_ref, map_out),
            (heads_ref, heads_out),
            (start_ref, start_out),
        ]
    )
    cube.finish(total_ref)
    inner = tail.total().astype(bf16)
    here = part_of(t, length)
    right = stacked([wide_out[core, 6] for core in range(2)])
    resid = x_ref[here, :].astype(f32) + total_ref[...] + SCALE * mm(inner, right)
    resid_ref[...] = resid
    out_inner_ref[here, :] = inner
    n2_ref[here, :] = normed(resid, gain2_ref[...]).astype(bf16)
    cube.spread()
    tail.start(1)
    for copy in across[local_count + 1 :]:
        copy.wait_recv()
    wd_load = pltpu.make_async_copy(wd_other, wd_ref.at[1 - f], load_sem.at[3])
    wd_load.start()
    own_loads[2].wait()
    down_from = stacked([wide_out[core, 7] for core in range(2)])
    for s in range(seqs):
        here = pl.ds(s * length, length)
        down_inner_ref[here, :] = (
            kept(lens_ref, s, c, length) * (SCALE * mt(grad_ref[here, :], down_from))
        ).astype(bf16)
    own_loads[1].wait()
    wd_load.wait()

    def activate(at):
        into_down = stacked([slim_out[core, :, pl.ds(down_at + at.start, at.size)] for core in range(2)])
        part = mt(grad_ref[:, :half_model], wd_ref[0, at, :])
        part = part + mt(grad_ref[:, half_model:], wd_ref[1, at, :])
        part = part + mm(down_inner_ref[...], into_down)
        for s in range(seqs):
            active_ref[s * length : (s + 1) * length, at] = (
                kept(lens_ref, s, c, length) * part[s * length : (s + 1) * length]
            )

    cube.relay()
    unit_steps(units, activate)
    store([(active_ref, active_out), (down_inner_ref, down_inner_out)])
    tail.wait(1)
    cube.done()
    tail.done()
    for copy in across:
        copy.wait_send()
    for copy in stores:
        copy.wait()

    @pl.when(c < ctx_size - 1)
    def _():
        @pl.loop(0, seqs)
        def _(s):
            halo_of(s).wait_send()

        @pl.loop(0, seqs * heads)
        def _(pair):
            hop_of(pair).wait_send()


def feed_kernel(
    sizes,
    lens_ref,
    n2_ref,
    gain_ref,
    wide_ref,
    slim_ref,
    down_grad_ref,
    grad_ref,
    wg_own,
    wg_other,
    wu_own,
    wu_other,
    wd_own,
    wd_other,
    active_hbm,
    resid_hbm,
    low_ref,
    inner_grad_ref,
    gresid_hbm,
    down_hbm,
    down_tail_ref,
    gate_right_ref,
    up_right_ref,
    down_left_ref,
    wg_ref,
    wu_ref,
    wd_ref,
    act_ref,
    dgate_ref,
    dup_ref,
    inner_ref,
    back_gate,
    back_up,
    own_grad,
    active_ref,
    resid_ref,
    gresid_ref,
    down_ref,
    load_sem,
    piece_sem,
    store_sem,
    grad_sem,
    *scratch,
):
    seqs, length, cols, ctx_size, tp_size = sizes
    model = n2_ref.shape[1]
    half_model = model // 2
    units = active_ref.shape[1]
    gate_at = 4 * cols + LANES
    up_at = gate_at + units
    down_at = up_at + units
    f = lax.axis_index("fsdp")
    c = lax.axis_index("ctx")
    t = lax.axis_index("tp")
    step = 2 * LANES
    spans = [pl.ds(at, min(step, units - at)) for at in range(0, units, step)]
    whole = [
        pltpu.make_async_copy(wd_own, wd_ref.at[f], load_sem.at[0]),
        pltpu.make_async_copy(wd_other, wd_ref.at[1 - f], load_sem.at[1]),
        pltpu.make_async_copy(resid_hbm, resid_ref, load_sem.at[2]),
    ]

    def piece_loads(at, k):
        return [
            pltpu.make_async_copy(source.at[:, at], target.at[:, at], piece_sem.at[k, i])
            for i, (source, target) in enumerate(
                (
                    (wg_own, wg_ref.at[f]),
                    (wg_other, wg_ref.at[1 - f]),
                    (wu_own, wu_ref.at[f]),
                    (wu_other, wu_ref.at[1 - f]),
                    (active_hbm, active_ref),
                )
            )
        ]

    for k, at in enumerate(spans):
        for load in piece_loads(at, k):
            load.start()
    for load in whole:
        load.start()
    here = part_of(t, length)
    own_load = pltpu.make_async_copy(grad_ref.at[here], own_grad, grad_sem)
    own_load.start()
    greet(pltpu.get_barrier_semaphore(), tp_peers(t, tp_size))
    src, first, second, held, total_ref, send_sem, recv_sem = scratch[:7]
    tail_src, tail_got, tail_send, tail_recv = scratch[7:]
    cube = Cube(t, src, low_ref, first, second, held, send_sem, recv_sem, CHUNKS)
    tail = Tail(t, tail_src, inner_grad_ref, tail_got, tail_send, tail_recv, tp_size)
    into = stacked([wide_ref[core, 4 + kind] for core in range(2) for kind in range(2)])
    blank = jnp.zeros((8, units), bf16)
    gates = [slim_ref[core, :, gate_at : gate_at + units] for core in range(2)]
    ups = [slim_ref[core, :, up_at : up_at + units] for core in range(2)]
    back_gate[...] = stacked([gates[0], blank, gates[1], blank])
    back_up[...] = stacked([blank, ups[0], blank, ups[1]])
    inner_ref[...] = mt(n2_ref[...], into).astype(bf16)
    def forward(at, k):
        for load in piece_loads(at, k):
            load.wait()
        pre = []
        for weight, back in ((wg_ref, back_gate), (wu_ref, back_up)):
            part = mm(n2_ref[:, :half_model], weight[0, :, at])
            part = part + mm(n2_ref[:, half_model:], weight[1, :, at])
            pre.append(part + SCALE * mm(inner_ref[...], back[:, at]))
        gate, up = pre
        sigma = jax.nn.sigmoid(gate)
        silu = gate * sigma
        active = active_ref[:, at]
        act_ref[:, at] = (silu * up).astype(bf16)
        dgate_ref[:, at] = (active * up * (sigma * (1.0 + gate * (1.0 - sigma)))).astype(bf16)
        dup_ref[:, at] = (active * silu).astype(bf16)

    full = units // step

    @pl.loop(0, full)
    def _(k):
        forward(part_of(k, step), k)

    if units % step:
        forward(spans[-1], full)
    tail_src[...] = (
        SCALE * (mt(dgate_ref[...], back_gate[...]) + mt(dup_ref[...], back_up[...]))
    ).astype(bf16)
    tail.start(0)

    def project(half, chunk):
        rows = part_of(chunk, cube.width)
        src[:, cube.columns(half, chunk)] = (
            mt(dgate_ref[...], wg_ref[half, rows, :]) + mt(dup_ref[...], wu_ref[half, rows, :])
        ).astype(bf16)
        cube.start(half, chunk)

    cube.each(project)
    cube.middle()
    for load in whole:
        load.wait()

    def descend(half, chunk):
        down_ref[:, cube.columns(half, chunk)] = mm(
            act_ref[...], wd_ref[half, :, part_of(chunk, cube.width)]
        ).astype(bf16)

    cube.each(descend)
    down_store = pltpu.make_async_copy(down_ref, down_hbm, store_sem.at[0])
    down_store.start()
    cube.finish(total_ref)
    own_load.wait()
    inner = tail.total().astype(bf16)
    grad_second = total_ref[...] + mm(inner, into)
    grad = own_grad[...].astype(f32) * kept(lens_ref, t, c, length) + norm_back(
        resid_ref[...], gain_ref[...], grad_second
    )
    gresid_ref[...] = grad
    grad_store = pltpu.make_async_copy(gresid_ref, gresid_hbm, store_sem.at[1])
    grad_store.start()
    low_ref[here, :] = grad.astype(bf16)
    inner_grad_ref[here, :] = inner
    cube.spread()
    tail.start(1)
    into_down = stacked([slim_ref[core, :, down_at : down_at + units] for core in range(2)])
    down_tail_ref[...] = mt(act_ref[...], into_down).astype(bf16)
    gate_right_ref[...] = SCALE * tm(inner_ref[...], dgate_ref[...])[:32]
    cube.relay()
    up_right_ref[...] = SCALE * tm(inner_ref[...], dup_ref[...])[:32]
    down_left_ref[...] = tm(down_grad_ref[...], act_ref[...])[:32]
    tail.wait(1)
    cube.done()
    tail.done()
    down_store.wait()
    grad_store.wait()


def strip_plan(cols, model, units):
    widths = (
        ("ql", model), ("qr", cols), ("kl", model), ("kr", cols), ("vl", model), ("vr", cols),
        ("rl", model), ("rr", LANES), ("ol", cols), ("or", model), ("gl", model), ("gr", units),
        ("ul", model), ("ur", units), ("dl", units), ("dr", model),
    )
    plan, at = {}, 0
    for name, wide in widths:
        plan[name] = (at, wide)
        at += wide
    return plan, at


BACK_LOADS = 24


def back_kernel(
    sizes,
    lens_ref,
    low_ref,
    head_gain_ref,
    gain_ref,
    qtaps_ref,
    ktaps_ref,
    vtaps_ref,
    wide_ref,
    slim_ref,
    tail_src,
    feed_grad_ref,
    out_inner_ref,
    inner_ref,
    gate_right_ref,
    up_right_ref,
    down_left_ref,
    start_hbm,
    map_hbm,
    reach_hbm,
    local_hbm,
    inv_hbm,
    wkey_hbm,
    wval_hbm,
    ext_hbm,
    rates_hbm,
    heads_hbm,
    down_hbm,
    resid_hbm,
    grad_hbm,
    n2_hbm,
    n1_hbm,
    x_hbm,
    gresid_hbm,
    w_hbm,
    back_hbm,
    into_hbm,
    wo_own,
    wo_other,
    block_hbm,
    input_grad_hbm,
    packed_ref,
    start_ref,
    map_ref,
    reach_ref,
    local_ref,
    inv_ref,
    wkey_ref,
    wval_ref,
    ext_ref,
    rates_ref,
    heads_ref,
    src,
    resid_ref,
    grad_ref,
    normed_ref,
    x_ref,
    gresid_ref,
    w_ref,
    back_ref,
    into_ref,
    wo_ref,
    out_ref,
    pre_ref,
    dmix_ref,
    after_ref,
    chain_out,
    gconv_ref,
    halo_out,
    halo_in,
    down_inner_ref,
    keys_ref,
    slopes_ref,
    values_ref,
    vslopes_ref,
    dfresh_ref,
    dkeys_ref,
    fresh_ref,
    tail2_src,
    inner_grad_ref,
    pack,
    mate_in,
    mine_ref,
    got,
    summed,
    load_sem,
    store_sem,
    chain_send,
    chain_recv,
    halo_send,
    halo_recv,
    swap_send,
    swap_recv,
    part_send,
    part_recv,
    first,
    second,
    held,
    total_ref,
    cube_send,
    cube_recv,
    cube2_send,
    cube2_recv,
    src2,
    first2,
    second2,
    held2,
    tail_got,
    tail_send,
    tail_recv,
    tail2_got,
    tail2_send,
    tail2_recv,
):
    seqs, length, heads, width, ctx_size, tp_size = sizes
    cols = heads * width
    model = low_ref.shape[1]
    half_model = model // 2
    units = gate_right_ref.shape[1]
    left_at = 3 * cols + LANES
    pairs = seqs * heads
    plan, used = strip_plan(cols, model, units)
    f = lax.axis_index("fsdp")
    c = lax.axis_index("ctx")
    t = lax.axis_index("tp")
    mate = {"fsdp": 1 - f}
    mine = part_of(t, length)
    loads = {}

    def fetch(name, source, target):
        loads[name] = pltpu.make_async_copy(source, target, load_sem.at[len(loads)])
        loads[name].start()

    fetch("wo_own", wo_own, wo_ref.at[f])
    fetch("wo_other", wo_other, wo_ref.at[1 - f])
    fetch("src", down_hbm, src)
    fetch("reach", reach_hbm, reach_ref)
    fetch("start", start_hbm, start_ref)
    fetch("local", local_hbm, local_ref)
    fetch("map", map_hbm, map_ref)
    fetch("ext", ext_hbm, ext_ref)
    fetch("rates", rates_hbm, rates_ref)
    fetch("wkey", wkey_hbm, wkey_ref)
    fetch("wval", wval_hbm, wval_ref)
    fetch("inv", inv_hbm, inv_ref)
    fetch("heads", heads_hbm, heads_ref)
    fetch("resid", resid_hbm, resid_ref)
    fetch("n2", n2_hbm, normed_ref)
    fetch("grad", grad_hbm, grad_ref)
    greet(
        pltpu.get_barrier_semaphore(),
        [(mate, None)] + tp_peers(t, tp_size),
        [({"ctx": c + 1 + i}, c + 1 + i < ctx_size) for i in range(ctx_size - 1)],
        c,
    )
    cube = Cube(t, src, out_ref, first, second, held, cube_send, cube_recv, CHUNKS)
    tail = Tail(t, tail_src, down_inner_ref, tail_got, tail_send, tail_recv, tp_size)
    cube2 = Cube(t, src2, src, first2, second2, held2, cube2_send, cube2_recv, CHUNKS)
    tail2 = Tail(t, tail2_src, inner_grad_ref, tail2_got, tail2_send, tail2_recv, tp_size)

    def put(name, core, rows):
        at, wide = plan[name]
        pack[core, :, at : at + wide] = rows.astype(bf16)

    tail.start(0)
    gain = head_gain_ref[...]
    taps = jnp.concatenate([qtaps_ref[...], ktaps_ref[...], vtaps_ref[...]], axis=1)
    row_at, col_at = grid_of(length)
    gconv_ref[...] = jnp.zeros_like(gconv_ref)
    from_out = stacked([wide_ref[core, 6] for core in range(2)])
    into_out = stacked([slim_ref[core, :, left_at : left_at + cols] for core in range(2)])
    out_grad = (SCALE * mt(low_ref[...], from_out)).astype(bf16)
    loads["wo_own"].wait()
    loads["wo_other"].wait()
    dheads = (
        mt(low_ref[:, :half_model], wo_ref[0])
        + mt(low_ref[:, half_model:], wo_ref[1])
        + mm(out_grad, into_out)
    )
    for s in range(seqs):
        for h in range(heads):
            dmix_ref[s * heads + h] = dheads[
                s * length : (s + 1) * length, h * width : (h + 1) * width
            ]
    loads["src"].wait()
    cube.each(cube.start)
    for name in ("reach", "start", "local", "map"):
        loads[name].wait()

    @pl.loop(0, seqs)
    def _(s):
        for h in range(heads):
            pair = s * heads + h
            mixed = mm(reach_ref[pair], start_ref[pair]) + local_ref[pair]
            dmix_ref[pair] = norm_back(mixed, gain, dmix_ref[pair])

    for name in ("ext", "rates", "wkey", "wval", "inv"):
        loads[name].wait()
    fetch("w", w_hbm, w_ref)
    fetch("back", back_hbm, back_ref)
    fetch("into", into_hbm, into_ref)
    fetch("x", x_hbm.at[mine], x_ref)
    fetch("gresid", gresid_hbm, gresid_ref)

    def hop_of(pair):
        return remote(
            chain_out.at[pair],
            after_ref.at[pair],
            chain_send.at[pair],
            chain_recv.at[pair],
            {"ctx": c - 1},
        )

    def link(s):
        for h in range(heads):
            pair = s * heads + h

            @pl.when(c == ctx_size - 1)
            def _(pair=pair):
                after_ref[pair] = jnp.zeros((width, width), bf16)

            @pl.when(c < ctx_size - 1)
            def _(pair=pair):
                hop_of(pair).wait_recv()

            @pl.when(c > 0)
            def _(pair=pair):
                chain_out[pair] = (
                    tm(map_ref[pair], after_ref[pair]) + tm(reach_ref[pair], dmix_ref[pair])
                ).astype(bf16)
                hop_of(pair).start()

    def unconvolve(s, kind):
        here = part_of(s, length)
        for h in range(heads):
            at = kind * cols + h * width
            total = None
            spill = None
            for j in range(CONV):
                tap = taps[j : j + 1, at : at + width]
                term = tap * gconv_ref[pl.ds(HALO + CONV - 1 - j, length), pl.ds(at, width)]
                edge = tap * gconv_ref[pl.ds(CONV - 1 - j, HALO), pl.ds(at, width)]
                total = term if total is None else total + term
                spill = edge if spill is None else spill + edge
            pre_ref[here, at : at + width] = total.astype(bf16)
            halo_out[0, s, :, at : at + width] = total[length - HALO :, :]
            halo_out[1, s, :, at : at + width] = spill

    def early(s):
        every = range(heads)
        at = [h * width for h in every]
        convs = [
            [convolved(ext_ref, taps, s, length, i * cols + at[h], width) for i in range(3)]
            for h in every
        ]
        starts_in = [start_ref[s * heads + h] for h in every]
        grads_in = [dmix_ref[s * heads + h] for h in every]
        wkeys = [wkey_ref[s * heads + h] for h in every]
        wvals = [wval_ref[s * heads + h] for h in every]
        fresh = [wval - mm(wkey, start) for wval, wkey, start in zip(wvals, wkeys, starts_in)]
        sigmas = [[jax.nn.sigmoid(a) for a in row] for row in convs]
        slopes = [
            [b * (1.0 + a * (1.0 - b)) for a, b in zip(row, sig)] for row, sig in zip(convs, sigmas)
        ]
        acts = [[a * b for a, b in zip(row, sig)] for row, sig in zip(convs, sigmas)]
        scales = [
            [lax.rsqrt(jnp.sum(a * a, axis=-1, keepdims=True) + EPS) for a in row[:2]] for row in acts
        ]
        query = [acts[h][0] * scales[h][0] for h in every]
        key = [acts[h][1] * scales[h][1] for h in every]
        lower = row_at >= col_at
        scores = [jnp.where(lower, finer(q, k, ((1,), (1,))), 0.0) for q, k in zip(query, key)]
        dscores = [
            jnp.where(lower, finer(g, v, ((1,), (1,))), 0.0) for g, v in zip(grads_in, fresh)
        ]
        dquery = [
            mt(g, start) + mm(d, k) for g, start, d, k in zip(grads_in, starts_in, dscores, key)
        ]
        dfresh = [tm(p, g) for p, g in zip(scores, grads_in)]
        dkeys = [tm(d, q) for d, q in zip(dscores, query)]
        along = [jnp.sum(q * g, axis=-1, keepdims=True) for q, g in zip(query, dquery)]
        for h in every:
            pair = s * heads + h
            keys_ref[pair] = key[h]
            slopes_ref[pair] = slopes[h][1] * scales[h][1]
            values_ref[pair] = acts[h][2]
            vslopes_ref[pair] = slopes[h][2]
            dfresh_ref[pair] = dfresh[h]
            dkeys_ref[pair] = dkeys[h]
            fresh_ref[pair] = fresh[h].astype(bf16)
            gconv_ref[pl.ds(HALO, length), pl.ds(at[h], width)] = (
                slopes[h][0] * scales[h][0] * (dquery[h] - query[h] * along[h])
            )
        unconvolve(s, 0)

    def late(s):
        every = range(heads)
        here = part_of(s, length)
        rate_block = rates_ref[here, :]
        lane = lax.broadcasted_iota(jnp.int32, (length, LANES), 1)
        rate = [column(rate_block, RATE_AT + h) for h in every]
        start = [start_ref[s * heads + h] for h in every]
        after = [after_ref[s * heads + h] for h in every]
        key = [keys_ref[s * heads + h] for h in every]
        fresh = [fresh_ref[s * heads + h] for h in every]
        before = [dfresh_ref[s * heads + h] for h in every]
        inverse = [inv_ref[s * heads + h] for h in every]
        dkeys = [dkeys_ref[s * heads + h] for h in every]
        values = [values_ref[s * heads + h] for h in every]
        keyed = [slopes_ref[s * heads + h] for h in every]
        valued = [vslopes_ref[s * heads + h] for h in every]
        low = [item.astype(bf16) for item in key]
        dfresh = [b + mm(k, a) for b, k, a in zip(before, low, after)]
        dvalue = [tm(inv, d) for inv, d in zip(inverse, dfresh)]
        dvalue_low = [item.astype(bf16) for item in dvalue]
        products = [mt(k, k) for k in low]
        outer = [mt(v, a) for v, a in zip(fresh, after)]
        dkey_in = [-mt(d, st) for d, st in zip(dvalue_low, start)]
        dstrict = [
            jnp.where(row_at > col_at, -mt(d, v), 0.0) for d, v in zip(dvalue_low, fresh)
        ]
        dprod = [(r * d).astype(bf16) for r, d in zip(rate, dstrict)]
        forth = [mm(d, k) for d, k in zip(dprod, low)]
        back = [tm(d, k) for d, k in zip(dprod, low)]
        dkey = [
            dkeys[h] + outer[h] + rate[h] * dkey_in[h] + forth[h] + back[h] for h in every
        ]
        drate = [
            jnp.sum(
                dstrict[h] * products[h] + dvalue[h] * values[h] + dkey_in[h] * key[h],
                axis=-1,
                keepdims=True,
            )
            for h in every
        ]
        along = [jnp.sum(k * d, axis=-1, keepdims=True) for k, d in zip(key, dkey)]
        rate_grads = jnp.zeros((length, LANES), f32)
        for h in every:
            at = h * width
            gconv_ref[pl.ds(HALO, length), pl.ds(cols + at, width)] = keyed[h] * (
                dkey[h] - key[h] * along[h]
            )
            gconv_ref[pl.ds(HALO, length), pl.ds(2 * cols + at, width)] = (
                rate[h] * dvalue[h] * valued[h]
            )
            rate_grads = rate_grads + jnp.where(
                lane == RATE_AT + h, drate[h] * rate[h] * (1.0 - rate[h]), 0.0
            )
        unconvolve(s, 1)
        unconvolve(s, 2)
        pre_ref[here, 3 * cols :] = rate_grads.astype(bf16)

    ends = c == ctx_size - 1
    starts = c == 0
    inside = (c > 0) & (c < ctx_size - 1)
    begins = (ctx_size - 1 - c) // (ctx_size - 1)

    final = c // (ctx_size - 1)
    block_store = pltpu.make_async_copy(out_ref, block_hbm, store_sem.at[0])

    def halo_of(s):
        return remote(
            halo_in.at[1, s], halo_in.at[0, s], halo_send.at[s], halo_recv.at[s], {"ctx": c - 1}
        )

    def project(i):
        s = cube2.block_at(i)
        here = part_of(s, length)

        @pl.when(c < ctx_size - 1)
        def _():
            halo_of(s).wait_recv()
            last = pl.ds(pl.multiple_of(s * length + length - 16, 16), 16)
            rows = pre_ref[last, : 3 * cols].astype(f32)
            edge = halo_out[0, s] + halo_in[0, s].astype(f32)
            pre_ref[last, : 3 * cols] = jnp.concatenate([rows[:HALO], edge], axis=0).astype(bf16)

        @pl.when(i == 0)
        def _():
            for name in ("w", "back", "into"):
                loads[name].wait()

        part = mm(pre_ref[here, 3 * cols :], into_ref[...])
        for kind in range(3):
            part = part + mt(pre_ref[here, kind * cols : (kind + 1) * cols], w_ref[kind])
        src2[here, :] = part.astype(bf16)
        tail2_src[here, :] = (SCALE * mt(pre_ref[here, :], back_ref[...])).astype(bf16)
        cube2.send_block(i)

        @pl.when(i < 3)
        def _():
            tail2.send_block(s)

        @pl.when(i == 2)
        def _():
            cube2.middle_half(1)

        @pl.when(i == 3)
        def _():
            cube2.middle_half(0)

    @pl.loop(0, 3 * seqs + 2)
    def _(k):
        part = k // seqs
        odd = lax.rem(k, 2) == seqs % 2
        s = cube2.block_at(lax.rem(k, seqs))
        later = cube2.block_at(
            (1 - begins) * lax.rem(k, seqs) + begins * lax.rem((k + seqs) // 2, seqs)
        )
        ready = (1 - begins) * (k - 2 * seqs - 1) + begins * ((k + seqs - 3) // 2 - seqs)

        @pl.when(k == 4 + 4 * final)
        def _():
            cube.middle()

        @pl.when(k == 7 + 3 * final)
        def _():
            cube.finish(total_ref)
            cube.first_sent()
            loads["resid"].wait()
            inner = tail.total().astype(bf16)
            right = stacked([wide_ref[core, 7] for core in range(2)])
            rows = resid_ref[...] + total_ref[...] + SCALE * mm(inner, right)
            out_ref[mine, :] = (kept(lens_ref, t, c, length) * rows).astype(bf16)
            down_inner_ref[mine, :] = inner
            cube.spread()
            tail.start(1)

        @pl.when(k == 9 + 3 * final)
        def _():
            cube.relay()

        @pl.when((ends & (part == 1)) | ((starts | inside) & (part == 0)))
        def _():
            early(s)

        @pl.when(
            (ends & (part == 0)) | (inside & (part == 1)) | (starts & (part > 0) & (part < 3) & odd)
        )
        def _():
            link(later)

        @pl.when(
            ((ends | inside) & (part == 2))
            | (starts & (part > 0) & (part < 3) & jnp.logical_not(odd))
        )
        def _():
            late(later)
            halo_in[1, later] = halo_out[1, later].astype(bf16)

            @pl.when(c > 0)
            def _():
                halo_of(later).start()

        @pl.when(
            ((ends | inside) & (k > 2 * seqs) & (k < 3 * seqs + 1))
            | (starts & (k > seqs + 2) & jnp.logical_not(odd))
        )
        def _():
            project(ready)


    @pl.when(c > 0)
    def _():
        @pl.loop(0, seqs)
        def _(s):
            halo_of(s).wait_send()

        @pl.loop(0, pairs)
        def _(pair):
            hop_of(pair).wait_send()

    inner = tail2.total().astype(bf16)
    inner_grad_ref[mine, :] = inner
    tail2.start(1)
    loads["n2"].wait()
    feed_left = tm(feed_grad_ref[...], normed_ref[...])
    fetch("n1", n1_hbm, normed_ref)
    pack[:, :, used:] = jnp.zeros((2, 8, pack.shape[2] - used), bf16)
    loads["heads"].wait()
    out_left = tm(out_grad, heads_ref[...])
    out_right = SCALE * tm(out_inner_ref[...], low_ref[...])
    right = SCALE * tm(inner_ref[...], pre_ref[...])
    tail.wait(1)
    masked = jnp.concatenate(
        [
            kept(lens_ref, s, c, length) * down_inner_ref[s * length : (s + 1) * length, :].astype(f32)
            for s in range(seqs)
        ],
        axis=0,
    )
    loads["grad"].wait()
    down_right = SCALE * tm(masked, grad_ref[...])
    for core in range(2):
        at = core * 8
        put("ol", core, out_left[at : at + 8])
        put("or", core, out_right[at : at + 8])
        put("dr", core, down_right[at : at + 8])
        put("dl", core, down_left_ref[at : at + 8, :])
        at = core * 16
        put("gl", core, feed_left[at : at + 8])
        put("ul", core, feed_left[at + 8 : at + 16])
        put("gr", core, gate_right_ref[at : at + 8, :])
        put("ur", core, up_right_ref[at + 8 : at + 16, :])
        for kind, name in enumerate(("qr", "kr", "vr", "rr")):
            at = core * 32 + kind * 8
            put(name, core, right[at : at + 8, kind * cols : kind * cols + plan[name][1]])
    loads["n1"].wait()
    tail2.wait(1)
    left = tm(inner_grad_ref[...], normed_ref[...])
    for core in range(2):
        for kind, name in enumerate(("ql", "kl", "vl", "rl")):
            at = core * 32 + kind * 8
            put(name, core, left[at : at + 8])
    swap = remote(pack.at[1 - f], mate_in, swap_send, swap_recv, mate)
    swap.start()
    cube2.finish(total_ref)
    loads["x"].wait()
    loads["gresid"].wait()
    grad_first = total_ref[...] + mm(inner, into_ref[...])
    grad = gresid_ref[...] + norm_back(x_ref[...].astype(f32), gain_ref[...], grad_first)
    src[mine, :] = grad.astype(bf16)
    cube2.spread()
    cube.done(1)
    block_store.start()
    swap.wait_recv()
    both = (pack[f].astype(f32) + mate_in[...].astype(f32)).astype(bf16)
    piece = both.shape[1] // ctx_size
    for j in range(ctx_size):
        mine_ref[j] = both[:, j * piece : (j + 1) * piece]
    sends = []
    spreads = []
    for i in range(ctx_size - 1):
        peer = {"ctx": lax.rem(c + 1 + i, ctx_size)}
        back = ctx_size - 2 - i
        sends.append(
            remote(
                mine_ref.at[lax.rem(c + 1 + i, ctx_size)],
                got.at[back],
                part_send.at[0, i],
                part_recv.at[0, back],
                peer,
            )
        )
        spreads.append(
            remote(summed.at[c], summed.at[c], part_send.at[1, i], part_recv.at[1, back], peer)
        )
    for copy in sends:
        copy.start()
    cube2.relay()
    for copy in sends:
        copy.wait_recv()
    total = mine_ref[c].astype(f32)
    for i in range(ctx_size - 1):
        total = total + got[i].astype(f32)
    summed[c] = total.astype(bf16)
    for copy in spreads:
        copy.start()
    for copy in spreads:
        copy.wait_recv()
    for j in range(ctx_size):
        packed_ref[:, j * piece : (j + 1) * piece] = summed[j].astype(f32)
    cube2.done()
    grad_store = pltpu.make_async_copy(src, input_grad_hbm, store_sem.at[1])
    grad_store.start()
    swap.wait_send()
    for copy in sends + spreads:
        copy.wait_send()
    tail.done()
    tail2.done()
    block_store.wait()
    grad_store.wait()


def deal_kernel(strips, heads, packed_hbm, block_in, grad_in, block_out, grad_out, *refs):
    outs, (block_ref, grad_ref, packed_ref, load_sem, store_sem, packed_sem) = refs[:-6], refs[-6:]
    count = load_sem.shape[1]
    size = block_ref.shape[0] // count
    moves = []
    for i, (source, middle, target) in enumerate(
        ((block_in, block_ref, block_out), (grad_in, grad_ref, grad_out))
    ):
        for k in range(count):
            here = pl.ds(k * size, size)
            load = pltpu.make_async_copy(source.at[here], middle.at[here], load_sem.at[i, k])
            load.start()
            moves.append(
                (load, pltpu.make_async_copy(middle.at[here], target.at[here], store_sem.at[i, k]))
            )
    packed_load = pltpu.make_async_copy(packed_hbm, packed_ref, packed_sem)
    packed_load.start()
    for load, store in moves:
        load.wait()
        store.start()
    packed_load.wait()
    for index, (out, (at, wide)) in enumerate(zip(outs, strips)):
        if index == 7:
            lanes = lax.broadcasted_iota(jnp.int32, (heads, LANES), 1)
            rows = lax.broadcasted_iota(jnp.int32, (heads, LANES), 0)
            pick = jnp.where(lanes == rows + RATE_AT, 1.0, 0.0)
            out[...] = mt(pick, packed_ref[:, at : at + wide])
        else:
            out[...] = packed_ref[:, at : at + wide]
    for _, store in moves:
        store.wait()


def local(ctx_size, tp_size, *arguments):
    (
        hidden_in,
        seq_lengths,
        mixer_gain,
        feed_gain,
        query_weight,
        key_weight,
        value_weight,
        rate_weight,
        query_conv,
        key_conv,
        value_conv,
        head_gain,
        output_weight,
        gate_weight,
        up_weight,
        down_weight,
        query_left,
        query_right,
        key_left,
        key_right,
        value_left,
        value_right,
        rate_left,
        rate_right,
        output_left,
        output_right,
        gate_left,
        gate_right,
        up_left,
        up_right,
        down_left,
        down_right,
        output_grad,
    ) = arguments
    seqs, length, model = hidden_in.shape
    heads = rate_weight.shape[1]
    width = head_gain.shape[0]
    cols = heads * width
    rows = seqs * length
    units = gate_weight.shape[1]
    half = query_weight.shape[0]
    pairs = seqs * heads
    x = hidden_in.reshape(rows, model)
    grad_rows = output_grad.reshape(rows, model)
    rate_rows = rate_weight.T
    wides = (
        query_left.T,
        key_left.T,
        value_left.T,
        rate_left.T,
        gate_left.T,
        up_left.T,
        output_right,
        down_right,
    )
    slims = (
        query_right,
        key_right,
        value_right,
        output_left.T,
        gate_right,
        up_right,
        down_left.T,
    )
    slim_wide = LANES + sum(item.shape[1] for item in slims)
    gain1, gain2, gain3 = mixer_gain[None, :], feed_gain[None, :], head_gain[None, :]
    ext = length + HALO
    square = (pairs, width, width)
    tall = (pairs, length, width)
    block = rows // tp_size
    smem = pl.BlockSpec(memory_space=pltpu.SMEM)
    mixer_sizes = (seqs, length, heads, width, ctx_size, tp_size)
    kept_shapes = (
        shape((rows, model), bf16),
        shape((2, 8, 8, model), bf16),
        shape((2, 8, slim_wide), bf16),
        shape((LANES, model), bf16),
        shape((LANES, 3 * cols + LANES), bf16),
        shape((seqs, ext, 3 * cols), f32),
        shape((rows, LANES), bf16),
        shape((rows, LANES), f32),
        shape((pairs, length, length), bf16),
        shape(tall, bf16),
        shape(tall, f32),
        shape(tall, bf16),
        shape(tall, f32),
        shape(square, bf16),
        shape((rows, cols), bf16),
        shape(square, bf16),
        shape((rows, units), f32),
        shape((rows, LANES), bf16),
    )
    (
        second,
        out_inner,
        residual,
        wo,
        wg,
        wu,
        wd,
        wqkv,
        n1,
        wide_all,
        slim_all,
        into,
        back,
        pre_ext,
        inner,
        rates,
        inverse,
        wkey,
        wval,
        reach,
        local_out,
        step_map,
        heads_low,
        start,
        active,
        down_grad,
    ) = pl.pallas_call(
        functools.partial(mixer_kernel, mixer_sizes),
        out_shape=(
            shape((rows, model), bf16),
            shape((rows, LANES), bf16),
            shape((block, model), f32),
            shape(output_weight.shape, bf16),
            shape(gate_weight.shape, bf16),
            shape(up_weight.shape, bf16),
            shape(down_weight.shape, bf16),
            shape((3, model, cols), bf16),
        )
        + kept_shapes,
        in_specs=[smem] + [VMEM] * 8 + [ANY] * 24,
        out_specs=(VMEM,) * 3 + (ANY,) * (5 + len(kept_shapes)),
        scratch_shapes=[pltpu.VMEM(item.shape, item.dtype) for item in kept_shapes]
        + [
            pltpu.VMEM(square, f32),
            pltpu.VMEM((3, model, cols), bf16),
            pltpu.VMEM((heads, model), bf16),
            pltpu.VMEM((seqs, HALO, 3 * cols), bf16),
            pltpu.VMEM((seqs, HALO, 3 * cols), bf16),
            pltpu.VMEM((LANES, 3 * cols + LANES), f32),
            pltpu.VMEM((LANES, model), f32),
            pltpu.VMEM(square, bf16),
            pltpu.VMEM((2,) + output_weight.shape, bf16),
            pltpu.VMEM((2,) + down_weight.shape, bf16),
            pltpu.VMEM((rows, model), bf16),
            pltpu.VMEM((8, LANES), bf16),
            DMA((24,)),
            DMA((24,)),
            DMA((20,)),
            DMA((20,)),
            DMA((seqs,)),
            DMA((seqs,)),
            DMA((4,)),
            DMA,
            DMA((pairs,)),
            DMA((pairs,)),
        ]
        + cube_scratch(rows, model)
        + tail_scratch(rows, tp_size),
        compiler_params=params(0),
        name="mixer",
    )(
        seq_lengths,
        x,
        gain1,
        gain2,
        gain3,
        query_conv,
        key_conv,
        value_conv,
        rate_right.T,
        query_weight,
        key_weight,
        value_weight,
        rate_rows,
        *wides,
        *slims,
        output_weight,
        gate_weight,
        up_weight,
        down_weight,
        grad_rows,
    )
    (
        resid_low,
        feed_grad,
        grad_residual,
        down_part,
        down_tail,
        gate_right_grad,
        up_right_grad,
        down_left_grad,
    ) = pl.pallas_call(
        functools.partial(feed_kernel, (seqs, length, cols, ctx_size, tp_size)),
        out_shape=(
            shape((rows, model), bf16),
            shape((rows, LANES), bf16),
            shape((block, model), f32),
            shape((rows, model), bf16),
            shape((rows, LANES), bf16),
            shape((32, units), f32),
            shape((32, units), f32),
            shape((32, units), f32),
        ),
        in_specs=[smem] + [VMEM] * 5 + [ANY] * 9,
        out_specs=(VMEM, VMEM, ANY, ANY) + (VMEM,) * 4,
        scratch_shapes=[
            pltpu.VMEM((2,) + gate_weight.shape, bf16),
            pltpu.VMEM((2,) + up_weight.shape, bf16),
            pltpu.VMEM((2,) + down_weight.shape, bf16),
            pltpu.VMEM((rows, units), bf16),
            pltpu.VMEM((rows, units), bf16),
            pltpu.VMEM((rows, units), bf16),
            pltpu.VMEM((rows, LANES), bf16),
            pltpu.VMEM((LANES, units), bf16),
            pltpu.VMEM((LANES, units), bf16),
            pltpu.VMEM((block, model), bf16),
            pltpu.VMEM((rows, units), f32),
            pltpu.VMEM((block, model), f32),
            pltpu.VMEM((block, model), f32),
            pltpu.VMEM((rows, model), bf16),
            DMA((3,)),
            DMA((-(-units // (2 * LANES)), 5)),
            DMA((2,)),
            DMA,
        ]
        + cube_scratch(rows, model)
        + tail_scratch(rows, tp_size),
        compiler_params=params(2),
        name="feed",
    )(
        seq_lengths,
        second,
        gain2,
        wide_all,
        slim_all,
        down_grad,
        grad_rows,
        gate_weight,
        wg,
        up_weight,
        wu,
        down_weight,
        wd,
        active,
        residual,
    )
    plan, used = strip_plan(cols, model, units)
    grain = LANES * ctx_size
    total_wide = -(-used // grain) * grain
    piece = total_wide // ctx_size
    block_out, input_grad, packed = pl.pallas_call(
        functools.partial(back_kernel, mixer_sizes),
        out_shape=(
            shape((rows, model), bf16),
            shape((rows, model), bf16),
            shape((8, total_wide), f32),
        ),
        in_specs=[smem] + [VMEM] * 15 + [ANY] * 22,
        out_specs=(ANY, ANY, VMEM),
        scratch_shapes=[
            pltpu.VMEM(square, bf16),
            pltpu.VMEM(square, bf16),
            pltpu.VMEM(tall, bf16),
            pltpu.VMEM(tall, f32),
            pltpu.VMEM((pairs, length, length), bf16),
            pltpu.VMEM(tall, bf16),
            pltpu.VMEM(tall, f32),
            pltpu.VMEM((seqs, ext, 3 * cols), f32),
            pltpu.VMEM((rows, LANES), f32),
            pltpu.VMEM((rows, cols), bf16),
            pltpu.VMEM((rows, model), bf16),
            pltpu.VMEM((block, model), f32),
            pltpu.VMEM((rows, model), bf16),
            pltpu.VMEM((rows, model), bf16),
            pltpu.VMEM((block, model), bf16),
            pltpu.VMEM((block, model), f32),
            pltpu.VMEM((3, model, cols), bf16),
            pltpu.VMEM((LANES, 3 * cols + LANES), bf16),
            pltpu.VMEM((LANES, model), bf16),
            pltpu.VMEM((2,) + output_weight.shape, bf16),
            pltpu.VMEM((rows, model), bf16),
            pltpu.VMEM((rows, 3 * cols + LANES), bf16),
            pltpu.VMEM(tall, f32),
            pltpu.VMEM(square, bf16),
            pltpu.VMEM(square, bf16),
            pltpu.VMEM((HALO + length + HALO, 3 * cols), f32),
            pltpu.VMEM((2, seqs, HALO, 3 * cols), f32),
            pltpu.VMEM((2, seqs, HALO, 3 * cols), bf16),
            pltpu.VMEM((rows, LANES), bf16),
            pltpu.VMEM(tall, f32),
            pltpu.VMEM(tall, f32),
            pltpu.VMEM(tall, f32),
            pltpu.VMEM(tall, f32),
            pltpu.VMEM(tall, f32),
            pltpu.VMEM(tall, f32),
            pltpu.VMEM(tall, bf16),
            pltpu.VMEM((rows, LANES), bf16),
            pltpu.VMEM((rows, LANES), bf16),
            pltpu.VMEM((2, 8, total_wide), bf16),
            pltpu.VMEM((8, total_wide), bf16),
            pltpu.VMEM((ctx_size, 8, piece), bf16),
            pltpu.VMEM((ctx_size - 1, 8, piece), bf16),
            pltpu.VMEM((ctx_size, 8, piece), bf16),
            DMA((BACK_LOADS,)),
            DMA((2,)),
            DMA((pairs,)),
            DMA((pairs,)),
            DMA((seqs,)),
            DMA((seqs,)),
            DMA,
            DMA,
            DMA((2, ctx_size - 1)),
            DMA((2, ctx_size - 1)),
        ]
        + cube_scratch(rows, model)[1:]
        + [DMA((4, 2, CHUNKS, 2)), DMA((4, 2, CHUNKS, 2))]
        + cube_scratch(rows, model)[:4]
        + tail_scratch(rows, tp_size)[1:] * 2,
        compiler_params=params(3, 60 << 20),
        name="back",
    )(
        seq_lengths,
        resid_low,
        gain3,
        gain1,
        query_conv,
        key_conv,
        value_conv,
        wide_all,
        slim_all,
        down_tail,
        feed_grad,
        out_inner,
        inner,
        gate_right_grad,
        up_right_grad,
        down_left_grad,
        start,
        step_map,
        reach,
        local_out,
        inverse,
        wkey,
        wval,
        pre_ext,
        rates,
        heads_low,
        down_part,
        residual,
        grad_rows,
        second,
        n1,
        x,
        grad_residual,
        wqkv,
        back,
        into,
        output_weight,
        wo,
    )
    strips = tuple(plan.values())
    dealt = pl.pallas_call(
        functools.partial(deal_kernel, strips, heads),
        out_shape=(shape((rows, model), bf16),) * 2
        + tuple(
            shape((heads, 8) if i == 7 else (8, wide), f32) for i, (_, wide) in enumerate(strips)
        ),
        in_specs=[ANY, ANY, ANY],
        out_specs=(ANY, ANY) + (VMEM,) * len(strips),
        scratch_shapes=[
            pltpu.VMEM((rows, model), bf16),
            pltpu.VMEM((rows, model), bf16),
            pltpu.VMEM((8, total_wide), f32),
            DMA((2, 4)),
            DMA((2, 4)),
            DMA,
        ],
        name="deal",
    )(packed, block_out, input_grad)
    block_out, input_grad = dealt[:2]
    shares = list(dealt[2:])
    lefts = (0, 2, 4, 6, 7, 8, 10, 12, 14)
    shares = [item.T if i in lefts else item for i, item in enumerate(shares)]
    return (
        block_out.reshape(seqs, length, model),
        input_grad.reshape(seqs, length, model),
    ) + tuple(shares)


def solution(mesh):
    placed = (
        P("fsdp", "ctx", None),
        P("fsdp"),
        P(),
        P(),
        P("fsdp", "tp"),
        P("fsdp", "tp"),
        P("fsdp", "tp"),
        P("fsdp", "tp"),
        P(None, "tp"),
        P(None, "tp"),
        P(None, "tp"),
        P(),
        P("tp", "fsdp"),
        P("fsdp", "tp"),
        P("fsdp", "tp"),
        P("tp", "fsdp"),
    )
    left_in, left_over, right_over, right_in = (
        P(None, "fsdp"),
        P("tp", "fsdp"),
        P("fsdp", None),
        P("fsdp", "tp"),
    )
    adapters = (left_in, right_in) * 4 + (left_over, right_over) + (left_in, right_in) * 2 + (
        left_over,
        right_over,
    )
    rows = P("fsdp", "ctx", None)
    return jax.shard_map(
        functools.partial(local, mesh.shape["ctx"], mesh.shape["tp"]),
        mesh=mesh,
        in_specs=placed + adapters + (rows,),
        out_specs=(rows, rows) + adapters,
        check_vma=False,
    )
```

```python
import functools

import jax
import jax.numpy as jnp
from jax import lax
from jax.experimental import pallas as pl
from jax.experimental.pallas import tpu as pltpu
from jax.sharding import PartitionSpec as P

MESH = pl.DeviceIdType.MESH
ANY = pl.BlockSpec(memory_space=pl.ANY)
VMEM = pl.BlockSpec(memory_space=pltpu.VMEM)
DMA = pltpu.SemaphoreType.DMA
f32, bf16 = jnp.float32, jnp.bfloat16

CONV = 4
SCALE = 0.5
EPS = 1e-06
LANES = 128
RATE_AT = 64
HALO = 8


def shape(dims, kind):
    return jax.ShapeDtypeStruct(tuple(dims), kind)


def product(left, right, dims):
    return lax.dot_general(
        left.astype(bf16), right.astype(bf16), (dims, ((), ())), preferred_element_type=f32
    )


def mm(left, right):
    return product(left, right, ((1,), (0,)))


def mt(left, right):
    return product(left, right, ((1,), (1,)))


def tm(left, right):
    return product(left, right, ((0,), (0,)))


def params(collective, limit=58 << 20):
    return pltpu.CompilerParams(
        collective_id=collective, has_side_effects=True, vmem_limit_bytes=limit
    )


def grid_of(size):
    rows = lax.broadcasted_iota(jnp.int32, (size, size), 0)
    cols = lax.broadcasted_iota(jnp.int32, (size, size), 1)
    return rows, cols


def halves(values):
    high = values.astype(bf16)
    return high, (values - high.astype(f32)).astype(bf16)


def finer(left, right, dims):
    lhigh, llow = halves(left)
    rhigh, rlow = halves(right)
    (la,), (ra,) = dims
    return lax.dot_general(
        jnp.concatenate([lhigh, llow, lhigh], axis=la),
        jnp.concatenate([rhigh, rhigh, rlow], axis=ra),
        (dims, ((), ())),
        preferred_element_type=f32,
    )


def unit_inverses(stricts):
    size = stricts[0].shape[0]
    rows, cols = grid_of(size)
    eye = jnp.where(rows == cols, 1.0, 0.0)
    found = [eye - jnp.where((rows >> 1) == (cols >> 1), item, 0.0) for item in stricts]
    level = 1
    while (1 << level) < size:
        joined = ((rows >> (level + 1)) == (cols >> (level + 1))) & ((rows >> level) != (cols >> level))
        lows = [item.astype(bf16) for item in found]
        inner = [mm(jnp.where(joined, item, 0.0), low) for item, low in zip(stricts, lows)]
        found = [item - mm(low, part) for item, low, part in zip(found, lows, inner)]
        level += 1
    lows = [item.astype(bf16) for item in found]
    errors = []
    for item, low in zip(stricts, lows):
        pair = jnp.concatenate(halves(item), axis=1)
        errors.append(eye - low.astype(f32) - mm(pair, jnp.concatenate([low, low], axis=0)))
    return [low.astype(f32) + mm(low, error) for low, error in zip(lows, errors)]


def normed(values, gain):
    return values * lax.rsqrt(jnp.mean(values * values, axis=-1, keepdims=True) + EPS) * gain


def norm_back(values, gain, grad):
    scale = lax.rsqrt(jnp.mean(values * values, axis=-1, keepdims=True) + EPS)
    weighted = gain * grad
    return scale * weighted - values * (scale * scale * scale) * jnp.mean(
        values * weighted, axis=-1, keepdims=True
    )


def greet(barrier, peers, later=(), expected=0):
    count = expected
    for peer, condition in list(peers) + list(later):

        def tell(peer=peer):
            pl.semaphore_signal(barrier, inc=1, device_id=peer, device_id_type=MESH)

        if condition is None:
            tell()
        else:
            pl.when(condition)(tell)
    for peer, condition in peers:
        count = count + (1 if condition is None else jnp.where(condition, 1, 0))
    pl.semaphore_wait(barrier, count)


def remote(source, target, send_sem, recv_sem, peer):
    return pltpu.make_async_remote_copy(
        src_ref=source,
        dst_ref=target,
        send_sem=send_sem,
        recv_sem=recv_sem,
        device_id=peer,
        device_id_type=MESH,
    )


def column(block, lane):
    return block[:, lane : lane + 1]


def convolved(ext_ref, taps, s, length, at, width):
    total = None
    for i in range(CONV):
        rows = ext_ref[s, pl.ds(HALO - (CONV - 1) + i, length), pl.ds(at, width)]
        term = taps[i : i + 1, at : at + width] * rows
        total = term if total is None else total + term
    return total


def kept(lens_ref, s, c, length):
    place = c * length + lax.broadcasted_iota(jnp.int32, (length, 1), 0)
    return jnp.where(place < lens_ref[s], 1.0, 0.0)


def part_of(at, size):
    return pl.ds(pl.multiple_of(at * size, size), size)


class Cube:
    def __init__(self, t, src, out, first, second, held, send_sem, recv_sem, chunks):
        self.y, self.x = t // 2, lax.rem(t, 2)
        self.t, self.src, self.out = t, src, out
        self.first, self.second, self.held = first, second, held
        self.send_sem, self.recv_sem = send_sem, recv_sem
        self.chunks = chunks
        self.block = src.shape[0] // 4
        self.half_width = src.shape[1] // 2
        self.width = self.half_width // chunks
        self.beside = self.y * 2 + (1 - self.x)
        self.above = (1 - self.y) * 2 + self.x

    def peer(self, side):
        return {"tp": self.beside * (1 - side) + self.above * side}

    def columns(self, half, chunk):
        return pl.ds(
            pl.multiple_of(half * self.half_width + chunk * self.width, self.width), self.width
        )

    def copy(self, stage, half, chunk, j):
        wide = self.columns(half, chunk)
        slim = part_of(chunk, self.width)
        send, recv = self.send_sem.at[stage, half, chunk, j], self.recv_sem.at[stage, half, chunk, j]
        across = self.above * (1 - half) + self.beside * half
        if stage == 0:
            g = (1 - half) * (2 * j + 1 - self.x) + half * (2 * (1 - self.y) + j)
            source, target = self.src.at[part_of(g, self.block), wide], self.first.at[half, j, :, slim]
            side = half
        elif stage == 1:
            source, target = self.held.at[half, :, slim], self.second.at[half, :, slim]
            side = 1 - half
        else:
            g = self.t if j == 0 else across
            source = target = self.out.at[part_of(g, self.block), wide]
            side = 1 - half if stage == 2 else half
        return remote(source, target, send, recv, self.peer(side))

    def each(self, body):
        @pl.loop(0, 2 * self.chunks)
        def _(k):
            body(lax.rem(k, 2), k // 2)

    def start(self, half, chunk):
        self.copy(0, half, chunk, 0).start()
        self.copy(0, half, chunk, 1).start()

    def block_at(self, i):
        flip_x, flip_y = (3 - i) // 2, lax.rem(i + 1, 2)
        y = self.y + flip_y * (1 - 2 * self.y)
        return y * 2 + self.x + flip_x * (1 - 2 * self.x)

    def send_block(self, i):
        def go(half, j):
            for chunk in range(self.chunks):
                self.copy(0, half, chunk, j).start()

        @pl.when(i == 0)
        def _():
            go(0, 1 - self.y)
            go(1, 1 - self.x)

        @pl.when(i == 1)
        def _():
            go(0, self.y)

        @pl.when(i == 2)
        def _():
            go(1, self.x)

    def pass_on(self, half, chunk):
        wide = self.columns(half, chunk)
        slim = part_of(chunk, self.width)
        across = self.above * (1 - half) + self.beside * half
        other = (1 - half) * (1 - self.y) + half * (1 - self.x)
        self.copy(0, half, chunk, other).wait_recv()
        self.held[half, :, slim] = (
            self.src[part_of(across, self.block), wide].astype(f32)
            + self.first[half, other, :, slim].astype(f32)
        ).astype(bf16)
        self.copy(1, half, chunk, 0).start()

    def middle(self):
        self.each(self.pass_on)

    def middle_half(self, half):
        @pl.loop(0, self.chunks)
        def _(chunk):
            self.pass_on(half, chunk)

    def finish(self, total_ref):
        def body(half, chunk):
            wide = self.columns(half, chunk)
            slim = part_of(chunk, self.width)
            mine = (1 - half) * self.y + half * self.x
            self.copy(0, half, chunk, mine).wait_recv()
            self.copy(1, half, chunk, 0).wait_recv()
            total_ref[:, wide] = (
                self.src[part_of(self.t, self.block), wide].astype(f32)
                + self.first[half, mine, :, slim].astype(f32)
                + self.second[half, :, slim].astype(f32)
            )

        self.each(body)

    def spread(self):
        def body(half, chunk):
            self.copy(2, half, chunk, 0).start()
            self.copy(3, half, chunk, 0).start()

        self.each(body)

    def relay(self):
        def body(half, chunk):
            self.copy(2, half, chunk, 0).wait_recv()
            self.copy(3, half, chunk, 1).start()

        self.each(body)

    def first_sent(self):
        def body(half, chunk):
            for j in range(2):
                self.copy(0, half, chunk, j).wait_send()

        self.each(body)

    def done(self, since=0):
        def body(half, chunk):
            for j in range(2):
                self.copy(3, half, chunk, j).wait_recv()
            for stage in range(since, 4):
                for j in range(2 if stage in (0, 3) else 1):
                    self.copy(stage, half, chunk, j).wait_send()

        self.each(body)


class Tail:
    def __init__(self, t, src, out, got, send_sem, recv_sem, size):
        self.t, self.src, self.out, self.got, self.size = t, src, out, got, size
        self.send_sem, self.recv_sem = send_sem, recv_sem
        self.block = src.shape[0] // size

    def copies(self, stage):
        found = []
        for i in range(self.size - 1):
            g = lax.rem(self.t + 1 + i, self.size)
            if stage == 0:
                source, target = self.src.at[part_of(g, self.block)], self.got.at[self.size - 2 - i]
            else:
                source = target = self.out.at[part_of(self.t, self.block)]
            found.append(
                remote(
                    source,
                    target,
                    self.send_sem.at[stage, i],
                    self.recv_sem.at[stage, self.size - 2 - i],
                    {"tp": g},
                )
            )
        return found

    def start(self, stage):
        for copy in self.copies(stage):
            copy.start()

    def send_block(self, g):
        i = lax.rem(g - self.t - 1 + self.size, self.size)
        back = self.size - 2 - i
        remote(
            self.src.at[part_of(g, self.block)],
            self.got.at[back],
            self.send_sem.at[0, i],
            self.recv_sem.at[0, back],
            {"tp": g},
        ).start()

    def wait(self, stage):
        for copy in self.copies(stage):
            copy.wait_recv()

    def total(self):
        self.wait(0)
        total = self.src[part_of(self.t, self.block), :].astype(f32)
        for i in range(self.size - 1):
            total = total + self.got[i].astype(f32)
        return total

    def done(self):
        for stage in range(2):
            for copy in self.copies(stage):
                copy.wait_send()


CHUNKS = 2


def cube_scratch(rows, model):
    block = rows // 4
    return [
        pltpu.VMEM((rows, model), bf16),
        pltpu.VMEM((2, 2, block, model // 2), bf16),
        pltpu.VMEM((2, block, model // 2), bf16),
        pltpu.VMEM((2, block, model // 2), bf16),
        pltpu.VMEM((block, model), f32),
        DMA((4, 2, CHUNKS, 2)),
        DMA((4, 2, CHUNKS, 2)),
    ]


def tail_scratch(rows, size):
    return [
        pltpu.VMEM((rows, LANES), bf16),
        pltpu.VMEM((size - 1, rows // size, LANES), bf16),
        DMA((2, size - 1)),
        DMA((2, size - 1)),
    ]


def tp_peers(t, size):
    return [({"tp": lax.rem(t + 1 + i, size)}, None) for i in range(size - 1)]


def stacked(pieces):
    rows = sum(piece.shape[0] for piece in pieces)
    fill = jnp.zeros((LANES - rows, pieces[0].shape[1]), f32)
    return jnp.concatenate([piece.astype(f32) for piece in pieces] + [fill], axis=0).astype(bf16)


def slot_loads(pairs, f, sems):
    loads = []
    for i, (own, other, scratch) in enumerate(pairs):
        loads.append(pltpu.make_async_copy(own, scratch.at[f], sems.at[i, 0]))
        loads.append(pltpu.make_async_copy(other, scratch.at[1 - f], sems.at[i, 1]))
    for load in loads:
        load.start()
    return loads


def unit_steps(units, body):
    step = 2 * LANES
    whole = units // step

    @pl.loop(0, whole)
    def _(k):
        body(part_of(k, step))

    if units % step:
        body(pl.ds(whole * step, units % step))


def mixer_kernel(
    sizes,
    lens_ref,
    x_ref,
    gain_ref,
    gain2_ref,
    head_gain_ref,
    qtaps_ref,
    ktaps_ref,
    vtaps_ref,
    rate_from_ref,
    wq_ref,
    wk_ref,
    wv_ref,
    wr_ref,
    wide0,
    wide1,
    wide2,
    wide3,
    wide4,
    wide5,
    wide6,
    wide7,
    slim0,
    slim1,
    slim2,
    slim4,
    slim5,
    slim6,
    slim7,
    wo_own,
    wg_own,
    wu_own,
    wd_own,
    grad_hbm,
    n2_ref,
    out_inner_ref,
    resid_ref,
    wo_other,
    wg_other,
    wu_other,
    wd_other,
    wqkv_out,
    n1_out,
    wide_hbm,
    slim_hbm,
    into_out,
    back_out,
    ext_out,
    inner_out,
    rates_out,
    inv_out,
    wkey_out,
    wval_out,
    reach_out,
    local_out,
    map_out,
    heads_out,
    start_out,
    active_out,
    down_inner_out,
    n1_ref,
    wide_out,
    slim_out,
    into_ref,
    back_ref,
    ext_ref,
    inner_ref,
    rates_ref,
    inv_ref,
    wkey_ref,
    wval_ref,
    reach_ref,
    local_ref,
    map_ref,
    heads_ref,
    start_ref,
    active_ref,
    down_inner_ref,
    end_ref,
    w_ref,
    wr_all,
    halo_out,
    halo_in,
    back_f32,
    into_f32,
    chain_out,
    wo_ref,
    wd_ref,
    grad_ref,
    slim3,
    send_sem,
    recv_sem,
    local_sem,
    store_sem,
    halo_send,
    halo_recv,
    load_sem,
    grad_sem,
    chain_send,
    chain_recv,
    *scratch,
):
    seqs, length, heads, width, ctx_size, tp_size = sizes
    cols = heads * width
    half = wq_ref.shape[0]
    model = 2 * half
    half_model = half
    units = active_ref.shape[1]
    left_at = 3 * cols + LANES
    down_at = left_at + cols + 2 * units
    f = lax.axis_index("fsdp")
    c = lax.axis_index("ctx")
    t = lax.axis_index("tp")
    mate = {"fsdp": 1 - f}
    greet(
        pltpu.get_barrier_semaphore(),
        [(mate, None), ({"ctx": c - 1}, c > 0), ({"ctx": c + 1}, c < ctx_size - 1)]
        + tp_peers(t, tp_size),
    )
    src, first, second, held, total_ref, cube_send, cube_recv = scratch[:7]
    tail_src, tail_got, tail_send, tail_recv = scratch[7:]
    cube = Cube(t, src, n2_ref, first, second, held, cube_send, cube_recv, CHUNKS)
    tail = Tail(t, tail_src, out_inner_ref, tail_got, tail_send, tail_recv, tp_size)
    stores = []

    def store(pairs):
        for source, target in pairs:
            copy = pltpu.make_async_copy(source, target, store_sem.at[len(stores)])
            copy.start()
            stores.append(copy)

    top = pl.ds(pl.multiple_of(f * half, half), half)
    rows, lanes = grid_of(8)
    wide_lanes = lax.broadcasted_iota(jnp.int32, (8, LANES), 1)
    spread = jnp.zeros((8, LANES), f32)
    for h in range(heads):
        row = jnp.broadcast_to(rate_from_ref[h : h + 1, :].astype(f32), (8, 8))
        turned = jnp.sum(jnp.where(rows == lanes, row, 0.0), axis=1, keepdims=True)
        spread = spread + jnp.where(wide_lanes == RATE_AT + h, turned, 0.0)
    slim3[...] = spread.astype(bf16)
    moves = []
    for i, ref in enumerate((wide0, wide1, wide2, wide3, wide4, wide5, wide6, wide7)):
        moves.append((ref, wide_out.at[f, i]))
    at = 0
    for ref in (slim0, slim1, slim2, slim3, slim4, slim5, slim6, slim7):
        moves.append((ref, slim_out.at[f, :, at : at + ref.shape[1]]))
        at += ref.shape[1]
    moves += [
        (wr_ref, wr_all.at[:, top]),
        (wq_ref, w_ref.at[0, top]),
        (wk_ref, w_ref.at[1, top]),
        (wv_ref, w_ref.at[2, top]),
    ]
    near = [pltpu.make_async_copy(src, dst, local_sem.at[i]) for i, (src, dst) in enumerate(moves)]
    local_count = len(moves)
    moves += [(wo_own, wo_ref.at[f]), (wg_own, wg_other), (wu_own, wu_other), (wd_own, wd_other)]
    across = [
        remote(src, dst, send_sem.at[i], recv_sem.at[i], mate) for i, (src, dst) in enumerate(moves)
    ]
    for copy in across[:local_count] + near:
        copy.start()
    own_loads = [
        pltpu.make_async_copy(wo_own, wo_ref.at[f], load_sem.at[0]),
        pltpu.make_async_copy(wd_own, wd_ref.at[f], load_sem.at[2]),
        pltpu.make_async_copy(grad_hbm, grad_ref, grad_sem),
    ]

    @pl.loop(0, seqs)
    def _(s):
        here = pl.ds(pl.multiple_of(s * length, length), length)
        n1_ref[here, :] = normed(x_ref[here, :].astype(f32), gain_ref[...]).astype(bf16)

    for i in range(local_count):
        near[i].wait()
        across[i].wait_recv()
    for copy in across[local_count:] + own_loads:
        copy.start()
    kinds = 4
    into_f32[...] = jnp.zeros_like(into_f32)
    back_f32[...] = jnp.zeros_like(back_f32)
    for core in range(2):
        for kind in range(kinds):
            spot = core * 32 + kind * 8
            into_f32[spot : spot + 8, :] = wide_out[core, kind].astype(f32)
        for kind in range(kinds):
            at = kind * cols
            wide = cols if kind < 3 else LANES
            back_f32[core * 32 + kind * 8 : core * 32 + kind * 8 + 8, at : at + wide] = slim_out[
                core, :, at : at + wide
            ].astype(f32)
    into_f32[RATE_AT : RATE_AT + heads, :] = wr_all[...].astype(f32)
    into_ref[...] = into_f32[...].astype(bf16)
    back_ref[...] = back_f32[...].astype(bf16)
    store([(w_ref, wqkv_out), (n1_ref, n1_out), (wide_out, wide_hbm), (slim_out, slim_hbm)])
    store([(into_ref, into_out), (back_ref, back_out)])

    def halo_of(s):
        return remote(
            halo_out.at[s], halo_in.at[s], halo_send.at[s], halo_recv.at[s], {"ctx": c + 1}
        )

    @pl.loop(0, seqs)
    def _(k):
        s = cube.block_at(k)
        here = pl.ds(pl.multiple_of(s * length, length), length)
        block = n1_ref[here, :]
        tail = mt(block, into_ref[...])
        inner = tail.astype(bf16)
        inner_ref[here, :] = inner
        for i in range(3):
            pre = mm(block, w_ref[i]) + SCALE * mm(inner, back_ref[:, i * cols : (i + 1) * cols])
            ext_ref[s, HALO : HALO + length, i * cols : (i + 1) * cols] = pre
            halo_out[s, :, i * cols : (i + 1) * cols] = pre[length - HALO :, :].astype(bf16)
        pre_rate = tail + SCALE * mm(inner, back_ref[:, 3 * cols :])
        rates_ref[here, :] = jax.nn.sigmoid(pre_rate) * kept(lens_ref, s, c, length)

        @pl.when(c < ctx_size - 1)
        def _():
            halo_of(s).start()

    taps = jnp.concatenate([qtaps_ref[...], ktaps_ref[...], vtaps_ref[...]], axis=1)
    row_at, col_at = grid_of(length)

    def solve(s):
        @pl.when(c > 0)
        def _():
            halo_of(s).wait_recv()
            ext_ref[s, 0:HALO, :] = halo_in[s].astype(f32)

        @pl.when(c == 0)
        def _():
            ext_ref[s, 0:HALO, :] = jnp.zeros((HALO, 3 * cols), f32)

        here = pl.ds(pl.multiple_of(s * length, length), length)
        rate_block = rates_ref[here, :]
        queries, keys, values, rates, stricts = [], [], [], [], []
        for h in range(heads):
            at = h * width
            parts = [
                jax.nn.silu(convolved(ext_ref, taps, s, length, i * cols + at, width))
                for i in range(3)
            ]
            query, key = [
                a * lax.rsqrt(jnp.sum(a * a, axis=-1, keepdims=True) + EPS) for a in parts[:2]
            ]
            rate = column(rate_block, RATE_AT + h)
            queries.append(query)
            keys.append(key)
            values.append(parts[2])
            rates.append(rate)
            stricts.append(
                jnp.where(row_at > col_at, rate * finer(key, key, ((1,), (1,))), 0.0)
            )
        inverses = unit_inverses(stricts)
        for h in range(heads):
            pair = s * heads + h
            query, key, value, rate, inverse = queries[h], keys[h], values[h], rates[h], inverses[h]
            wkey = mm(inverse, rate * key)
            wval = mm(inverse, rate * value)
            scores = jnp.where(row_at >= col_at, finer(query, key, ((1,), (1,))), 0.0)
            inv_ref[pair] = inverse.astype(bf16)
            wkey_ref[pair] = wkey.astype(bf16)
            wval_ref[pair] = wval
            reach_ref[pair] = (query - mm(scores, wkey)).astype(bf16)
            local_ref[pair] = finer(scores, wval, ((1,), (0,)))
            map_ref[pair] = (jnp.where(row_at == col_at, 1.0, 0.0) - tm(key, wkey)).astype(bf16)
            end_ref[pair] = tm(key, wval)

    gain = head_gain_ref[...]

    def hop_of(pair):
        return remote(
            chain_out.at[pair],
            start_ref.at[pair],
            chain_send.at[pair],
            chain_recv.at[pair],
            {"ctx": c + 1},
        )

    def link(s):
        for h in range(heads):
            pair = s * heads + h

            @pl.when(c > 0)
            def _(pair=pair):
                hop_of(pair).wait_recv()

            @pl.when(c == 0)
            def _(pair=pair):
                start_ref[pair] = jnp.zeros((width, width), bf16)

            @pl.when(c < ctx_size - 1)
            def _(pair=pair):
                chain_out[pair] = (mm(map_ref[pair], start_ref[pair]) + end_ref[pair]).astype(bf16)
                hop_of(pair).start()

        here = part_of(s, length)
        for h in range(heads):
            pair = s * heads + h
            mixed = mm(reach_ref[pair], start_ref[pair]) + local_ref[pair]
            heads_ref[here, h * width : (h + 1) * width] = normed(mixed, gain).astype(bf16)

    into = stacked([slim_out[core, :, left_at : left_at + cols] for core in range(2)])
    across[local_count].wait_recv()
    own_loads[0].wait()
    store([(wo_ref.at[1 - f], wo_other)])

    def project(i):
        here = part_of(cube.block_at(i), length)
        low = heads_ref[here, :]
        for side in range(2):
            src[here, side * half_model : (side + 1) * half_model] = mm(low, wo_ref[side]).astype(bf16)
        tail_src[here, :] = mt(low, into).astype(bf16)
        cube.send_block(i)

        @pl.when(i < 3)
        def _():
            tail.send_block(cube.block_at(i))

        @pl.when(i == 2)
        def _():
            cube.middle_half(1)

        @pl.when(i == 3)
        def _():
            cube.middle_half(0)

    @pl.loop(0, seqs + ctx_size)
    def _(k):
        @pl.when((k > c) & (k < c + seqs + 1))
        def _():
            project(k - c - 1)

        @pl.when(k < seqs)
        def _():
            solve(cube.block_at(k))

        @pl.when((k >= c) & (k < c + seqs))
        def _():
            link(cube.block_at(k - c))

    store(
        [
            (ext_ref, ext_out),
            (inner_ref, inner_out),
            (rates_ref, rates_out),
            (inv_ref, inv_out),
            (wkey_ref, wkey_out),
            (wval_ref, wval_out),
            (reach_ref, reach_out),
            (local_ref, local_out),
            (map_ref, map_out),
            (heads_ref, heads_out),
            (start_ref, start_out),
        ]
    )
    cube.finish(total_ref)
    inner = tail.total().astype(bf16)
    here = part_of(t, length)
    right = stacked([wide_out[core, 6] for core in range(2)])
    resid = x_ref[here, :].astype(f32) + total_ref[...] + SCALE * mm(inner, right)
    resid_ref[...] = resid
    out_inner_ref[here, :] = inner
    n2_ref[here, :] = normed(resid, gain2_ref[...]).astype(bf16)
    cube.spread()
    tail.start(1)
    for copy in across[local_count + 1 :]:
        copy.wait_recv()
    wd_load = pltpu.make_async_copy(wd_other, wd_ref.at[1 - f], load_sem.at[3])
    wd_load.start()
    own_loads[2].wait()
    down_from = stacked([wide_out[core, 7] for core in range(2)])
    for s in range(seqs):
        here = pl.ds(s * length, length)
        down_inner_ref[here, :] = (
            kept(lens_ref, s, c, length) * (SCALE * mt(grad_ref[here, :], down_from))
        ).astype(bf16)
    own_loads[1].wait()
    wd_load.wait()

    def activate(at):
        into_down = stacked([slim_out[core, :, pl.ds(down_at + at.start, at.size)] for core in range(2)])
        part = mt(grad_ref[:, :half_model], wd_ref[0, at, :])
        part = part + mt(grad_ref[:, half_model:], wd_ref[1, at, :])
        part = part + mm(down_inner_ref[...], into_down)
        for s in range(seqs):
            active_ref[s * length : (s + 1) * length, at] = (
                kept(lens_ref, s, c, length) * part[s * length : (s + 1) * length]
            )

    cube.relay()
    unit_steps(units, activate)
    store([(active_ref, active_out), (down_inner_ref, down_inner_out)])
    tail.wait(1)
    cube.done()
    tail.done()
    for copy in across:
        copy.wait_send()
    for copy in stores:
        copy.wait()

    @pl.when(c < ctx_size - 1)
    def _():
        @pl.loop(0, seqs)
        def _(s):
            halo_of(s).wait_send()

        @pl.loop(0, seqs * heads)
        def _(pair):
            hop_of(pair).wait_send()


def feed_kernel(
    sizes,
    lens_ref,
    n2_ref,
    gain_ref,
    wide_ref,
    slim_ref,
    down_grad_ref,
    grad_ref,
    wg_own,
    wg_other,
    wu_own,
    wu_other,
    wd_own,
    wd_other,
    active_hbm,
    resid_hbm,
    low_ref,
    inner_grad_ref,
    gresid_hbm,
    down_hbm,
    down_tail_ref,
    gate_right_ref,
    up_right_ref,
    down_left_ref,
    wg_ref,
    wu_ref,
    wd_ref,
    act_ref,
    dgate_ref,
    dup_ref,
    inner_ref,
    back_gate,
    back_up,
    own_grad,
    active_ref,
    resid_ref,
    gresid_ref,
    down_ref,
    load_sem,
    piece_sem,
    store_sem,
    grad_sem,
    *scratch,
):
    seqs, length, cols, ctx_size, tp_size = sizes
    model = n2_ref.shape[1]
    half_model = model // 2
    units = active_ref.shape[1]
    gate_at = 4 * cols + LANES
    up_at = gate_at + units
    down_at = up_at + units
    f = lax.axis_index("fsdp")
    c = lax.axis_index("ctx")
    t = lax.axis_index("tp")
    step = 2 * LANES
    spans = [pl.ds(at, min(step, units - at)) for at in range(0, units, step)]
    whole = [
        pltpu.make_async_copy(wd_own, wd_ref.at[f], load_sem.at[0]),
        pltpu.make_async_copy(wd_other, wd_ref.at[1 - f], load_sem.at[1]),
        pltpu.make_async_copy(resid_hbm, resid_ref, load_sem.at[2]),
    ]

    def piece_loads(at, k):
        return [
            pltpu.make_async_copy(source.at[:, at], target.at[:, at], piece_sem.at[k, i])
            for i, (source, target) in enumerate(
                (
                    (wg_own, wg_ref.at[f]),
                    (wg_other, wg_ref.at[1 - f]),
                    (wu_own, wu_ref.at[f]),
                    (wu_other, wu_ref.at[1 - f]),
                    (active_hbm, active_ref),
                )
            )
        ]

    for k, at in enumerate(spans):
        for load in piece_loads(at, k):
            load.start()
    for load in whole:
        load.start()
    here = part_of(t, length)
    own_load = pltpu.make_async_copy(grad_ref.at[here], own_grad, grad_sem)
    own_load.start()
    greet(pltpu.get_barrier_semaphore(), tp_peers(t, tp_size))
    src, first, second, held, total_ref, send_sem, recv_sem = scratch[:7]
    tail_src, tail_got, tail_send, tail_recv = scratch[7:]
    cube = Cube(t, src, low_ref, first, second, held, send_sem, recv_sem, CHUNKS)
    tail = Tail(t, tail_src, inner_grad_ref, tail_got, tail_send, tail_recv, tp_size)
    into = stacked([wide_ref[core, 4 + kind] for core in range(2) for kind in range(2)])
    blank = jnp.zeros((8, units), bf16)
    gates = [slim_ref[core, :, gate_at : gate_at + units] for core in range(2)]
    ups = [slim_ref[core, :, up_at : up_at + units] for core in range(2)]
    back_gate[...] = stacked([gates[0], blank, gates[1], blank])
    back_up[...] = stacked([blank, ups[0], blank, ups[1]])
    inner_ref[...] = mt(n2_ref[...], into).astype(bf16)
    def forward(at, k):
        for load in piece_loads(at, k):
            load.wait()
        pre = []
        for weight, back in ((wg_ref, back_gate), (wu_ref, back_up)):
            part = mm(n2_ref[:, :half_model], weight[0, :, at])
            part = part + mm(n2_ref[:, half_model:], weight[1, :, at])
            pre.append(part + SCALE * mm(inner_ref[...], back[:, at]))
        gate, up = pre
        sigma = jax.nn.sigmoid(gate)
        silu = gate * sigma
        active = active_ref[:, at]
        act_ref[:, at] = (silu * up).astype(bf16)
        dgate_ref[:, at] = (active * up * (sigma * (1.0 + gate * (1.0 - sigma)))).astype(bf16)
        dup_ref[:, at] = (active * silu).astype(bf16)

    full = units // step

    @pl.loop(0, full)
    def _(k):
        forward(part_of(k, step), k)

    if units % step:
        forward(spans[-1], full)
    tail_src[...] = (
        SCALE * (mt(dgate_ref[...], back_gate[...]) + mt(dup_ref[...], back_up[...]))
    ).astype(bf16)
    tail.start(0)

    def project(half, chunk):
        rows = part_of(chunk, cube.width)
        src[:, cube.columns(half, chunk)] = (
            mt(dgate_ref[...], wg_ref[half, rows, :]) + mt(dup_ref[...], wu_ref[half, rows, :])
        ).astype(bf16)
        cube.start(half, chunk)

    cube.each(project)
    cube.middle()
    for load in whole:
        load.wait()

    def descend(half, chunk):
        down_ref[:, cube.columns(half, chunk)] = mm(
            act_ref[...], wd_ref[half, :, part_of(chunk, cube.width)]
        ).astype(bf16)

    cube.each(descend)
    down_store = pltpu.make_async_copy(down_ref, down_hbm, store_sem.at[0])
    down_store.start()
    cube.finish(total_ref)
    own_load.wait()
    inner = tail.total().astype(bf16)
    grad_second = total_ref[...] + mm(inner, into)
    grad = own_grad[...].astype(f32) * kept(lens_ref, t, c, length) + norm_back(
        resid_ref[...], gain_ref[...], grad_second
    )
    gresid_ref[...] = grad
    grad_store = pltpu.make_async_copy(gresid_ref, gresid_hbm, store_sem.at[1])
    grad_store.start()
    low_ref[here, :] = grad.astype(bf16)
    inner_grad_ref[here, :] = inner
    cube.spread()
    tail.start(1)
    into_down = stacked([slim_ref[core, :, down_at : down_at + units] for core in range(2)])
    down_tail_ref[...] = mt(act_ref[...], into_down).astype(bf16)
    gate_right_ref[...] = SCALE * tm(inner_ref[...], dgate_ref[...])[:32]
    cube.relay()
    up_right_ref[...] = SCALE * tm(inner_ref[...], dup_ref[...])[:32]
    down_left_ref[...] = tm(down_grad_ref[...], act_ref[...])[:32]
    tail.wait(1)
    cube.done()
    tail.done()
    down_store.wait()
    grad_store.wait()


def strip_plan(cols, model, units):
    widths = (
        ("ql", model), ("qr", cols), ("kl", model), ("kr", cols), ("vl", model), ("vr", cols),
        ("rl", model), ("rr", LANES), ("ol", cols), ("or", model), ("gl", model), ("gr", units),
        ("ul", model), ("ur", units), ("dl", units), ("dr", model),
    )
    plan, at = {}, 0
    for name, wide in widths:
        plan[name] = (at, wide)
        at += wide
    return plan, at


BACK_LOADS = 24


def back_kernel(
    sizes,
    lens_ref,
    low_ref,
    head_gain_ref,
    gain_ref,
    qtaps_ref,
    ktaps_ref,
    vtaps_ref,
    wide_ref,
    slim_ref,
    tail_src,
    feed_grad_ref,
    out_inner_ref,
    inner_ref,
    gate_right_ref,
    up_right_ref,
    down_left_ref,
    start_hbm,
    map_hbm,
    reach_hbm,
    local_hbm,
    inv_hbm,
    wkey_hbm,
    wval_hbm,
    ext_hbm,
    rates_hbm,
    heads_hbm,
    down_hbm,
    resid_hbm,
    grad_hbm,
    n2_hbm,
    n1_hbm,
    x_hbm,
    gresid_hbm,
    w_hbm,
    back_hbm,
    into_hbm,
    wo_own,
    wo_other,
    block_hbm,
    input_grad_hbm,
    packed_ref,
    start_ref,
    map_ref,
    reach_ref,
    local_ref,
    inv_ref,
    wkey_ref,
    wval_ref,
    ext_ref,
    rates_ref,
    heads_ref,
    src,
    resid_ref,
    grad_ref,
    normed_ref,
    x_ref,
    gresid_ref,
    w_ref,
    back_ref,
    into_ref,
    wo_ref,
    out_ref,
    pre_ref,
    dmix_ref,
    after_ref,
    chain_out,
    gconv_ref,
    halo_out,
    halo_in,
    down_inner_ref,
    keys_ref,
    slopes_ref,
    values_ref,
    vslopes_ref,
    dfresh_ref,
    dkeys_ref,
    fresh_ref,
    tail2_src,
    inner_grad_ref,
    pack,
    mate_in,
    mine_ref,
    got,
    summed,
    load_sem,
    store_sem,
    chain_send,
    chain_recv,
    halo_send,
    halo_recv,
    swap_send,
    swap_recv,
    part_send,
    part_recv,
    first,
    second,
    held,
    total_ref,
    cube_send,
    cube_recv,
    cube2_send,
    cube2_recv,
    src2,
    first2,
    second2,
    held2,
    tail_got,
    tail_send,
    tail_recv,
    tail2_got,
    tail2_send,
    tail2_recv,
):
    seqs, length, heads, width, ctx_size, tp_size = sizes
    cols = heads * width
    model = low_ref.shape[1]
    half_model = model // 2
    units = gate_right_ref.shape[1]
    left_at = 3 * cols + LANES
    pairs = seqs * heads
    plan, used = strip_plan(cols, model, units)
    f = lax.axis_index("fsdp")
    c = lax.axis_index("ctx")
    t = lax.axis_index("tp")
    mate = {"fsdp": 1 - f}
    mine = part_of(t, length)
    loads = {}

    def fetch(name, source, target):
        loads[name] = pltpu.make_async_copy(source, target, load_sem.at[len(loads)])
        loads[name].start()

    fetch("wo_own", wo_own, wo_ref.at[f])
    fetch("wo_other", wo_other, wo_ref.at[1 - f])
    fetch("src", down_hbm, src)
    fetch("reach", reach_hbm, reach_ref)
    fetch("start", start_hbm, start_ref)
    fetch("local", local_hbm, local_ref)
    fetch("map", map_hbm, map_ref)
    fetch("ext", ext_hbm, ext_ref)
    fetch("rates", rates_hbm, rates_ref)
    fetch("wkey", wkey_hbm, wkey_ref)
    fetch("wval", wval_hbm, wval_ref)
    fetch("inv", inv_hbm, inv_ref)
    fetch("heads", heads_hbm, heads_ref)
    fetch("resid", resid_hbm, resid_ref)
    fetch("n2", n2_hbm, normed_ref)
    fetch("grad", grad_hbm, grad_ref)
    greet(
        pltpu.get_barrier_semaphore(),
        [(mate, None)] + tp_peers(t, tp_size),
        [({"ctx": c + 1 + i}, c + 1 + i < ctx_size) for i in range(ctx_size - 1)],
        c,
    )
    cube = Cube(t, src, out_ref, first, second, held, cube_send, cube_recv, CHUNKS)
    tail = Tail(t, tail_src, down_inner_ref, tail_got, tail_send, tail_recv, tp_size)
    cube2 = Cube(t, src2, src, first2, second2, held2, cube2_send, cube2_recv, CHUNKS)
    tail2 = Tail(t, tail2_src, inner_grad_ref, tail2_got, tail2_send, tail2_recv, tp_size)

    def put(name, core, rows):
        at, wide = plan[name]
        pack[core, :, at : at + wide] = rows.astype(bf16)

    tail.start(0)
    gain = head_gain_ref[...]
    taps = jnp.concatenate([qtaps_ref[...], ktaps_ref[...], vtaps_ref[...]], axis=1)
    row_at, col_at = grid_of(length)
    gconv_ref[...] = jnp.zeros_like(gconv_ref)
    from_out = stacked([wide_ref[core, 6] for core in range(2)])
    into_out = stacked([slim_ref[core, :, left_at : left_at + cols] for core in range(2)])
    out_grad = (SCALE * mt(low_ref[...], from_out)).astype(bf16)
    loads["wo_own"].wait()
    loads["wo_other"].wait()
    dheads = (
        mt(low_ref[:, :half_model], wo_ref[0])
        + mt(low_ref[:, half_model:], wo_ref[1])
        + mm(out_grad, into_out)
    )
    for s in range(seqs):
        for h in range(heads):
            dmix_ref[s * heads + h] = dheads[
                s * length : (s + 1) * length, h * width : (h + 1) * width
            ]
    loads["src"].wait()
    cube.each(cube.start)
    for name in ("reach", "start", "local", "map"):
        loads[name].wait()

    @pl.loop(0, seqs)
    def _(s):
        for h in range(heads):
            pair = s * heads + h
            mixed = mm(reach_ref[pair], start_ref[pair]) + local_ref[pair]
            dmix_ref[pair] = norm_back(mixed, gain, dmix_ref[pair])

    for name in ("ext", "rates", "wkey", "wval", "inv"):
        loads[name].wait()
    fetch("w", w_hbm, w_ref)
    fetch("back", back_hbm, back_ref)
    fetch("into", into_hbm, into_ref)
    fetch("x", x_hbm.at[mine], x_ref)
    fetch("gresid", gresid_hbm, gresid_ref)

    def hop_of(pair):
        return remote(
            chain_out.at[pair],
            after_ref.at[pair],
            chain_send.at[pair],
            chain_recv.at[pair],
            {"ctx": c - 1},
        )

    def link(s):
        for h in range(heads):
            pair = s * heads + h

            @pl.when(c == ctx_size - 1)
            def _(pair=pair):
                after_ref[pair] = jnp.zeros((width, width), bf16)

            @pl.when(c < ctx_size - 1)
            def _(pair=pair):
                hop_of(pair).wait_recv()

            @pl.when(c > 0)
            def _(pair=pair):
                chain_out[pair] = (
                    tm(map_ref[pair], after_ref[pair]) + tm(reach_ref[pair], dmix_ref[pair])
                ).astype(bf16)
                hop_of(pair).start()

    def unconvolve(s, kind):
        here = part_of(s, length)
        for h in range(heads):
            at = kind * cols + h * width
            total = None
            spill = None
            for j in range(CONV):
                tap = taps[j : j + 1, at : at + width]
                term = tap * gconv_ref[pl.ds(HALO + CONV - 1 - j, length), pl.ds(at, width)]
                edge = tap * gconv_ref[pl.ds(CONV - 1 - j, HALO), pl.ds(at, width)]
                total = term if total is None else total + term
                spill = edge if spill is None else spill + edge
            pre_ref[here, at : at + width] = total.astype(bf16)
            halo_out[0, s, :, at : at + width] = total[length - HALO :, :]
            halo_out[1, s, :, at : at + width] = spill

    def early(s):
        every = range(heads)
        at = [h * width for h in every]
        convs = [
            [convolved(ext_ref, taps, s, length, i * cols + at[h], width) for i in range(3)]
            for h in every
        ]
        starts_in = [start_ref[s * heads + h] for h in every]
        grads_in = [dmix_ref[s * heads + h] for h in every]
        wkeys = [wkey_ref[s * heads + h] for h in every]
        wvals = [wval_ref[s * heads + h] for h in every]
        fresh = [wval - mm(wkey, start) for wval, wkey, start in zip(wvals, wkeys, starts_in)]
        sigmas = [[jax.nn.sigmoid(a) for a in row] for row in convs]
        slopes = [
            [b * (1.0 + a * (1.0 - b)) for a, b in zip(row, sig)] for row, sig in zip(convs, sigmas)
        ]
        acts = [[a * b for a, b in zip(row, sig)] for row, sig in zip(convs, sigmas)]
        scales = [
            [lax.rsqrt(jnp.sum(a * a, axis=-1, keepdims=True) + EPS) for a in row[:2]] for row in acts
        ]
        query = [acts[h][0] * scales[h][0] for h in every]
        key = [acts[h][1] * scales[h][1] for h in every]
        lower = row_at >= col_at
        scores = [jnp.where(lower, finer(q, k, ((1,), (1,))), 0.0) for q, k in zip(query, key)]
        dscores = [
            jnp.where(lower, finer(g, v, ((1,), (1,))), 0.0) for g, v in zip(grads_in, fresh)
        ]
        dquery = [
            mt(g, start) + mm(d, k) for g, start, d, k in zip(grads_in, starts_in, dscores, key)
        ]
        dfresh = [tm(p, g) for p, g in zip(scores, grads_in)]
        dkeys = [tm(d, q) for d, q in zip(dscores, query)]
        along = [jnp.sum(q * g, axis=-1, keepdims=True) for q, g in zip(query, dquery)]
        for h in every:
            pair = s * heads + h
            keys_ref[pair] = key[h]
            slopes_ref[pair] = slopes[h][1] * scales[h][1]
            values_ref[pair] = acts[h][2]
            vslopes_ref[pair] = slopes[h][2]
            dfresh_ref[pair] = dfresh[h]
            dkeys_ref[pair] = dkeys[h]
            fresh_ref[pair] = fresh[h].astype(bf16)
            gconv_ref[pl.ds(HALO, length), pl.ds(at[h], width)] = (
                slopes[h][0] * scales[h][0] * (dquery[h] - query[h] * along[h])
            )
        unconvolve(s, 0)

    def late(s):
        every = range(heads)
        here = part_of(s, length)
        rate_block = rates_ref[here, :]
        lane = lax.broadcasted_iota(jnp.int32, (length, LANES), 1)
        rate = [column(rate_block, RATE_AT + h) for h in every]
        start = [start_ref[s * heads + h] for h in every]
        after = [after_ref[s * heads + h] for h in every]
        key = [keys_ref[s * heads + h] for h in every]
        fresh = [fresh_ref[s * heads + h] for h in every]
        before = [dfresh_ref[s * heads + h] for h in every]
        inverse = [inv_ref[s * heads + h] for h in every]
        dkeys = [dkeys_ref[s * heads + h] for h in every]
        values = [values_ref[s * heads + h] for h in every]
        keyed = [slopes_ref[s * heads + h] for h in every]
        valued = [vslopes_ref[s * heads + h] for h in every]
        low = [item.astype(bf16) for item in key]
        dfresh = [b + mm(k, a) for b, k, a in zip(before, low, after)]
        dvalue = [tm(inv, d) for inv, d in zip(inverse, dfresh)]
        dvalue_low = [item.astype(bf16) for item in dvalue]
        products = [mt(k, k) for k in low]
        outer = [mt(v, a) for v, a in zip(fresh, after)]
        dkey_in = [-mt(d, st) for d, st in zip(dvalue_low, start)]
        dstrict = [
            jnp.where(row_at > col_at, -mt(d, v), 0.0) for d, v in zip(dvalue_low, fresh)
        ]
        dprod = [(r * d).astype(bf16) for r, d in zip(rate, dstrict)]
        forth = [mm(d, k) for d, k in zip(dprod, low)]
        back = [tm(d, k) for d, k in zip(dprod, low)]
        dkey = [
            dkeys[h] + outer[h] + rate[h] * dkey_in[h] + forth[h] + back[h] for h in every
        ]
        drate = [
            jnp.sum(
                dstrict[h] * products[h] + dvalue[h] * values[h] + dkey_in[h] * key[h],
                axis=-1,
                keepdims=True,
            )
            for h in every
        ]
        along = [jnp.sum(k * d, axis=-1, keepdims=True) for k, d in zip(key, dkey)]
        rate_grads = jnp.zeros((length, LANES), f32)
        for h in every:
            at = h * width
            gconv_ref[pl.ds(HALO, length), pl.ds(cols + at, width)] = keyed[h] * (
                dkey[h] - key[h] * along[h]
            )
            gconv_ref[pl.ds(HALO, length), pl.ds(2 * cols + at, width)] = (
                rate[h] * dvalue[h] * valued[h]
            )
            rate_grads = rate_grads + jnp.where(
                lane == RATE_AT + h, drate[h] * rate[h] * (1.0 - rate[h]), 0.0
            )
        unconvolve(s, 1)
        unconvolve(s, 2)
        pre_ref[here, 3 * cols :] = rate_grads.astype(bf16)

    ends = c == ctx_size - 1
    starts = c == 0
    inside = (c > 0) & (c < ctx_size - 1)
    begins = (ctx_size - 1 - c) // (ctx_size - 1)

    final = c // (ctx_size - 1)
    block_store = pltpu.make_async_copy(out_ref, block_hbm, store_sem.at[0])

    def halo_of(s):
        return remote(
            halo_in.at[1, s], halo_in.at[0, s], halo_send.at[s], halo_recv.at[s], {"ctx": c - 1}
        )

    def project(i):
        s = cube2.block_at(i)
        here = part_of(s, length)

        @pl.when(c < ctx_size - 1)
        def _():
            halo_of(s).wait_recv()
            last = pl.ds(pl.multiple_of(s * length + length - 16, 16), 16)
            rows = pre_ref[last, : 3 * cols].astype(f32)
            edge = halo_out[0, s] + halo_in[0, s].astype(f32)
            pre_ref[last, : 3 * cols] = jnp.concatenate([rows[:HALO], edge], axis=0).astype(bf16)

        @pl.when(i == 0)
        def _():
            for name in ("w", "back", "into"):
                loads[name].wait()

        part = mm(pre_ref[here, 3 * cols :], into_ref[...])
        for kind in range(3):
            part = part + mt(pre_ref[here, kind * cols : (kind + 1) * cols], w_ref[kind])
        src2[here, :] = part.astype(bf16)
        tail2_src[here, :] = (SCALE * mt(pre_ref[here, :], back_ref[...])).astype(bf16)
        cube2.send_block(i)

        @pl.when(i < 3)
        def _():
            tail2.send_block(s)

        @pl.when(i == 2)
        def _():
            cube2.middle_half(1)

        @pl.when(i == 3)
        def _():
            cube2.middle_half(0)

    @pl.loop(0, 3 * seqs + 2)
    def _(k):
        part = k // seqs
        odd = lax.rem(k, 2) == seqs % 2
        s = cube2.block_at(lax.rem(k, seqs))
        later = cube2.block_at(
            (1 - begins) * lax.rem(k, seqs) + begins * lax.rem((k + seqs) // 2, seqs)
        )
        ready = (1 - begins) * (k - 2 * seqs - 1) + begins * ((k + seqs - 3) // 2 - seqs)

        @pl.when(k == 4 + 4 * final)
        def _():
            cube.middle()

        @pl.when(k == 7 + 3 * final)
        def _():
            cube.finish(total_ref)
            cube.first_sent()
            loads["resid"].wait()
            inner = tail.total().astype(bf16)
            right = stacked([wide_ref[core, 7] for core in range(2)])
            rows = resid_ref[...] + total_ref[...] + SCALE * mm(inner, right)
            out_ref[mine, :] = (kept(lens_ref, t, c, length) * rows).astype(bf16)
            down_inner_ref[mine, :] = inner
            cube.spread()
            tail.start(1)

        @pl.when(k == 9 + 3 * final)
        def _():
            cube.relay()

        @pl.when((ends & (part == 1)) | ((starts | inside) & (part == 0)))
        def _():
            early(s)

        @pl.when(
            (ends & (part == 0)) | (inside & (part == 1)) | (starts & (part > 0) & (part < 3) & odd)
        )
        def _():
            link(later)

        @pl.when(
            ((ends | inside) & (part == 2))
            | (starts & (part > 0) & (part < 3) & jnp.logical_not(odd))
        )
        def _():
            late(later)
            halo_in[1, later] = halo_out[1, later].astype(bf16)

            @pl.when(c > 0)
            def _():
                halo_of(later).start()

        @pl.when(
            ((ends | inside) & (k > 2 * seqs) & (k < 3 * seqs + 1))
            | (starts & (k > seqs + 2) & jnp.logical_not(odd))
        )
        def _():
            project(ready)


    @pl.when(c > 0)
    def _():
        @pl.loop(0, seqs)
        def _(s):
            halo_of(s).wait_send()

        @pl.loop(0, pairs)
        def _(pair):
            hop_of(pair).wait_send()

    inner = tail2.total().astype(bf16)
    inner_grad_ref[mine, :] = inner
    tail2.start(1)
    loads["n2"].wait()
    feed_left = tm(feed_grad_ref[...], normed_ref[...])
    fetch("n1", n1_hbm, normed_ref)
    pack[:, :, used:] = jnp.zeros((2, 8, pack.shape[2] - used), bf16)
    loads["heads"].wait()
    out_left = tm(out_grad, heads_ref[...])
    out_right = SCALE * tm(out_inner_ref[...], low_ref[...])
    right = SCALE * tm(inner_ref[...], pre_ref[...])
    tail.wait(1)
    masked = jnp.concatenate(
        [
            kept(lens_ref, s, c, length) * down_inner_ref[s * length : (s + 1) * length, :].astype(f32)
            for s in range(seqs)
        ],
        axis=0,
    )
    loads["grad"].wait()
    down_right = SCALE * tm(masked, grad_ref[...])
    for core in range(2):
        at = core * 8
        put("ol", core, out_left[at : at + 8])
        put("or", core, out_right[at : at + 8])
        put("dr", core, down_right[at : at + 8])
        put("dl", core, down_left_ref[at : at + 8, :])
        at = core * 16
        put("gl", core, feed_left[at : at + 8])
        put("ul", core, feed_left[at + 8 : at + 16])
        put("gr", core, gate_right_ref[at : at + 8, :])
        put("ur", core, up_right_ref[at + 8 : at + 16, :])
        for kind, name in enumerate(("qr", "kr", "vr", "rr")):
            at = core * 32 + kind * 8
            put(name, core, right[at : at + 8, kind * cols : kind * cols + plan[name][1]])
    loads["n1"].wait()
    tail2.wait(1)
    left = tm(inner_grad_ref[...], normed_ref[...])
    for core in range(2):
        for kind, name in enumerate(("ql", "kl", "vl", "rl")):
            at = core * 32 + kind * 8
            put(name, core, left[at : at + 8])
    swap = remote(pack.at[1 - f], mate_in, swap_send, swap_recv, mate)
    swap.start()
    cube2.finish(total_ref)
    loads["x"].wait()
    loads["gresid"].wait()
    grad_first = total_ref[...] + mm(inner, into_ref[...])
    grad = gresid_ref[...] + norm_back(x_ref[...].astype(f32), gain_ref[...], grad_first)
    src[mine, :] = grad.astype(bf16)
    cube2.spread()
    cube.done(1)
    block_store.start()
    swap.wait_recv()
    both = (pack[f].astype(f32) + mate_in[...].astype(f32)).astype(bf16)
    piece = both.shape[1] // ctx_size
    for j in range(ctx_size):
        mine_ref[j] = both[:, j * piece : (j + 1) * piece]
    sends = []
    spreads = []
    for i in range(ctx_size - 1):
        peer = {"ctx": lax.rem(c + 1 + i, ctx_size)}
        back = ctx_size - 2 - i
        sends.append(
            remote(
                mine_ref.at[lax.rem(c + 1 + i, ctx_size)],
                got.at[back],
                part_send.at[0, i],
                part_recv.at[0, back],
                peer,
            )
        )
        spreads.append(
            remote(summed.at[c], summed.at[c], part_send.at[1, i], part_recv.at[1, back], peer)
        )
    for copy in sends:
        copy.start()
    cube2.relay()
    for copy in sends:
        copy.wait_recv()
    total = mine_ref[c].astype(f32)
    for i in range(ctx_size - 1):
        total = total + got[i].astype(f32)
    summed[c] = total.astype(bf16)
    for copy in spreads:
        copy.start()
    for copy in spreads:
        copy.wait_recv()
    for j in range(ctx_size):
        packed_ref[:, j * piece : (j + 1) * piece] = summed[j].astype(f32)
    cube2.done()
    grad_store = pltpu.make_async_copy(src, input_grad_hbm, store_sem.at[1])
    grad_store.start()
    swap.wait_send()
    for copy in sends + spreads:
        copy.wait_send()
    tail.done()
    tail2.done()
    block_store.wait()
    grad_store.wait()


def deal_kernel(strips, heads, packed_hbm, block_in, grad_in, block_out, grad_out, *refs):
    outs, (block_ref, grad_ref, packed_ref, load_sem, store_sem, packed_sem) = refs[:-6], refs[-6:]
    count = load_sem.shape[1]
    size = block_ref.shape[0] // count
    moves = []
    for i, (source, middle, target) in enumerate(
        ((block_in, block_ref, block_out), (grad_in, grad_ref, grad_out))
    ):
        for k in range(count):
            here = pl.ds(k * size, size)
            load = pltpu.make_async_copy(source.at[here], middle.at[here], load_sem.at[i, k])
            load.start()
            moves.append(
                (load, pltpu.make_async_copy(middle.at[here], target.at[here], store_sem.at[i, k]))
            )
    packed_load = pltpu.make_async_copy(packed_hbm, packed_ref, packed_sem)
    packed_load.start()
    for load, store in moves:
        load.wait()
        store.start()
    packed_load.wait()
    for index, (out, (at, wide)) in enumerate(zip(outs, strips)):
        if index == 7:
            lanes = lax.broadcasted_iota(jnp.int32, (heads, LANES), 1)
            rows = lax.broadcasted_iota(jnp.int32, (heads, LANES), 0)
            pick = jnp.where(lanes == rows + RATE_AT, 1.0, 0.0)
            out[...] = mt(pick, packed_ref[:, at : at + wide])
        else:
            out[...] = packed_ref[:, at : at + wide]
    for _, store in moves:
        store.wait()


def local(ctx_size, tp_size, *arguments):
    (
        hidden_in,
        seq_lengths,
        mixer_gain,
        feed_gain,
        query_weight,
        key_weight,
        value_weight,
        rate_weight,
        query_conv,
        key_conv,
        value_conv,
        head_gain,
        output_weight,
        gate_weight,
        up_weight,
        down_weight,
        query_left,
        query_right,
        key_left,
        key_right,
        value_left,
        value_right,
        rate_left,
        rate_right,
        output_left,
        output_right,
        gate_left,
        gate_right,
        up_left,
        up_right,
        down_left,
        down_right,
        output_grad,
    ) = arguments
    seqs, length, model = hidden_in.shape
    heads = rate_weight.shape[1]
    width = head_gain.shape[0]
    cols = heads * width
    rows = seqs * length
    units = gate_weight.shape[1]
    half = query_weight.shape[0]
    pairs = seqs * heads
    x = hidden_in.reshape(rows, model)
    grad_rows = output_grad.reshape(rows, model)
    rate_rows = rate_weight.T
    wides = (
        query_left.T,
        key_left.T,
        value_left.T,
        rate_left.T,
        gate_left.T,
        up_left.T,
        output_right,
        down_right,
    )
    slims = (
        query_right,
        key_right,
        value_right,
        output_left.T,
        gate_right,
        up_right,
        down_left.T,
    )
    slim_wide = LANES + sum(item.shape[1] for item in slims)
    gain1, gain2, gain3 = mixer_gain[None, :], feed_gain[None, :], head_gain[None, :]
    ext = length + HALO
    square = (pairs, width, width)
    tall = (pairs, length, width)
    block = rows // tp_size
    smem = pl.BlockSpec(memory_space=pltpu.SMEM)
    mixer_sizes = (seqs, length, heads, width, ctx_size, tp_size)
    kept_shapes = (
        shape((rows, model), bf16),
        shape((2, 8, 8, model), bf16),
        shape((2, 8, slim_wide), bf16),
        shape((LANES, model), bf16),
        shape((LANES, 3 * cols + LANES), bf16),
        shape((seqs, ext, 3 * cols), f32),
        shape((rows, LANES), bf16),
        shape((rows, LANES), f32),
        shape((pairs, length, length), bf16),
        shape(tall, bf16),
        shape(tall, f32),
        shape(tall, bf16),
        shape(tall, f32),
        shape(square, bf16),
        shape((rows, cols), bf16),
        shape(square, bf16),
        shape((rows, units), f32),
        shape((rows, LANES), bf16),
    )
    (
        second,
        out_inner,
        residual,
        wo,
        wg,
        wu,
        wd,
        wqkv,
        n1,
        wide_all,
        slim_all,
        into,
        back,
        pre_ext,
        inner,
        rates,
        inverse,
        wkey,
        wval,
        reach,
        local_out,
        step_map,
        heads_low,
        start,
        active,
        down_grad,
    ) = pl.pallas_call(
        functools.partial(mixer_kernel, mixer_sizes),
        out_shape=(
            shape((rows, model), bf16),
            shape((rows, LANES), bf16),
            shape((block, model), f32),
            shape(output_weight.shape, bf16),
            shape(gate_weight.shape, bf16),
            shape(up_weight.shape, bf16),
            shape(down_weight.shape, bf16),
            shape((3, model, cols), bf16),
        )
        + kept_shapes,
        in_specs=[smem] + [VMEM] * 8 + [ANY] * 24,
        out_specs=(VMEM,) * 3 + (ANY,) * (5 + len(kept_shapes)),
        scratch_shapes=[pltpu.VMEM(item.shape, item.dtype) for item in kept_shapes]
        + [
            pltpu.VMEM(square, f32),
            pltpu.VMEM((3, model, cols), bf16),
            pltpu.VMEM((heads, model), bf16),
            pltpu.VMEM((seqs, HALO, 3 * cols), bf16),
            pltpu.VMEM((seqs, HALO, 3 * cols), bf16),
            pltpu.VMEM((LANES, 3 * cols + LANES), f32),
            pltpu.VMEM((LANES, model), f32),
            pltpu.VMEM(square, bf16),
            pltpu.VMEM((2,) + output_weight.shape, bf16),
            pltpu.VMEM((2,) + down_weight.shape, bf16),
            pltpu.VMEM((rows, model), bf16),
            pltpu.VMEM((8, LANES), bf16),
            DMA((24,)),
            DMA((24,)),
            DMA((20,)),
            DMA((20,)),
            DMA((seqs,)),
            DMA((seqs,)),
            DMA((4,)),
            DMA,
            DMA((pairs,)),
            DMA((pairs,)),
        ]
        + cube_scratch(rows, model)
        + tail_scratch(rows, tp_size),
        compiler_params=params(0),
        name="mixer",
    )(
        seq_lengths,
        x,
        gain1,
        gain2,
        gain3,
        query_conv,
        key_conv,
        value_conv,
        rate_right.T,
        query_weight,
        key_weight,
        value_weight,
        rate_rows,
        *wides,
        *slims,
        output_weight,
        gate_weight,
        up_weight,
        down_weight,
        grad_rows,
    )
    (
        resid_low,
        feed_grad,
        grad_residual,
        down_part,
        down_tail,
        gate_right_grad,
        up_right_grad,
        down_left_grad,
    ) = pl.pallas_call(
        functools.partial(feed_kernel, (seqs, length, cols, ctx_size, tp_size)),
        out_shape=(
            shape((rows, model), bf16),
            shape((rows, LANES), bf16),
            shape((block, model), f32),
            shape((rows, model), bf16),
            shape((rows, LANES), bf16),
            shape((32, units), f32),
            shape((32, units), f32),
            shape((32, units), f32),
        ),
        in_specs=[smem] + [VMEM] * 5 + [ANY] * 9,
        out_specs=(VMEM, VMEM, ANY, ANY) + (VMEM,) * 4,
        scratch_shapes=[
            pltpu.VMEM((2,) + gate_weight.shape, bf16),
            pltpu.VMEM((2,) + up_weight.shape, bf16),
            pltpu.VMEM((2,) + down_weight.shape, bf16),
            pltpu.VMEM((rows, units), bf16),
            pltpu.VMEM((rows, units), bf16),
            pltpu.VMEM((rows, units), bf16),
            pltpu.VMEM((rows, LANES), bf16),
            pltpu.VMEM((LANES, units), bf16),
            pltpu.VMEM((LANES, units), bf16),
            pltpu.VMEM((block, model), bf16),
            pltpu.VMEM((rows, units), f32),
            pltpu.VMEM((block, model), f32),
            pltpu.VMEM((block, model), f32),
            pltpu.VMEM((rows, model), bf16),
            DMA((3,)),
            DMA((-(-units // (2 * LANES)), 5)),
            DMA((2,)),
            DMA,
        ]
        + cube_scratch(rows, model)
        + tail_scratch(rows, tp_size),
        compiler_params=params(2),
        name="feed",
    )(
        seq_lengths,
        second,
        gain2,
        wide_all,
        slim_all,
        down_grad,
        grad_rows,
        gate_weight,
        wg,
        up_weight,
        wu,
        down_weight,
        wd,
        active,
        residual,
    )
    plan, used = strip_plan(cols, model, units)
    grain = LANES * ctx_size
    total_wide = -(-used // grain) * grain
    piece = total_wide // ctx_size
    block_out, input_grad, packed = pl.pallas_call(
        functools.partial(back_kernel, mixer_sizes),
        out_shape=(
            shape((rows, model), bf16),
            shape((rows, model), bf16),
            shape((8, total_wide), f32),
        ),
        in_specs=[smem] + [VMEM] * 15 + [ANY] * 22,
        out_specs=(ANY, ANY, VMEM),
        scratch_shapes=[
            pltpu.VMEM(square, bf16),
            pltpu.VMEM(square, bf16),
            pltpu.VMEM(tall, bf16),
            pltpu.VMEM(tall, f32),
            pltpu.VMEM((pairs, length, length), bf16),
            pltpu.VMEM(tall, bf16),
            pltpu.VMEM(tall, f32),
            pltpu.VMEM((seqs, ext, 3 * cols), f32),
            pltpu.VMEM((rows, LANES), f32),
            pltpu.VMEM((rows, cols), bf16),
            pltpu.VMEM((rows, model), bf16),
            pltpu.VMEM((block, model), f32),
            pltpu.VMEM((rows, model), bf16),
            pltpu.VMEM((rows, model), bf16),
            pltpu.VMEM((block, model), bf16),
            pltpu.VMEM((block, model), f32),
            pltpu.VMEM((3, model, cols), bf16),
            pltpu.VMEM((LANES, 3 * cols + LANES), bf16),
            pltpu.VMEM((LANES, model), bf16),
            pltpu.VMEM((2,) + output_weight.shape, bf16),
            pltpu.VMEM((rows, model), bf16),
            pltpu.VMEM((rows, 3 * cols + LANES), bf16),
            pltpu.VMEM(tall, f32),
            pltpu.VMEM(square, bf16),
            pltpu.VMEM(square, bf16),
            pltpu.VMEM((HALO + length + HALO, 3 * cols), f32),
            pltpu.VMEM((2, seqs, HALO, 3 * cols), f32),
            pltpu.VMEM((2, seqs, HALO, 3 * cols), bf16),
            pltpu.VMEM((rows, LANES), bf16),
            pltpu.VMEM(tall, f32),
            pltpu.VMEM(tall, f32),
            pltpu.VMEM(tall, f32),
            pltpu.VMEM(tall, f32),
            pltpu.VMEM(tall, f32),
            pltpu.VMEM(tall, f32),
            pltpu.VMEM(tall, bf16),
            pltpu.VMEM((rows, LANES), bf16),
            pltpu.VMEM((rows, LANES), bf16),
            pltpu.VMEM((2, 8, total_wide), bf16),
            pltpu.VMEM((8, total_wide), bf16),
            pltpu.VMEM((ctx_size, 8, piece), bf16),
            pltpu.VMEM((ctx_size - 1, 8, piece), bf16),
            pltpu.VMEM((ctx_size, 8, piece), bf16),
            DMA((BACK_LOADS,)),
            DMA((2,)),
            DMA((pairs,)),
            DMA((pairs,)),
            DMA((seqs,)),
            DMA((seqs,)),
            DMA,
            DMA,
            DMA((2, ctx_size - 1)),
            DMA((2, ctx_size - 1)),
        ]
        + cube_scratch(rows, model)[1:]
        + [DMA((4, 2, CHUNKS, 2)), DMA((4, 2, CHUNKS, 2))]
        + cube_scratch(rows, model)[:4]
        + tail_scratch(rows, tp_size)[1:] * 2,
        compiler_params=params(3, 60 << 20),
        name="back",
    )(
        seq_lengths,
        resid_low,
        gain3,
        gain1,
        query_conv,
        key_conv,
        value_conv,
        wide_all,
        slim_all,
        down_tail,
        feed_grad,
        out_inner,
        inner,
        gate_right_grad,
        up_right_grad,
        down_left_grad,
        start,
        step_map,
        reach,
        local_out,
        inverse,
        wkey,
        wval,
        pre_ext,
        rates,
        heads_low,
        down_part,
        residual,
        grad_rows,
        second,
        n1,
        x,
        grad_residual,
        wqkv,
        back,
        into,
        output_weight,
        wo,
    )
    strips = tuple(plan.values())
    dealt = pl.pallas_call(
        functools.partial(deal_kernel, strips, heads),
        out_shape=(shape((rows, model), bf16),) * 2
        + tuple(
            shape((heads, 8) if i == 7 else (8, wide), f32) for i, (_, wide) in enumerate(strips)
        ),
        in_specs=[ANY, ANY, ANY],
        out_specs=(ANY, ANY) + (VMEM,) * len(strips),
        scratch_shapes=[
            pltpu.VMEM((rows, model), bf16),
            pltpu.VMEM((rows, model), bf16),
            pltpu.VMEM((8, total_wide), f32),
            DMA((2, 4)),
            DMA((2, 4)),
            DMA,
        ],
        name="deal",
    )(packed, block_out, input_grad)
    block_out, input_grad = dealt[:2]
    shares = list(dealt[2:])
    lefts = (0, 2, 4, 6, 7, 8, 10, 12, 14)
    shares = [item.T if i in lefts else item for i, item in enumerate(shares)]
    return (
        block_out.reshape(seqs, length, model),
        input_grad.reshape(seqs, length, model),
    ) + tuple(shares)


def solution(mesh):
    placed = (
        P("fsdp", "ctx", None),
        P("fsdp"),
        P(),
        P(),
        P("fsdp", "tp"),
        P("fsdp", "tp"),
        P("fsdp", "tp"),
        P("fsdp", "tp"),
        P(None, "tp"),
        P(None, "tp"),
        P(None, "tp"),
        P(),
        P("tp", "fsdp"),
        P("fsdp", "tp"),
        P("fsdp", "tp"),
        P("tp", "fsdp"),
    )
    left_in, left_over, right_over, right_in = (
        P(None, "fsdp"),
        P("tp", "fsdp"),
        P("fsdp", None),
        P("fsdp", "tp"),
    )
    adapters = (left_in, right_in) * 4 + (left_over, right_over) + (left_in, right_in) * 2 + (
        left_over,
        right_over,
    )
    rows = P("fsdp", "ctx", None)
    return jax.shard_map(
        functools.partial(local, mesh.shape["ctx"], mesh.shape["tp"]),
        mesh=mesh,
        in_specs=placed + adapters + (rows,),
        out_specs=(rows, rows) + adapters,
        check_vma=False,
    )
```
